32 devices in a mesh: row: 4 (over y, x), col: 8 (over z, core).
Axes of the slice: x: 2, y: 2, z: 4, core: 2. Of those that a mesh axis runs over, the one named last changes fastest.
Arguments:
- parent_front: bfloat16 [28672, 28672], P('row', 'col'), may hold values from -6 to 6
- child_update: bfloat16 [2, 14336, 14336], P(None, 'row', 'col'), may hold values from -6 to 6
- parent_test: bfloat16 [28672, 448], P('col'), may hold values from -0.03125 to 0.03125
- child_test: bfloat16 [2, 14336, 448], P(None, 'col'), may hold values from -0.046875 to 0.046875
- child_map: int32 [2, 112], replicated, may hold values from 0 to 223, as said below
Outputs:
- leaf_basis: bfloat16 [224, 128, 448], P('row', 'col')
- couplings: float32 [32, 448, 448], P('row', 'col')
The draws below stay inside these ranges and needn't reach their ends.
Inputs may be any that keep to these rules, and one draw needn't show every extreme that they name: `child_map`: for each child the entries rise strictly along its blocks, and entry j is at least j.
All inputs are finite; a program needn't handle non-finite values.
Results may differ from the reference program's by a relative error of at most 0.006.
Values may be sent and summed in bfloat16 or wider, within the bound.
A program may use at most 192 MiB of HBM per device.

```python
import math
import jax
import jax.numpy as jnp
from jax import lax

M = 14336
R = 448
LEAF = 896
BLOCK = 128
P_SIZE = 28672


def draw_child_map(key, part):
    blocks = M // BLOCK
    half = blocks // 2
    positions = jnp.arange(blocks, dtype=jnp.int32)
    first_key = jax.random.fold_in(key, 11)
    level = jax.random.randint(jax.random.fold_in(first_key, 1), (), 1, 4)
    draws = jax.random.randint(jax.random.fold_in(first_key, 2), (blocks,), 0, 4)
    steps_up = (draws < level).astype(jnp.int32)
    first = positions + jnp.cumsum(steps_up).astype(jnp.int32)
    second_key = jax.random.fold_in(key, 12)
    gaps = jax.random.randint(jax.random.fold_in(second_key, 2), (blocks,), 0, 2)
    gaps = jnp.where(positions < half, gaps, 0).astype(jnp.int32)
    later = jnp.cumsum(gaps[::-1])[::-1].astype(jnp.int32) - gaps
    second = positions + blocks - later
    return jnp.stack([first, second]).astype(jnp.int32)


def level_of(own_key, dims, split, low, high):
    factor_of = 1.0
    for axis_at, blocks in split:
        heights = jax.random.uniform(jax.random.fold_in(jax.random.fold_in(own_key, 6), axis_at), (blocks,), jnp.float32, low / len(split), high / len(split))
        factor_of = factor_of * jnp.repeat(jnp.exp(heights), dims[axis_at] // blocks).reshape((-1,) + (1,) * (len(dims) - 1 - axis_at))
    return factor_of


def scatter_about(key, extent, spread, most, pieces=(), kind=jnp.bfloat16):
    drawn = jax.random.normal(key, extent, jnp.float32) * spread
    if len(pieces) > 0:
        drawn = level_of(key, extent, pieces, -0.22, 0.18) * drawn
    return jnp.clip(drawn, min=-most, max=most).astype(kind)


def setup_inputs(seed: int = 0) -> dict:
    keys = jax.random.split(jax.random.key(seed), 6)
    parent_front = scatter_about(keys[0], (P_SIZE, P_SIZE), 1.0, 6.0, ((0, 4), (1, 8)))
    child_update = scatter_about(keys[1], (2, M, M), 1.0, 6.0, ((1, 4), (2, 8)))
    parent_test = scatter_about(keys[2], (P_SIZE, R), P_SIZE ** -0.5, 0.03125, ((0, 8),))
    child_test = scatter_about(keys[3], (2, M, R), M ** -0.5, 0.046875, ((1, 8),))
    child_map = draw_child_map(jax.random.fold_in(keys[5], 71), 0)
    return {"parent_front": parent_front, "child_update": child_update, "parent_test": parent_test, "child_test": child_test, "child_map": child_map}


HIGH = lax.Precision.HIGHEST

def orthonormal(leaves):
    gram_matrix = jnp.einsum('lkr,lks->lrs', leaves, leaves, precision=HIGH)
    factor = jnp.linalg.cholesky(gram_matrix)
    solved = lax.linalg.triangular_solve(factor, leaves, left_side=False, lower=True, transpose_a=True)
    return (solved * math.sqrt(LEAF)).astype(jnp.bfloat16)

def reference(parent_front, child_update, parent_test, child_test, child_map):
    sample = jnp.dot(parent_front.astype(jnp.float32), parent_test.astype(jnp.float32), preferred_element_type=jnp.float32)
    sample = sample.reshape(2 * M // BLOCK, BLOCK, R)
    for which in range(2):
        probed = jnp.dot(child_update[which].astype(jnp.float32), child_test[which].astype(jnp.float32), preferred_element_type=jnp.float32)
        sample = sample.at[child_map[which]].add(probed.reshape(M // BLOCK, BLOCK, R))
    leaves = sample.reshape(2 * M // LEAF, LEAF, R)
    bases = orthonormal(leaves)
    shrink = 1.0 / math.sqrt(LEAF)

    def coupling(leaf_index):
        sibling = jnp.bitwise_xor(leaf_index, 1)
        front_tile = lax.dynamic_slice(parent_front, (leaf_index * LEAF, sibling * LEAF), (LEAF, LEAF))
        product = (jnp.dot(front_tile.astype(jnp.float32), bases[sibling].astype(jnp.float32), preferred_element_type=jnp.float32) * shrink).astype(jnp.bfloat16)
        return jnp.dot(bases[leaf_index].T.astype(jnp.float32), product.astype(jnp.float32), preferred_element_type=jnp.float32) * shrink
    couplings = lax.map(coupling, jnp.arange(2 * M // LEAF, dtype=jnp.int32))
    return (bases.reshape(2 * M // BLOCK, BLOCK, R), couplings)
```

```python
import functools
import math

import jax
import jax.numpy as jnp
from jax import lax
from jax.experimental import pallas as pl
from jax.experimental.pallas import tpu as pltpu
from jax.sharding import PartitionSpec as P


LEAF = 896
BLOCK = 128
PIVOTS = 64
GROUP = 4

HIGH = lax.Precision.HIGHEST
MESH = pl.DeviceIdType.MESH


def dot(a, b, dims):
    return lax.dot_general(
        a, b, (dims, ((), ())), precision=HIGH, preferred_element_type=jnp.float32
    )


def inverse_factor(tile, nb):
    ridx = lax.broadcasted_iota(jnp.int32, tile.shape, 0)
    lane = lax.broadcasted_iota(jnp.int32, tile.shape, 1)
    for j in range(0, nb, GROUP):
        cols = [
            jnp.broadcast_to(tile[:, nb + j + k : nb + j + k + 1], tile.shape)
            for k in range(GROUP)
        ]
        rows = [tile[j + k : j + k + 1, :] for k in range(GROUP)]
        for k in range(GROUP):
            at = j + k
            factor = jnp.where(ridx > at, cols[k] * (1.0 / cols[k][at : at + 1, :]), 0.0)
            for m in range(k + 1, GROUP):
                cols[m] = cols[m] - factor * cols[m][at : at + 1, :]
                rows[m] = rows[m] - factor[j + m : j + m + 1, :] * rows[k]
            cols[k] = factor
        for k in range(GROUP):
            tile = tile - cols[k] * rows[k]
    pivots = jnp.sum(jnp.where(lane == ridx + nb, tile, 0.0), axis=1, keepdims=True)
    return tile[:, :nb] * lax.rsqrt(pivots)


def basis_kernel(scale, yt_ref, qt_ref, gram_ref, work_ref):
    nb = PIVOTS
    probes = yt_ref.shape[0]
    work_ref[...] = yt_ref[...]
    gram_ref[...] = dot(yt_ref[...], yt_ref[...], ((1,), (1,)))

    def step(index, carry):
        start = pl.multiple_of(index * nb, nb)
        panel = gram_ref[pl.ds(start, nb), :]
        source = lax.broadcasted_iota(jnp.int32, (probes, 2 * nb), 0)
        lane = lax.broadcasted_iota(jnp.int32, (probes, 2 * nb), 1)
        pick = jnp.where((lane >= nb) & (source == lane - nb + start), 1.0, 0.0)
        eye = jnp.where(
            lax.broadcasted_iota(jnp.int32, (nb, 2 * nb), 0)
            == lax.broadcasted_iota(jnp.int32, (nb, 2 * nb), 1),
            1.0,
            0.0,
        )
        inverse = inverse_factor(dot(panel, pick, ((1,), (0,))) + eye, nb)
        top = dot(inverse, panel, ((1,), (0,)))
        solved = dot(inverse, work_ref[pl.ds(start, nb), :], ((1,), (0,)))
        qt_ref[pl.ds(start, nb), :] = (solved * scale).astype(qt_ref.dtype)
        gram_ref[...] -= dot(top, top, ((0,), (0,)))
        work_ref[...] -= dot(top, solved, ((0,), (0,)))
        return carry

    lax.fori_loop(0, probes // nb, step, 0)


def leaf_basis_of(yt):
    probes, rows = yt.shape
    return pl.pallas_call(
        functools.partial(basis_kernel, math.sqrt(LEAF)),
        out_shape=jax.ShapeDtypeStruct((probes, rows), jnp.bfloat16),
        in_specs=[pl.BlockSpec(memory_space=pltpu.VMEM)],
        out_specs=pl.BlockSpec(memory_space=pltpu.VMEM),
        scratch_shapes=[
            pltpu.VMEM((probes, probes), jnp.float32),
            pltpu.VMEM((probes, rows), jnp.float32),
        ],
        compiler_params=pltpu.CompilerParams(vmem_limit_bytes=40 << 20),
        cost_estimate=pl.CostEstimate(
            flops=40 * probes * probes * rows,
            bytes_accessed=6 * probes * rows,
            transcendentals=0,
        ),
        name="leaf_basis",
    )(yt)


def probe_kernel(parity_ref, front_ref, test_ref, kept_ref, sent_ref):
    total = jnp.dot(front_ref[...], test_ref[...], preferred_element_type=jnp.float32)
    blocks, pairs, slab, probes = kept_ref.shape
    view = total.reshape(blocks * pairs, 2, slab, probes)
    even = parity_ref[0] == 0
    kept_ref[...] = jnp.where(even, view[:, 0], view[:, 1]).reshape(kept_ref.shape)
    sent_ref[...] = jnp.where(even, view[:, 1], view[:, 0]).reshape(sent_ref.shape)


def probe(front, test, which, first_row, rows, col_count, parity):
    depth, probes = test.shape[1:]
    tile = max(t for t in range(BLOCK, 4 * BLOCK + 1, BLOCK) if rows % t == 0)
    pairs, slab = col_count // 2, BLOCK // col_count
    half = jax.ShapeDtypeStruct((rows // BLOCK, pairs, slab, probes), jnp.float32)
    out_spec = pl.BlockSpec((tile // BLOCK, pairs, slab, probes), lambda i, p: (i, 0, 0, 0))
    skip = first_row // tile
    return pl.pallas_call(
        probe_kernel,
        out_shape=(half, half),
        grid_spec=pltpu.PrefetchScalarGridSpec(
            num_scalar_prefetch=1,
            grid=(rows // tile,),
            in_specs=[
                pl.BlockSpec((None, tile, depth), lambda i, p: (which, skip + i, 0)),
                pl.BlockSpec((None, depth, probes), lambda i, p: (which, 0, 0)),
            ],
            out_specs=(out_spec, out_spec),
        ),
        compiler_params=pltpu.CompilerParams(vmem_limit_bytes=40 << 20),
        cost_estimate=pl.CostEstimate(
            flops=2 * rows * depth * probes,
            bytes_accessed=2 * rows * depth + 2 * depth * probes + 4 * rows * probes,
            transcendentals=0,
        ),
        name="probe",
    )(parity, front, test)


def swap_pair(halves, col_count):
    kept, sent = halves
    return kept, lax.ppermute(sent, "col", [(c, c ^ 1) for c in range(col_count)])


def send_pairs(kept, swapped, col_count, pair_index):
    pairs = col_count // 2

    def piece(pair):
        return lax.dynamic_index_in_dim(kept, pair, 1, False) + lax.dynamic_index_in_dim(
            swapped, pair, 1, False
        )

    came = [
        lax.ppermute(
            piece((pair_index + shift) % pairs).astype(jnp.bfloat16),
            "col",
            [(c, (c + 2 * shift) % col_count) for c in range(col_count)],
        )
        for shift in range(1, pairs)
    ]
    return piece(pair_index), came


def add_up(own, came):
    for term in came:
        own = own + term.astype(jnp.float32)
    return own


def spread(total, parts, grain):
    base = total // grain
    cuts = [base * (i + 1) // parts * grain for i in range(parts)]
    starts = [0] + cuts[:-1]
    return [(s, e - s) for s, e in zip(starts, cuts)]


def sample_kernel(
    dims,
    picks_ref,
    kid_test_hbm,
    test_hbm,
    kids_hbm,
    front_hbm,
    yt_ref,
    kid_test,
    test,
    ring,
    parts,
    kid_sum,
    sums,
    kid_out,
    kid_in,
    kid_in_two,
    out,
    came,
    came_two,
    kids,
    merged,
    landed,
    load_sem,
    test_sem,
    swap_send,
    swap_recv,
    kid_send,
    kid_recv,
    kid_recv_two,
    line_send,
    line_recv,
    line_recv_two,
    row_send,
    row_recv,
    leaf_send,
    leaf_recv,
):
    row_count, col_count, kid_tiles, kid_each, order, slots, subs = dims
    chips = col_count // 2
    probes, rows = yt_ref.shape
    half = probes // 2
    per_leaf = rows // BLOCK
    blocks = merged.shape[0]
    pieces = slots
    row, col = lax.axis_index("row"), lax.axis_index("col")
    chip, core = col // 2, col % 2
    sibling = {"col": chip * 2 + 1 - core}

    def remote(src, dst, send, recv, target):
        return pltpu.make_async_remote_copy(
            src_ref=src, dst_ref=dst, send_sem=send, recv_sem=recv,
            device_id=target, device_id_type=MESH,
        )

    barrier = pltpu.get_barrier_semaphore()
    for shift in range(1, col_count):
        pl.semaphore_signal(
            barrier, inc=1, device_id={"col": (col + shift) % col_count}, device_id_type=MESH
        )
    for shift in range(1, row_count):
        pl.semaphore_signal(
            barrier, inc=1, device_id={"row": (row + shift) % row_count}, device_id_type=MESH
        )

    kid_depth = kid_test.shape[2]
    tiles = kid_tiles + 2 * chips

    def load(index):
        slot = index % 2
        if index < kid_tiles:
            src = kids_hbm.at[index // kid_each, pl.ds(index % kid_each * rows, rows)]
            dst = ring.at[slot, :, pl.ds(0, kid_depth)]
        else:
            pair, kept = order[(index - kid_tiles) // 2], (index - kid_tiles) % 2
            leaf = 2 * pair + (core if kept else 1 - core)
            src = front_hbm.at[pl.ds(pl.multiple_of(leaf * rows, rows), rows)]
            dst = ring.at[slot]
        return pltpu.make_async_copy(src, dst, load_sem.at[slot])

    kid_test_load = pltpu.make_async_copy(kid_test_hbm, kid_test, test_sem.at[0])
    test_load = pltpu.make_async_copy(test_hbm, test, test_sem.at[1])
    kid_test_load.start()
    load(0).start()
    load(1).start()
    test_load.start()
    kid_test_load.wait()

    def multiply(index):
        slot = index % 2
        load(index).wait()
        if index < kid_tiles:
            left, right = kid_test[index // kid_each], ring[slot, :, :kid_depth]
        else:
            left, right = test[...], ring[slot]
        parts[index % 4] = lax.dot_general(
            left, right, (((1,), (1,)), ((), ())), preferred_element_type=jnp.float32
        )
        if index + 2 < tiles:
            load(index + 2).start()

    def kid_swap(tile):
        away = pl.ds(pl.multiple_of((1 - core) * half, half), half)
        return remote(
            parts.at[tile % 4, away], kid_sum.at[tile],
            swap_send.at[tile], swap_recv.at[tile], sibling,
        )

    def swap(pair):
        at = order.index(pair)
        return remote(
            parts.at[(kid_tiles + 2 * at) % 4], sums.at[pair],
            swap_send.at[kid_tiles + at], swap_recv.at[kid_tiles + at], sibling,
        )

    def kid_combine(tile):
        kid_swap(tile).wait_recv()
        own = pl.ds(pl.multiple_of(core * half, half), half)
        kid_sum[tile] += parts[tile % 4, own]

    def combine(pair):
        swap(pair).wait_recv()
        sums[pair] += parts[(kid_tiles + 2 * order.index(pair) + 1) % 4]

    def kid_hop(tile, goal, here, toward=1):
        start, size = pieces[goal]
        step = toward if goal > here else -toward
        span = pl.ds(start, size)
        last = goal == here - 1
        dst = kid_in_two.at[tile, pl.ds(0, size)] if last else kid_in.at[tile, span]
        sem = kid_recv_two.at[tile] if last else kid_recv.at[tile, goal]
        return remote(
            kid_out.at[tile, span], dst, kid_send.at[tile, goal], sem,
            {"col": col + 2 * step},
        )

    def kid_push(tile, goal, here):
        start, size = pieces[goal]
        span = pl.ds(start, size)
        kid_out[tile, span] = kid_sum[tile, span].astype(jnp.bfloat16)
        kid_hop(tile, goal, here).start()

    def kid_take(tile, goal, here):
        start, size = pieces[goal]
        span = pl.ds(start, size)
        if goal >= here > 0:
            kid_hop(tile, goal, here - 1, -1).wait_recv()
            kid_sum[tile, span] += kid_in[tile, span].astype(jnp.float32)
        if goal <= here < chips - 1:
            kid_hop(tile, goal, here + 1, -1).wait_recv()
            if goal == here:
                kid_sum[tile, span] += kid_in_two[tile, :size].astype(jnp.float32)
            else:
                kid_sum[tile, span] += kid_in[tile, span].astype(jnp.float32)

    def kid_share(tile, shift, here, toward=1):
        size = pieces[here][1]
        other = (row + toward * shift + row_count) % row_count
        owner = row if toward == 1 else other
        span = kids.at[pl.ds(owner * blocks + tile * per_leaf, per_leaf), pl.ds(0, size)]
        return remote(
            span, span, row_send.at[tile, shift - 1], row_recv.at[tile, shift - 1],
            {"row": other},
        )

    def is_end(goal, here):
        return (goal > here and here == 0) or (goal < here and here == chips - 1)

    def each_chip(body):
        for here in range(chips):
            pl.when(chip == here)(functools.partial(body, here))

    def kid_head(tile):
        def body(here):
            for goal in range(chips):
                if is_end(goal, here):
                    kid_push(tile, goal, here)

        for here in (0, chips - 1):
            pl.when(chip == here)(functools.partial(body, here))

    def kid_rest(tile):
        def body(here):
            for goal in range(chips):
                if goal != here and not is_end(goal, here):
                    kid_take(tile, goal, here)
                    kid_push(tile, goal, here)
            kid_take(tile, here, here)
            start, size = pieces[here]
            for block in range(per_leaf):
                kids[row * blocks + tile * per_leaf + block, :size] = kid_sum[
                    tile, start : start + size, block * BLOCK : (block + 1) * BLOCK
                ]
            for shift in range(1, row_count):
                kid_share(tile, shift, here).start()

        each_chip(body)

    sub = probes // subs

    def hop(pair, piece, here, toward=1):
        span = pl.ds(piece * sub, sub)
        step = toward if pair > here else -toward
        last = pair == here - 1
        dst = came_two.at[span] if last else came.at[pair, span]
        sem = line_recv_two.at[piece] if last else line_recv.at[pair, piece]
        return remote(
            out.at[pair, span], dst, line_send.at[pair, piece], sem, {"col": col + 2 * step}
        )

    def push(pair, piece, here):
        span = pl.ds(piece * sub, sub)
        out[pair, span] = sums[pair, span].astype(jnp.bfloat16)
        hop(pair, piece, here).start()

    def take(pair, piece, here):
        span = pl.ds(piece * sub, sub)
        if pair >= here > 0:
            hop(pair, piece, here - 1, -1).wait_recv()
            sums[pair, span] += came[pair, span].astype(jnp.float32)
        if pair <= here < chips - 1:
            hop(pair, piece, here + 1, -1).wait_recv()
            if pair == here:
                sums[pair, span] += came_two[span].astype(jnp.float32)
            else:
                sums[pair, span] += came[pair, span].astype(jnp.float32)

    def head(pair):
        for here in (0, chips - 1):
            if is_end(pair, here):

                def body(here=here):
                    for piece in range(subs):
                        push(pair, piece, here)

                pl.when(chip == here)(body)

    def rest(pair):
        def body(here):
            if not is_end(pair, here):
                for piece in range(subs):
                    take(pair, piece, here)
                    if pair != here:
                        push(pair, piece, here)

        each_chip(body)

    kids[row_count * blocks] = jnp.zeros(kids.shape[1:], kids.dtype)

    multiply(0)
    pl.semaphore_wait(barrier, col_count - 1 + row_count - 1)
    kid_swap(0).start()
    for tile in range(1, kid_tiles):
        if tile >= 4:
            kid_swap(tile - 4).wait_send()
        multiply(tile)
        kid_swap(tile).start()
        kid_combine(tile - 1)
        kid_head(tile - 1)
    test_load.wait()
    rests = list(range(kid_tiles))
    for at, pair in enumerate(order):
        for kept in range(2):
            back = kid_tiles + 2 * at + kept - 4
            if back < kid_tiles:
                kid_swap(back).wait_send()
            elif kept == 0:
                swap(order[at - 2]).wait_send()
            multiply(kid_tiles + 2 * at + kept)
            if kept == 0:
                swap(pair).start()
                if at == 0:
                    kid_combine(kid_tiles - 1)
                    kid_head(kid_tiles - 1)
                else:
                    combine(order[at - 1])
                    head(order[at - 1])
            if 2 * at + kept >= 2:
                kid_rest(rests.pop(0))
    combine(order[-1])
    head(order[-1])
    while rests:
        kid_rest(rests.pop(0))
    rest(order[0])
    rest(order[1])

    def leaf_move(shift, here):
        size = pieces[here][1]
        goal = (col + shift) % col_count
        return remote(
            merged.at[pl.ds(goal * per_leaf, per_leaf), pl.ds(0, size)],
            landed.at[col, :, pl.ds(0, size)],
            leaf_send.at[shift - 1], leaf_recv.at[shift - 1], {"col": goal},
        )

    def merge(here):
        size = pieces[here][1]
        for tile in range(kid_tiles):
            for shift in range(1, row_count):
                kid_share(tile, shift, here, -1).wait_recv()

        def one(block, carry):
            first = kids[picks_ref[0, block], :size]
            second = kids[picks_ref[1, block], :size]
            merged[block, :size] = (first + second).astype(jnp.bfloat16)
            return carry

        lax.fori_loop(0, blocks, one, 0)
        for shift in range(1, col_count):
            leaf_move(shift, here).start()
        landed[col, :, :size] = merged[pl.ds(col * per_leaf, per_leaf), :size]

    each_chip(merge)
    for pair in order[2:]:
        rest(pair)

    def land():
        for shift in range(1, col_count):
            source = (col - shift + col_count) % col_count
            far = source // 2
            for there in range(chips):

                def wait(there=there):
                    size = pieces[there][1]
                    remote(
                        merged.at[pl.ds(0, per_leaf), pl.ds(0, size)],
                        landed.at[source, :, pl.ds(0, size)],
                        leaf_send.at[shift - 1], leaf_recv.at[shift - 1], {"col": source},
                    ).wait_recv()

                pl.when(far == there)(wait)

    land()
    for source in range(col_count):
        start, size = pieces[source // 2]
        start += source % 2 * half
        for block in range(per_leaf):
            lanes = pl.ds(block * BLOCK, BLOCK)
            yt_ref[pl.ds(start, size), lanes] = (
                sums[chip, pl.ds(start, size), lanes]
                + landed[source, block, :size].astype(jnp.float32)
            )

    def drain(here):
        for tile in range(kid_tiles):
            for goal in range(chips):
                if goal != here:
                    kid_hop(tile, goal, here).wait_send()
            for shift in range(1, row_count):
                kid_share(tile, shift, here).wait_send()
        for pair in range(chips):
            if pair != here:
                for piece in range(subs):
                    hop(pair, piece, here).wait_send()
        for shift in range(1, col_count):
            leaf_move(shift, here).wait_send()

    each_chip(drain)
    for pair in order[-2:]:
        swap(pair).wait_send()


def sample_of(picks, kid_test, test, kids, front, row_count, col_count):
    depth = front.shape[1]
    probes = test.shape[0]
    kid_rows, kid_depth = kids.shape[1:]
    chips = col_count // 2
    half = probes // 2
    kid_each = kid_rows // LEAF
    kid_tiles = kids.shape[0] * kid_each
    per_leaf = LEAF // BLOCK
    blocks = front.shape[0] // BLOCK
    subs = 4
    pieces = spread(half, chips, 16)
    most = max(size for _, size in pieces)
    low, high, order = 0, chips - 1, []
    while low <= high:
        order += [high] if low == high else [high, low]
        low, high = low + 1, high - 1
    f32, bf16 = jnp.float32, jnp.bfloat16
    dims = (row_count, col_count, kid_tiles, kid_each, tuple(order), tuple(pieces), subs)
    any_spec = pl.BlockSpec(memory_space=pl.ANY)
    dma = pltpu.SemaphoreType.DMA
    return pl.pallas_call(
        functools.partial(sample_kernel, dims),
        out_shape=jax.ShapeDtypeStruct((probes, LEAF), f32),
        in_specs=[pl.BlockSpec(memory_space=pltpu.SMEM)] + [any_spec] * 4,
        out_specs=pl.BlockSpec(memory_space=pltpu.VMEM),
        scratch_shapes=[
            pltpu.VMEM((kids.shape[0], probes, kid_depth), bf16),
            pltpu.VMEM((probes, depth), bf16),
            pltpu.VMEM((2, LEAF, depth), bf16),
            pltpu.VMEM((4, probes, LEAF), f32),
            pltpu.VMEM((kid_tiles, half, LEAF), f32),
            pltpu.VMEM((chips, probes, LEAF), f32),
            pltpu.VMEM((kid_tiles, half, LEAF), bf16),
            pltpu.VMEM((kid_tiles, half, LEAF), bf16),
            pltpu.VMEM((kid_tiles, most, LEAF), bf16),
            pltpu.VMEM((chips, probes, LEAF), bf16),
            pltpu.VMEM((chips, probes, LEAF), bf16),
            pltpu.VMEM((probes, LEAF), bf16),
            pltpu.VMEM((row_count * blocks + 1, most, BLOCK), f32),
            pltpu.VMEM((blocks, most, BLOCK), bf16),
            pltpu.VMEM((col_count, per_leaf, most, BLOCK), bf16),
            dma((2,)),
            dma((2,)),
            dma((kid_tiles + chips,)),
            dma((kid_tiles + chips,)),
            dma((kid_tiles, chips)),
            dma((kid_tiles, chips)),
            dma((kid_tiles,)),
            dma((chips, subs)),
            dma((chips, subs)),
            dma((subs,)),
            dma((kid_tiles, row_count - 1)),
            dma((kid_tiles, row_count - 1)),
            dma((col_count - 1,)),
            dma((col_count - 1,)),
        ],
        compiler_params=pltpu.CompilerParams(
            collective_id=0, has_side_effects=True, vmem_limit_bytes=67043328
        ),
        cost_estimate=pl.CostEstimate(
            flops=4 * front.shape[0] * depth * probes,
            bytes_accessed=4 * front.shape[0] * depth,
            transcendentals=0,
        ),
        name="sample",
    )(picks, kid_test, test, kids, front)


def finish_kernel(
    dims,
    yt_ref,
    front_hbm,
    basis_ref,
    core_ref,
    gram,
    work,
    exact,
    high,
    low,
    near_high,
    near_low,
    far,
    tile,
    slab,
    slab_in,
    stage,
    stage_in,
    tile_send,
    tile_recv,
    near_send,
    near_recv,
    far_send,
    far_recv,
    slab_send,
    slab_recv,
    core_send,
    core_recv,
):
    _, col_count, tile_leaves = dims
    nb = PIVOTS
    chips = col_count // 2
    probes, rows = yt_ref.shape
    per_leaf = rows // BLOCK
    rank_rows = probes // col_count
    groups = slab.shape[0]
    steps = probes // nb
    scale = math.sqrt(LEAF)
    shrink = 1.0 / scale
    row, col = lax.axis_index("row"), lax.axis_index("col")
    chip, core = col // 2, col % 2
    sibling = {"col": chip * 2 + 1 - core}
    at_home = chip == row

    def far_of(pair):
        return (pair >= row + 2) | (pair + 2 <= row)

    def remote(src, dst, send, recv, target):
        return pltpu.make_async_remote_copy(
            src_ref=src, dst_ref=dst, send_sem=send, recv_sem=recv,
            device_id=target, device_id_type=MESH,
        )

    barrier = pltpu.get_barrier_semaphore()
    for shift in range(1, col_count):
        pl.semaphore_signal(
            barrier, inc=1, device_id={"col": (col + shift) % col_count}, device_id_type=MESH
        )
    pl.semaphore_wait(barrier, col_count - 1)

    def tile_source(position):
        slot = core * tile_leaves + (position ^ 1)
        return front_hbm.at[
            pl.ds(pl.multiple_of(slot * rows, rows), rows), pl.ds(position * rows, rows)
        ]

    def each_tile(act):
        for position in range(tile_leaves):
            parity = (position ^ 1) % 2
            pair = (core * tile_leaves + (position ^ 1)) // 2
            slot = pair * 2 + parity
            is_far = far_of(pair)
            goal = jnp.where(is_far, 2 * row + pair % 2, slot)
            for place, chosen in ((0, jnp.logical_not(is_far)), (1 + parity, is_far)):
                here = at_home & chosen & (goal == col)
                there = at_home & chosen & (goal != col)

                def stay(place=place, position=position):
                    act(
                        pltpu.make_async_copy(
                            tile_source(position), tile.at[place], tile_recv.at[place]
                        ),
                        False,
                    )

                def go(place=place, position=position, goal=goal):
                    act(
                        remote(
                            tile_source(position), tile.at[place], tile_send.at[position],
                            tile_recv.at[place], {"col": goal},
                        ),
                        True,
                    )

                pl.when(here)(stay)
                pl.when(there)(go)

    each_tile(lambda copy, away: copy.start())

    work[...] = yt_ref[...]
    gram[...] = dot(yt_ref[...], yt_ref[...], ((1,), (1,)))

    def near_copy(step, which):
        span = pl.ds(pl.multiple_of(step * nb, nb), nb)
        src, dst = ((high, near_high), (low, near_low))[which]
        return remote(
            src.at[span], dst.at[span], near_send.at[which, step], near_recv.at[which, step],
            sibling,
        )

    def far_copy(step, parity):
        span = pl.ds(pl.multiple_of(step * nb, nb), nb)
        return remote(
            high.at[span], far.at[parity, span], far_send.at[step], far_recv.at[parity, step],
            {"col": 2 * row + chip % 2},
        )

    def slab_copy(group, shift, toward=1):
        other = (col + toward * shift + col_count) % col_count
        owner = col if toward == 1 else other
        return remote(
            slab.at[group, other], slab_in.at[group, owner],
            slab_send.at[group, shift], slab_recv.at[group, shift], {"col": other},
        )

    per_slab = BLOCK // col_count

    def send_slabs(group, count):
        start = pl.multiple_of(group * BLOCK, BLOCK)
        for block in range(per_leaf):
            turned = exact[pl.ds(start, count), block * BLOCK : (block + 1) * BLOCK].T
            for goal in range(col_count):
                slab[group, goal, block, :, :count] = turned[
                    goal * per_slab : (goal + 1) * per_slab
                ].astype(slab.dtype)
        for shift in range(1, col_count):
            slab_copy(group, shift).start()
        slab_in[group, col] = slab[group, col]

    def step(index, carry):
        start = pl.multiple_of(index * nb, nb)
        panel = gram[pl.ds(start, nb), :]
        source = lax.broadcasted_iota(jnp.int32, (probes, 2 * nb), 0)
        lane = lax.broadcasted_iota(jnp.int32, (probes, 2 * nb), 1)
        pick = jnp.where((lane >= nb) & (source == lane - nb + start), 1.0, 0.0)
        eye = jnp.where(
            lax.broadcasted_iota(jnp.int32, (nb, 2 * nb), 0)
            == lax.broadcasted_iota(jnp.int32, (nb, 2 * nb), 1),
            1.0,
            0.0,
        )
        inverse = inverse_factor(dot(panel, pick, ((1,), (0,))) + eye, nb)
        top = dot(inverse, panel, ((1,), (0,)))
        solved = dot(inverse, work[pl.ds(start, nb), :], ((1,), (0,)))
        scaled = solved * scale
        rounded = scaled.astype(high.dtype)
        exact[pl.ds(start, nb), :] = scaled
        high[pl.ds(start, nb), :] = rounded
        low[pl.ds(start, nb), :] = (scaled - rounded.astype(jnp.float32)).astype(low.dtype)
        gram[...] -= dot(top, top, ((0,), (0,)))
        work[...] -= dot(top, solved, ((0,), (0,)))

        @pl.when(far_of(chip))
        def _():
            for parity in range(2):
                pl.when(core == parity)(lambda parity=parity: far_copy(index, parity).start())

        @pl.when(jnp.logical_not(far_of(chip)))
        def _():
            near_copy(index, 0).start()
            near_copy(index, 1).start()

        @pl.when(index % 2 == 1)
        def _():
            send_slabs(index // 2, BLOCK)

        return carry

    lax.fori_loop(0, steps, step, 0)
    if steps % 2 == 1:
        send_slabs(groups - 1, nb)

    def times(a, b):
        return lax.dot_general(
            a, b, (((1,), (1,)), ((), ())), preferred_element_type=jnp.float32
        )

    def core_copy(place, goal, slot):
        return remote(
            stage.at[place, goal], stage_in.at[slot], core_send.at[place, goal],
            core_recv.at[slot], {"col": goal},
        )

    def send_core(place, slot, value):
        value = (value * shrink).astype(stage.dtype)
        for goal in range(col_count):
            stage[place, goal, :rank_rows] = value[goal * rank_rows : (goal + 1) * rank_rows]

            @pl.when(goal != col)
            def _(goal=goal):
                core_copy(place, goal, slot).start()

            @pl.when(goal == col)
            def _(goal=goal):
                stage_in[slot] = stage[place, goal]

    def wait_tile(place, source):
        @pl.when(source == col)
        def _():
            pltpu.make_async_copy(
                front_hbm.at[pl.ds(0, rows), pl.ds(0, rows)], tile.at[place],
                tile_recv.at[place],
            ).wait()

        @pl.when(source != col)
        def _():
            remote(
                front_hbm.at[pl.ds(0, rows), pl.ds(0, rows)], tile.at[place], tile_send.at[0],
                tile_recv.at[place], {"col": source},
            ).wait_recv()

    @pl.when(jnp.logical_not(far_of(chip)))
    def _():
        wait_tile(0, 2 * row + col // tile_leaves)
        for index in range(steps):
            near_copy(index, 0).wait_recv()
            near_copy(index, 1).wait_recv()
        product = (times(near_high[...], tile[0]) + times(near_low[...], tile[0])) * shrink
        rounded = product.astype(jnp.bfloat16)
        rest = (product - rounded.astype(jnp.float32)).astype(jnp.bfloat16)
        send_core(
            0, col,
            times(high[...], rounded) + (times(low[...], rounded) + times(high[...], rest)),
        )

    for pair in range(chips):

        @pl.when(at_home & far_of(pair) & (core == pair % 2))
        def _(pair=pair):
            for parity in range(2):
                for index in range(steps):
                    span = pl.ds(index * nb, nb)
                    remote(
                        high.at[span], far.at[parity, span], far_send.at[index],
                        far_recv.at[parity, index], {"col": 2 * pair + parity},
                    ).wait_recv()
            for parity in range(2):
                slot = 2 * pair + parity
                wait_tile(1 + parity, 2 * row + slot // tile_leaves)
                product = times(far[1 - parity], tile[1 + parity]) * shrink
                send_core(1 + parity, slot, times(far[parity], product.astype(jnp.bfloat16)))

    for group in range(groups):
        for shift in range(1, col_count):
            slab_copy(group, shift, -1).wait_recv()
    for slot in range(col_count):
        for group in range(groups):
            count = min(BLOCK, probes - group * BLOCK)
            basis_ref[
                slot * per_leaf : (slot + 1) * per_leaf, :, group * BLOCK : group * BLOCK + count
            ] = slab_in[group, slot, :, :, :count]
    for slot in range(col_count):
        pair = slot // 2
        source = jnp.where(far_of(pair), 2 * row + pair % 2, slot)

        @pl.when(source != col)
        def _(slot=slot, source=source):
            remote(
                stage.at[0, 0], stage_in.at[slot], core_send.at[0, 0], core_recv.at[slot],
                {"col": source},
            ).wait_recv()

        core_ref[slot] = stage_in[slot, :rank_rows].astype(jnp.float32)

    def settle(copy, away):
        if away:
            copy.wait_send()

    each_tile(settle)

    @pl.when(far_of(chip))
    def _():
        for index in range(steps):
            far_copy(index, 0).wait_send()

    @pl.when(jnp.logical_not(far_of(chip)))
    def _():
        for index in range(steps):
            near_copy(index, 0).wait_send()
            near_copy(index, 1).wait_send()
        for goal in range(col_count):
            pl.when(goal != col)(lambda goal=goal: core_copy(0, goal, col).wait_send())

    for group in range(groups):
        for shift in range(1, col_count):
            slab_copy(group, shift).wait_send()
    for pair in range(chips):

        @pl.when(at_home & far_of(pair) & (core == pair % 2))
        def _(pair=pair):
            for parity in range(2):
                for goal in range(col_count):
                    pl.when(goal != col)(
                        lambda goal=goal, parity=parity: core_copy(
                            1 + parity, goal, 2 * pair + parity
                        ).wait_send()
                    )


def finish(yt, front, row_count, col_count):
    probes, rows = yt.shape
    steps = probes // PIVOTS
    per_leaf = rows // BLOCK
    blocks = front.shape[0] // BLOCK
    groups = -(-probes // BLOCK)
    rank_rows = probes // col_count
    padded = -(-rank_rows // 16) * 16
    f32, bf16 = jnp.float32, jnp.bfloat16
    dma = pltpu.SemaphoreType.DMA
    slab = pltpu.VMEM((groups, col_count, per_leaf, BLOCK // col_count, BLOCK), bf16)
    dims = (row_count, col_count, front.shape[1] // LEAF)
    return pl.pallas_call(
        functools.partial(finish_kernel, dims),
        out_shape=(
            jax.ShapeDtypeStruct((blocks, BLOCK // col_count, probes), bf16),
            jax.ShapeDtypeStruct((col_count, rank_rows, probes), f32),
        ),
        in_specs=[
            pl.BlockSpec(memory_space=pltpu.VMEM),
            pl.BlockSpec(memory_space=pl.ANY),
        ],
        out_specs=(
            pl.BlockSpec(memory_space=pltpu.VMEM),
            pl.BlockSpec(memory_space=pltpu.VMEM),
        ),
        scratch_shapes=[
            pltpu.VMEM((probes, probes), f32),
            pltpu.VMEM((probes, rows), f32),
            pltpu.VMEM((probes, rows), f32),
            pltpu.VMEM((probes, rows), bf16),
            pltpu.VMEM((probes, rows), bf16),
            pltpu.VMEM((probes, rows), bf16),
            pltpu.VMEM((probes, rows), bf16),
            pltpu.VMEM((2, probes, rows), bf16),
            pltpu.VMEM((3, rows, rows), bf16),
            slab,
            slab,
            pltpu.VMEM((3, col_count, padded, probes), bf16),
            pltpu.VMEM((col_count, padded, probes), bf16),
            dma((dims[2],)),
            dma((3,)),
            dma((2, steps)),
            dma((2, steps)),
            dma((steps,)),
            dma((2, steps)),
            dma((groups, col_count)),
            dma((groups, col_count)),
            dma((3, col_count)),
            dma((col_count,)),
        ],
        compiler_params=pltpu.CompilerParams(
            collective_id=1, has_side_effects=True, vmem_limit_bytes=56 << 20
        ),
        cost_estimate=pl.CostEstimate(
            flops=40 * probes * probes * rows,
            bytes_accessed=6 * probes * rows,
            transcendentals=0,
        ),
        name="finish",
    )(yt, front)


def general(parent_front, child_update, parent_test, child_test, child_map):
    row_count = lax.axis_size("row")
    col_count = lax.axis_size("col")
    row_index = lax.axis_index("row")
    col_index = lax.axis_index("col")
    slab = BLOCK // col_count
    own_blocks = parent_front.shape[0] // BLOCK
    probes = parent_test.shape[1]
    per_leaf = LEAF // BLOCK
    leaf_count = own_blocks // per_leaf
    col_leaves = parent_front.shape[1] // LEAF
    shrink = 1.0 / math.sqrt(LEAF)

    tie = lax.optimization_barrier
    pair_index = col_index // 2
    parity = col_index % 2
    half = own_blocks // 2 * BLOCK
    sign = jnp.reshape(parity, (1,)).astype(jnp.int32)
    fronts, tests = parent_front[None], parent_test[None]
    kid_rows = child_update.shape[1]

    def send_tile(position, front):
        sibling = col_index * col_leaves + position
        row_start = jnp.bitwise_xor(sibling, 1) % leaf_count * LEAF
        tile = lax.dynamic_slice(front, (row_start, position * LEAF), (LEAF, LEAF))
        routes = []
        for row in range(row_count):
            for slot in range(leaf_count):
                other = (row * leaf_count + slot) ^ 1
                if other % col_leaves == position:
                    routes.append(
                        (row * col_count + other // col_leaves, row * col_count + slot)
                    )
        return lax.ppermute(tile, ("row", "col"), routes)

    pieces = {position: send_tile(position, parent_front) for position in range(0, col_leaves, 2)}

    jobs = (
        (child_update, child_test, 0, 0, kid_rows),
        (child_update, child_test, 1, 0, kid_rows),
        (fronts, tests, 0, 0, half),
        (fronts, tests, 0, half, half),
    )
    sums = []
    for front, test, which, first_row, rows in jobs:
        halves = probe(front, test, which, first_row, rows, col_count, sign)
        kept, swapped = swap_pair(halves, col_count)
        sums.append(send_pairs(kept, swapped, col_count, pair_index))
    (first_own, first_came), (second_own, second_came) = sums[:2]
    (upper_own, upper_came), (lower_own, lower_came) = sums[2:]

    kid_share = jnp.stack([add_up(first_own, first_came), add_up(second_own, second_came)])
    all_kids = lax.all_gather(kid_share, "row", axis=1, tiled=True)
    own_share = jnp.concatenate([add_up(upper_own, upper_came), add_up(lower_own, lower_came)])

    targets = jnp.arange(own_blocks, dtype=jnp.int32)
    mapped = child_map - row_index * own_blocks
    onehot = (mapped[:, None, :] == targets[None, :, None]).astype(jnp.float32)
    sample = own_share + jnp.einsum("cpn,cnsr->psr", onehot, all_kids, precision=HIGH)

    by_leaf = sample.reshape(leaf_count, per_leaf * slab, probes)
    by_leaf = jnp.pad(by_leaf, ((0, col_count - leaf_count), (0, 0), (0, 0)))
    leaf_rows = lax.all_to_all(by_leaf, "col", 0, 0, tiled=True).reshape(LEAF, probes)

    leaf_rows, front = tie((leaf_rows, parent_front))
    for position in range(1, col_leaves, 2):
        pieces[position] = send_tile(position, front)
    wanted = jnp.bitwise_xor(col_index, 1) % col_leaves
    front_tile = pieces[0]
    for position in range(1, col_leaves):
        front_tile = jnp.where(wanted == position, pieces[position], front_tile)

    basis_t = leaf_basis_of(leaf_rows.T)
    basis = basis_t.T
    slabs = lax.all_to_all(
        basis.reshape(col_count, per_leaf * slab, probes), "col", 0, 0, tiled=True
    )
    leaf_basis = slabs[:leaf_count].reshape(own_blocks, slab, probes)

    natural = (
        basis.reshape(col_count, per_leaf, slab, probes)
        .transpose(1, 0, 2, 3)
        .reshape(LEAF, probes)
    )
    sibling_basis = lax.ppermute(natural, "col", [(c, c ^ 1) for c in range(col_count)])
    product = jnp.dot(front_tile, sibling_basis, preferred_element_type=jnp.float32) * shrink
    core = (
        lax.dot_general(
            natural,
            product.astype(jnp.bfloat16),
            (((0,), (0,)), ((), ())),
            preferred_element_type=jnp.float32,
        )
        * shrink
    )
    cores = lax.all_to_all(
        core.reshape(col_count, probes // col_count, probes), "col", 0, 0, tiled=True
    )
    return (leaf_basis, cores[:leaf_count])


def fits(parent_front, child_update, row_count, col_count):
    leaf_count = parent_front.shape[0] // LEAF
    return (
        leaf_count == col_count
        and row_count * 2 == col_count
        and all(
            sum(abs(pair - row) > 1 and pair % 2 == core for pair in range(row_count)) < 2
            for row in range(row_count)
            for core in range(2)
        )
        and parent_front.shape[1] // LEAF * 2 == leaf_count
        and col_count % 2 == 0
        and parent_front.shape[1] % LEAF == 0
        and child_update.shape[1] % LEAF == 0
        and 2 * parent_front.shape[1] * LEAF * 2 < 16 << 20
    )


def picks_of(child_map, row_index, row_count, own_blocks):
    kid_count, kid_blocks = child_map.shape
    each = kid_blocks // row_count
    at = jnp.arange(kid_blocks, dtype=jnp.int32)
    which = jnp.arange(kid_count, dtype=jnp.int32)
    value = (at // each * own_blocks + at % each)[None, :] + which[:, None] * each
    targets = jnp.arange(own_blocks, dtype=jnp.int32)
    match = (child_map - row_index * own_blocks)[:, None, :] == targets[None, :, None]
    found = jnp.max(jnp.where(match, value[:, None, :], -1), axis=2)
    return jnp.where(found < 0, row_count * own_blocks, found)


def local(parent_front, child_update, parent_test, child_test, child_map):
    row_count = lax.axis_size("row")
    col_count = lax.axis_size("col")
    if not fits(parent_front, child_update, row_count, col_count):
        return general(parent_front, child_update, parent_test, child_test, child_map)
    row_index = lax.axis_index("row")
    own_blocks = parent_front.shape[0] // BLOCK
    picks = picks_of(child_map, row_index, row_count, own_blocks)
    yt = sample_of(
        picks, child_test.transpose(0, 2, 1), parent_test.T, child_update, parent_front,
        row_count, col_count,
    )
    return tuple(finish(yt, parent_front, row_count, col_count))


def solution(mesh):
    in_specs = (P("row", "col"), P(None, "row", "col"), P("col", None), P(None, "col", None), P())
    out_specs = (P("row", "col", None), P("row", "col", None))
    return jax.shard_map(local, mesh=mesh, in_specs=in_specs, out_specs=out_specs, check_vma=False)
```

```python
import functools
import math

import jax
import jax.numpy as jnp
from jax import lax
from jax.experimental import pallas as pl
from jax.experimental.pallas import tpu as pltpu
from jax.sharding import PartitionSpec as P


LEAF = 896
BLOCK = 128
PIVOTS = 64
GROUP = 4

HIGH = lax.Precision.HIGHEST
MESH = pl.DeviceIdType.MESH


def dot(a, b, dims):
    return lax.dot_general(
        a, b, (dims, ((), ())), precision=HIGH, preferred_element_type=jnp.float32
    )


def inverse_factor(tile, nb):
    ridx = lax.broadcasted_iota(jnp.int32, tile.shape, 0)
    lane = lax.broadcasted_iota(jnp.int32, tile.shape, 1)
    for j in range(0, nb, GROUP):
        cols = [
            jnp.broadcast_to(tile[:, nb + j + k : nb + j + k + 1], tile.shape)
            for k in range(GROUP)
        ]
        rows = [tile[j + k : j + k + 1, :] for k in range(GROUP)]
        for k in range(GROUP):
            at = j + k
            factor = jnp.where(ridx > at, cols[k] * (1.0 / cols[k][at : at + 1, :]), 0.0)
            for m in range(k + 1, GROUP):
                cols[m] = cols[m] - factor * cols[m][at : at + 1, :]
                rows[m] = rows[m] - factor[j + m : j + m + 1, :] * rows[k]
            cols[k] = factor
        for k in range(GROUP):
            tile = tile - cols[k] * rows[k]
    pivots = jnp.sum(jnp.where(lane == ridx + nb, tile, 0.0), axis=1, keepdims=True)
    return tile[:, :nb] * lax.rsqrt(pivots)


def basis_kernel(scale, yt_ref, qt_ref, gram_ref, work_ref):
    nb = PIVOTS
    probes = yt_ref.shape[0]
    work_ref[...] = yt_ref[...]
    gram_ref[...] = dot(yt_ref[...], yt_ref[...], ((1,), (1,)))

    def step(index, carry):
        start = pl.multiple_of(index * nb, nb)
        panel = gram_ref[pl.ds(start, nb), :]
        source = lax.broadcasted_iota(jnp.int32, (probes, 2 * nb), 0)
        lane = lax.broadcasted_iota(jnp.int32, (probes, 2 * nb), 1)
        pick = jnp.where((lane >= nb) & (source == lane - nb + start), 1.0, 0.0)
        eye = jnp.where(
            lax.broadcasted_iota(jnp.int32, (nb, 2 * nb), 0)
            == lax.broadcasted_iota(jnp.int32, (nb, 2 * nb), 1),
            1.0,
            0.0,
        )
        inverse = inverse_factor(dot(panel, pick, ((1,), (0,))) + eye, nb)
        top = dot(inverse, panel, ((1,), (0,)))
        solved = dot(inverse, work_ref[pl.ds(start, nb), :], ((1,), (0,)))
        qt_ref[pl.ds(start, nb), :] = (solved * scale).astype(qt_ref.dtype)
        gram_ref[...] -= dot(top, top, ((0,), (0,)))
        work_ref[...] -= dot(top, solved, ((0,), (0,)))
        return carry

    lax.fori_loop(0, probes // nb, step, 0)


def leaf_basis_of(yt):
    probes, rows = yt.shape
    return pl.pallas_call(
        functools.partial(basis_kernel, math.sqrt(LEAF)),
        out_shape=jax.ShapeDtypeStruct((probes, rows), jnp.bfloat16),
        in_specs=[pl.BlockSpec(memory_space=pltpu.VMEM)],
        out_specs=pl.BlockSpec(memory_space=pltpu.VMEM),
        scratch_shapes=[
            pltpu.VMEM((probes, probes), jnp.float32),
            pltpu.VMEM((probes, rows), jnp.float32),
        ],
        compiler_params=pltpu.CompilerParams(vmem_limit_bytes=40 << 20),
        cost_estimate=pl.CostEstimate(
            flops=40 * probes * probes * rows,
            bytes_accessed=6 * probes * rows,
            transcendentals=0,
        ),
        name="leaf_basis",
    )(yt)


def probe_kernel(parity_ref, front_ref, test_ref, kept_ref, sent_ref):
    total = jnp.dot(front_ref[...], test_ref[...], preferred_element_type=jnp.float32)
    blocks, pairs, slab, probes = kept_ref.shape
    view = total.reshape(blocks * pairs, 2, slab, probes)
    even = parity_ref[0] == 0
    kept_ref[...] = jnp.where(even, view[:, 0], view[:, 1]).reshape(kept_ref.shape)
    sent_ref[...] = jnp.where(even, view[:, 1], view[:, 0]).reshape(sent_ref.shape)


def probe(front, test, which, first_row, rows, col_count, parity):
    depth, probes = test.shape[1:]
    tile = max(t for t in range(BLOCK, 4 * BLOCK + 1, BLOCK) if rows % t == 0)
    pairs, slab = col_count // 2, BLOCK // col_count
    half = jax.ShapeDtypeStruct((rows // BLOCK, pairs, slab, probes), jnp.float32)
    out_spec = pl.BlockSpec((tile // BLOCK, pairs, slab, probes), lambda i, p: (i, 0, 0, 0))
    skip = first_row // tile
    return pl.pallas_call(
        probe_kernel,
        out_shape=(half, half),
        grid_spec=pltpu.PrefetchScalarGridSpec(
            num_scalar_prefetch=1,
            grid=(rows // tile,),
            in_specs=[
                pl.BlockSpec((None, tile, depth), lambda i, p: (which, skip + i, 0)),
                pl.BlockSpec((None, depth, probes), lambda i, p: (which, 0, 0)),
            ],
            out_specs=(out_spec, out_spec),
        ),
        compiler_params=pltpu.CompilerParams(vmem_limit_bytes=40 << 20),
        cost_estimate=pl.CostEstimate(
            flops=2 * rows * depth * probes,
            bytes_accessed=2 * rows * depth + 2 * depth * probes + 4 * rows * probes,
            transcendentals=0,
        ),
        name="probe",
    )(parity, front, test)


def swap_pair(halves, col_count):
    kept, sent = halves
    return kept, lax.ppermute(sent, "col", [(c, c ^ 1) for c in range(col_count)])


def send_pairs(kept, swapped, col_count, pair_index):
    pairs = col_count // 2

    def piece(pair):
        return lax.dynamic_index_in_dim(kept, pair, 1, False) + lax.dynamic_index_in_dim(
            swapped, pair, 1, False
        )

    came = [
        lax.ppermute(
            piece((pair_index + shift) % pairs).astype(jnp.bfloat16),
            "col",
            [(c, (c + 2 * shift) % col_count) for c in range(col_count)],
        )
        for shift in range(1, pairs)
    ]
    return piece(pair_index), came


def add_up(own, came):
    for term in came:
        own = own + term.astype(jnp.float32)
    return own


def spread(total, parts, grain):
    base = total // grain
    cuts = [base * (i + 1) // parts * grain for i in range(parts)]
    starts = [0] + cuts[:-1]
    return [(s, e - s) for s, e in zip(starts, cuts)]


def sample_kernel(
    dims,
    picks_ref,
    kid_test_hbm,
    test_hbm,
    kids_hbm,
    front_hbm,
    yt_ref,
    kid_test,
    test,
    ring,
    parts,
    kid_sum,
    sums,
    kid_in,
    kid_in_two,
    came,
    came_two,
    kids,
    merged,
    landed,
    load_sem,
    test_sem,
    swap_send,
    swap_recv,
    kid_send,
    kid_recv,
    kid_recv_two,
    line_send,
    line_recv,
    line_recv_two,
    row_send,
    row_recv,
    leaf_send,
    leaf_recv,
):
    row_count, col_count, kid_tiles, kid_each, order, slots, subs = dims
    chips = col_count // 2
    probes, rows = yt_ref.shape
    half = probes // 2
    per_leaf = rows // BLOCK
    blocks = merged.shape[0]
    pieces = slots
    row, col = lax.axis_index("row"), lax.axis_index("col")
    chip, core = col // 2, col % 2
    sibling = {"col": chip * 2 + 1 - core}

    def remote(src, dst, send, recv, target):
        return pltpu.make_async_remote_copy(
            src_ref=src, dst_ref=dst, send_sem=send, recv_sem=recv,
            device_id=target, device_id_type=MESH,
        )

    barrier = pltpu.get_barrier_semaphore()
    for shift in range(1, col_count):
        pl.semaphore_signal(
            barrier, inc=1, device_id={"col": (col + shift) % col_count}, device_id_type=MESH
        )
    for shift in range(1, row_count):
        pl.semaphore_signal(
            barrier, inc=1, device_id={"row": (row + shift) % row_count}, device_id_type=MESH
        )

    kid_depth = kid_test.shape[2]

    def pair_at(at):
        return jnp.where(at % 2 == 0, chips - 1 - at // 2, at // 2)

    def load_kid(index):
        index = jnp.asarray(index, jnp.int32)
        start = pl.multiple_of(index % kid_each * rows, rows)
        return pltpu.make_async_copy(
            kids_hbm.at[index // kid_each, pl.ds(start, rows)],
            ring.at[index % 2, :, pl.ds(0, kid_depth)],
            load_sem.at[index % 2],
        )

    def load_front(index):
        index = jnp.asarray(index, jnp.int32)
        leaf = 2 * pair_at(index // 2) + jnp.where(index % 2 == 0, 1 - core, core)
        return pltpu.make_async_copy(
            front_hbm.at[pl.ds(pl.multiple_of(leaf * rows, rows), rows)],
            ring.at[index % 2],
            load_sem.at[index % 2],
        )

    kid_test_load = pltpu.make_async_copy(kid_test_hbm, kid_test, test_sem.at[0])
    test_load = pltpu.make_async_copy(test_hbm, test, test_sem.at[1])
    load_kid(0).start()
    kid_test_load.start()
    load_kid(1).start()
    test_load.start()
    kid_test_load.wait()

    def product(left, right):
        return lax.dot_general(
            left, right, (((1,), (1,)), ((), ())), preferred_element_type=jnp.float32
        )

    def kid_swap(tile):
        away = pl.ds(pl.multiple_of((1 - core) * half, half), half)
        return remote(
            parts.at[tile % 4, away], kid_sum.at[tile],
            swap_send.at[tile], swap_recv.at[tile], sibling,
        )

    def swap(at):
        return remote(
            parts.at[2 * at % 4], sums.at[pair_at(at)],
            swap_send.at[kid_tiles + at], swap_recv.at[kid_tiles + at], sibling,
        )

    def kid_combine(tile):
        kid_swap(tile).wait_recv()
        own = pl.ds(pl.multiple_of(core * half, half), half)
        kid_sum[tile] += parts[tile % 4, own]

    def combine(at):
        swap(at).wait_recv()
        sums[pair_at(at)] += parts[(2 * at + 1) % 4]

    def kid_hop(tile, goal, right, last, target):
        start, size = pieces[goal]
        span = pl.ds(start, size)
        two = last and not right
        dst = kid_in_two.at[tile, pl.ds(0, size)] if two else kid_in.at[tile, span]
        sem = kid_recv_two.at[tile] if two else kid_recv.at[tile, goal]
        return remote(
            kid_in.at[tile, span], dst, kid_send.at[tile, goal], sem, {"col": target}
        )

    def kid_push(tile, goal, here):
        start, size = pieces[goal]
        span = pl.ds(start, size)
        right = goal > here
        last = goal == here + 1 if right else goal == here - 1
        kid_in[tile, span] = kid_sum[tile, span].astype(jnp.bfloat16)
        kid_hop(tile, goal, right, last, col + 2 if right else col - 2).start()

    def kid_take(tile, goal, here, right):
        start, size = pieces[goal]
        span = pl.ds(start, size)
        last = goal == here
        kid_hop(tile, goal, right, last, col - 2 if right else col + 2).wait_recv()
        if last and not right:
            kid_sum[tile, span] += kid_in_two[tile, :size].astype(jnp.float32)
        else:
            kid_sum[tile, span] += kid_in[tile, span].astype(jnp.float32)

    def kid_share(tile, shift, here, toward=1):
        size = pieces[here][1]
        other = (row + toward * shift + row_count) % row_count
        owner = row if toward == 1 else other
        span = kids.at[pl.ds(owner * blocks + tile * per_leaf, per_leaf), pl.ds(0, size)]
        return remote(
            span, span, row_send.at[tile, shift - 1], row_recv.at[tile, shift - 1],
            {"row": other},
        )

    def on_chip(here, body):
        pl.when(chip == here)(body)

    def each_chip(body):
        for here in range(chips):
            on_chip(here, functools.partial(body, here))

    end = chips - 1

    def kid_head(tile):
        def right():
            for goal in reversed(range(1, chips)):
                kid_push(tile, goal, 0)

        def left():
            for goal in range(end):
                kid_push(tile, goal, end)

        on_chip(0, right)
        on_chip(end, left)

    def kid_stage(stage, tile):
        def right():
            for goal in reversed(range(stage + 1, chips)):
                kid_take(tile, goal, stage, True)
                kid_push(tile, goal, stage)

        def left():
            for goal in range(end - stage):
                kid_take(tile, goal, end - stage, False)
                kid_push(tile, goal, end - stage)

        def final(here):
            if here > 0:
                kid_take(tile, here, here, True)
            if here < end:
                kid_take(tile, here, here, False)
            start, size = pieces[here]
            for block in range(per_leaf):
                kids[row * blocks + tile * per_leaf + block, :size] = kid_sum[
                    tile, start : start + size, block * BLOCK : (block + 1) * BLOCK
                ]
            for shift in range(1, row_count):
                kid_share(tile, shift, here).start()

        if stage < end:
            on_chip(stage, right)
            on_chip(end - stage, left)
        for here in range(chips):
            if max(here, end - here) == stage:
                on_chip(here, functools.partial(final, here))

    sub = probes // subs

    def hop(pair, piece, right, last, target):
        span = pl.ds(pl.multiple_of(piece * sub, sub), sub)
        two = last and not right
        dst = came_two.at[span] if two else came.at[pair, span]
        sem = line_recv_two.at[piece] if two else line_recv.at[pair, piece]
        return remote(
            came.at[pair, span], dst, line_send.at[pair, piece], sem, {"col": target}
        )

    def push(pair, piece, here):
        span = pl.ds(pl.multiple_of(piece * sub, sub), sub)
        right = pair > here
        last = pair == here + 1 if right else pair == here - 1
        came[pair, span] = sums[pair, span].astype(jnp.bfloat16)
        hop(pair, piece, right, last, col + 2 if right else col - 2).start()

    def take(pair, piece, here, right):
        span = pl.ds(pl.multiple_of(piece * sub, sub), sub)
        last = pair == here
        hop(pair, piece, right, last, col - 2 if right else col + 2).wait_recv()
        if last and not right:
            sums[pair, span] += came_two[span].astype(jnp.float32)
        else:
            sums[pair, span] += came[pair, span].astype(jnp.float32)

    def head(pair, here):
        def body():
            def one(piece, carry):
                push(pair, piece, here)
                return carry

            lax.fori_loop(0, subs, one, 0)

        on_chip(here, body)

    def stage_of(stage, pair, piece):
        def right():
            take(pair, piece, stage, True)
            push(pair, piece, stage)

        def left():
            take(pair, piece, end - stage, False)
            push(pair, piece, end - stage)

        def final():
            if pair > 0:
                take(pair, piece, pair, True)
            if pair < end:
                take(pair, piece, pair, False)

        if pair > stage and stage < end:
            on_chip(stage, right)
        if pair < end - stage and stage < end:
            on_chip(end - stage, left)
        if max(pair, end - pair) == stage:
            on_chip(pair, final)

    def chain(pairs):
        deepest = max(max(pair, end - pair) for pair in pairs)

        def one(turn, carry):
            for stage in range(1, deepest + 1):
                at = turn - (stage - 1)

                @pl.when((at >= 0) & (at < subs))
                def _(stage=stage, at=at):
                    for pair in pairs:
                        stage_of(stage, pair, at)

            return carry

        lax.fori_loop(0, subs + deepest - 1, one, 0)

    kids[row_count * blocks] = jnp.zeros(kids.shape[1:], kids.dtype)

    def kid_turn(tile, carry):
        pl.when(tile >= 4)(lambda: kid_swap(tile - 4).wait_send())
        load_kid(tile).wait()
        parts[tile % 4] = product(kid_test[tile // kid_each], ring[tile % 2, :, :kid_depth])
        pl.when(tile + 2 < kid_tiles)(lambda: load_kid(tile + 2).start())
        pl.when(tile + 2 >= kid_tiles)(lambda: load_front(tile + 2 - kid_tiles).start())

        @pl.when(tile == 0)
        def _():
            pl.semaphore_wait(barrier, col_count - 1 + row_count - 1)

        kid_swap(tile).start()

        @pl.when(tile > 0)
        def _():
            kid_combine(tile - 1)
            kid_head(tile - 1)

        return carry

    lax.fori_loop(0, kid_tiles, kid_turn, 0)
    test_load.wait()
    turns = 2 * chips

    def turn_of(index, carry):
        at = index // 2

        @pl.when(index < 4)
        def _():
            kid_swap(kid_tiles + index - 4).wait_send()

        @pl.when((index >= 4) & (index % 2 == 0))
        def _():
            swap(at - 2).wait_send()

        load_front(index).wait()
        parts[index % 4] = product(test[...], ring[index % 2])
        pl.when(index + 2 < turns)(lambda: load_front(index + 2).start())

        @pl.when(index % 2 == 0)
        def _():
            swap(at).start()

        @pl.when(index == 0)
        def _():
            kid_combine(kid_tiles - 1)
            kid_head(kid_tiles - 1)

        @pl.when((index % 2 == 0) & (index > 0))
        def _():
            combine(at - 1)

        for spot in range(chips - 1):

            @pl.when(index == 2 * spot + 2)
            def _(spot=spot):
                if order[spot] > 0:
                    head(order[spot], 0)
                if order[spot] < end and spot < chips - 2:
                    head(order[spot], end)

        for stage in range(1, chips):
            tile = index - (stage - 1)
            pl.when((tile >= 0) & (tile < kid_tiles))(
                functools.partial(kid_stage, stage, tile)
            )
        return carry

    lax.fori_loop(0, turns, turn_of, 0)
    combine(chips - 1)
    if order[-1] > 0:
        head(order[-1], 0)
    for pair in (order[-1], order[-2]):
        if pair < end:
            head(pair, end)

    def tail_turn(index, carry):
        for stage in range(1, chips):
            tile = index - (stage - 1)
            pl.when((tile >= 0) & (tile < kid_tiles))(
                functools.partial(kid_stage, stage, tile)
            )
        return carry

    lax.fori_loop(turns, kid_tiles + chips - 2, tail_turn, 0)
    chain(order[:2])
    chain(order[2:])

    def leaf_move(shift, here):
        size = pieces[here][1]
        goal = (col + shift) % col_count
        return remote(
            merged.at[pl.ds(goal * per_leaf, per_leaf), pl.ds(0, size)],
            landed.at[col, :, pl.ds(0, size)],
            leaf_send.at[shift - 1], leaf_recv.at[shift - 1], {"col": goal},
        )

    def merge(here):
        size = pieces[here][1]

        def arrive(tile, carry):
            for shift in range(1, row_count):
                kid_share(tile, shift, here, -1).wait_recv()
            return carry

        lax.fori_loop(0, kid_tiles, arrive, 0)

        def one(block, carry):
            first = kids[picks_ref[0, block], :size]
            second = kids[picks_ref[1, block], :size]
            merged[block, :size] = (first + second).astype(jnp.bfloat16)
            return carry

        lax.fori_loop(0, blocks, one, 0)
        for shift in range(1, col_count):
            leaf_move(shift, here).start()
        landed[col, :, :size] = merged[pl.ds(col * per_leaf, per_leaf), :size]

    each_chip(merge)

    def land():
        for shift in range(1, col_count):
            source = (col - shift + col_count) % col_count
            far = source // 2
            for there in range(chips):

                def wait(there=there):
                    size = pieces[there][1]
                    remote(
                        merged.at[pl.ds(0, per_leaf), pl.ds(0, size)],
                        landed.at[source, :, pl.ds(0, size)],
                        leaf_send.at[shift - 1], leaf_recv.at[shift - 1], {"col": source},
                    ).wait_recv()

                pl.when(far == there)(wait)

    land()
    for source in range(col_count):
        start, size = pieces[source // 2]
        start += source % 2 * half
        for block in range(per_leaf):
            lanes = pl.ds(block * BLOCK, BLOCK)
            yt_ref[pl.ds(start, size), lanes] = (
                sums[chip, pl.ds(start, size), lanes]
                + landed[source, block, :size].astype(jnp.float32)
            )

    def drain(here):
        def one(tile, carry):
            for goal in range(chips):
                if goal != here:
                    kid_hop(tile, goal, goal > here, False, col).wait_send()
            for shift in range(1, row_count):
                kid_share(tile, shift, here).wait_send()
            return carry

        lax.fori_loop(0, kid_tiles, one, 0)
        for pair in range(chips):
            if pair != here:
                for piece in range(subs):
                    hop(pair, piece, pair > here, False, col).wait_send()
        for shift in range(1, col_count):
            leaf_move(shift, here).wait_send()

    each_chip(drain)
    for at in range(chips - 2, chips):
        swap(at).wait_send()


def sample_of(picks, kid_test, test, kids, front, row_count, col_count):
    depth = front.shape[1]
    probes = test.shape[0]
    kid_rows, kid_depth = kids.shape[1:]
    chips = col_count // 2
    half = probes // 2
    kid_each = kid_rows // LEAF
    kid_tiles = kids.shape[0] * kid_each
    per_leaf = LEAF // BLOCK
    blocks = front.shape[0] // BLOCK
    subs = 4
    pieces = spread(half, chips, 16)
    most = max(size for _, size in pieces)
    low, high, order = 0, chips - 1, []
    while low <= high:
        order += [high] if low == high else [high, low]
        low, high = low + 1, high - 1
    f32, bf16 = jnp.float32, jnp.bfloat16
    dims = (row_count, col_count, kid_tiles, kid_each, tuple(order), tuple(pieces), subs)
    any_spec = pl.BlockSpec(memory_space=pl.ANY)
    dma = pltpu.SemaphoreType.DMA
    return pl.pallas_call(
        functools.partial(sample_kernel, dims),
        out_shape=jax.ShapeDtypeStruct((probes, LEAF), f32),
        in_specs=[pl.BlockSpec(memory_space=pltpu.SMEM)] + [any_spec] * 4,
        out_specs=pl.BlockSpec(memory_space=pltpu.VMEM),
        scratch_shapes=[
            pltpu.VMEM((kids.shape[0], probes, kid_depth), bf16),
            pltpu.VMEM((probes, depth), bf16),
            pltpu.VMEM((2, LEAF, depth), bf16),
            pltpu.VMEM((4, probes, LEAF), f32),
            pltpu.VMEM((kid_tiles, half, LEAF), f32),
            pltpu.VMEM((chips, probes, LEAF), f32),
            pltpu.VMEM((kid_tiles, half, LEAF), bf16),
            pltpu.VMEM((kid_tiles, most, LEAF), bf16),
            pltpu.VMEM((chips, probes, LEAF), bf16),
            pltpu.VMEM((probes, LEAF), bf16),
            pltpu.VMEM((row_count * blocks + 1, most, BLOCK), f32),
            pltpu.VMEM((blocks, most, BLOCK), bf16),
            pltpu.VMEM((col_count, per_leaf, most, BLOCK), bf16),
            dma((2,)),
            dma((2,)),
            dma((kid_tiles + chips,)),
            dma((kid_tiles + chips,)),
            dma((kid_tiles, chips)),
            dma((kid_tiles, chips)),
            dma((kid_tiles,)),
            dma((chips, subs)),
            dma((chips, subs)),
            dma((subs,)),
            dma((kid_tiles, row_count - 1)),
            dma((kid_tiles, row_count - 1)),
            dma((col_count - 1,)),
            dma((col_count - 1,)),
        ],
        compiler_params=pltpu.CompilerParams(
            collective_id=0, has_side_effects=True, vmem_limit_bytes=67043328
        ),
        cost_estimate=pl.CostEstimate(
            flops=4 * front.shape[0] * depth * probes,
            bytes_accessed=4 * front.shape[0] * depth,
            transcendentals=0,
        ),
        name="sample",
    )(picks, kid_test, test, kids, front)


def finish_kernel(
    dims,
    yt_ref,
    front_hbm,
    basis_ref,
    core_ref,
    gram,
    work,
    exact,
    high,
    low,
    near_high,
    near_low,
    far,
    tile,
    slab,
    slab_in,
    stage,
    stage_in,
    tile_send,
    tile_recv,
    near_send,
    near_recv,
    far_send,
    far_recv,
    slab_send,
    slab_recv,
    core_send,
    core_recv,
):
    _, col_count, tile_leaves = dims
    nb = PIVOTS
    chips = col_count // 2
    probes, rows = yt_ref.shape
    per_leaf = rows // BLOCK
    rank_rows = probes // col_count
    groups = slab.shape[0]
    steps = probes // nb
    scale = math.sqrt(LEAF)
    shrink = 1.0 / scale
    row, col = lax.axis_index("row"), lax.axis_index("col")
    chip, core = col // 2, col % 2
    sibling = {"col": chip * 2 + 1 - core}
    at_home = chip == row

    def far_of(pair):
        return (pair >= row + 2) | (pair + 2 <= row)

    def remote(src, dst, send, recv, target):
        return pltpu.make_async_remote_copy(
            src_ref=src, dst_ref=dst, send_sem=send, recv_sem=recv,
            device_id=target, device_id_type=MESH,
        )

    barrier = pltpu.get_barrier_semaphore()
    for shift in range(1, col_count):
        pl.semaphore_signal(
            barrier, inc=1, device_id={"col": (col + shift) % col_count}, device_id_type=MESH
        )
    pl.semaphore_wait(barrier, col_count - 1)

    def tile_source(position):
        slot = core * tile_leaves + (position ^ 1)
        return front_hbm.at[
            pl.ds(pl.multiple_of(slot * rows, rows), rows), pl.ds(position * rows, rows)
        ]

    def each_tile(act):
        for position in range(tile_leaves):
            parity = (position ^ 1) % 2
            pair = (core * tile_leaves + (position ^ 1)) // 2
            slot = pair * 2 + parity
            is_far = far_of(pair)
            goal = jnp.where(is_far, 2 * row + pair % 2, slot)
            for place, chosen in ((0, jnp.logical_not(is_far)), (1 + parity, is_far)):
                here = at_home & chosen & (goal == col)
                there = at_home & chosen & (goal != col)

                def stay(place=place, position=position):
                    act(
                        pltpu.make_async_copy(
                            tile_source(position), tile.at[place], tile_recv.at[place]
                        ),
                        False,
                    )

                def go(place=place, position=position, goal=goal):
                    act(
                        remote(
                            tile_source(position), tile.at[place], tile_send.at[position],
                            tile_recv.at[place], {"col": goal},
                        ),
                        True,
                    )

                pl.when(here)(stay)
                pl.when(there)(go)

    each_tile(lambda copy, away: copy.start())

    work[...] = yt_ref[...]
    gram[...] = dot(yt_ref[...], yt_ref[...], ((1,), (1,)))

    def near_copy(step, which):
        span = pl.ds(pl.multiple_of(step * nb, nb), nb)
        src, dst = ((high, near_high), (low, near_low))[which]
        return remote(
            src.at[span], dst.at[span], near_send.at[which, step], near_recv.at[which, step],
            sibling,
        )

    def far_copy(step, parity):
        span = pl.ds(pl.multiple_of(step * nb, nb), nb)
        return remote(
            high.at[span], far.at[parity, span], far_send.at[step], far_recv.at[parity, step],
            {"col": 2 * row + chip % 2},
        )

    def slab_copy(group, shift, toward=1):
        other = (col + toward * shift + col_count) % col_count
        owner = col if toward == 1 else other
        return remote(
            slab.at[group, other], slab_in.at[group, owner],
            slab_send.at[group, shift], slab_recv.at[group, shift], {"col": other},
        )

    per_slab = BLOCK // col_count

    def send_slabs(group, count):
        start = pl.multiple_of(group * BLOCK, BLOCK)
        for block in range(per_leaf):
            turned = exact[pl.ds(start, count), block * BLOCK : (block + 1) * BLOCK].T
            for goal in range(col_count):
                slab[group, goal, block, :, :count] = turned[
                    goal * per_slab : (goal + 1) * per_slab
                ].astype(slab.dtype)
        for shift in range(1, col_count):
            slab_copy(group, shift).start()
        slab_in[group, col] = slab[group, col]

    def step(index, carry):
        start = pl.multiple_of(index * nb, nb)
        panel = gram[pl.ds(start, nb), :]
        source = lax.broadcasted_iota(jnp.int32, (probes, 2 * nb), 0)
        lane = lax.broadcasted_iota(jnp.int32, (probes, 2 * nb), 1)
        pick = jnp.where((lane >= nb) & (source == lane - nb + start), 1.0, 0.0)
        eye = jnp.where(
            lax.broadcasted_iota(jnp.int32, (nb, 2 * nb), 0)
            == lax.broadcasted_iota(jnp.int32, (nb, 2 * nb), 1),
            1.0,
            0.0,
        )
        inverse = inverse_factor(dot(panel, pick, ((1,), (0,))) + eye, nb)
        top = dot(inverse, panel, ((1,), (0,)))
        solved = dot(inverse, work[pl.ds(start, nb), :], ((1,), (0,)))
        scaled = solved * scale
        rounded = scaled.astype(high.dtype)
        exact[pl.ds(start, nb), :] = scaled
        high[pl.ds(start, nb), :] = rounded
        low[pl.ds(start, nb), :] = (scaled - rounded.astype(jnp.float32)).astype(low.dtype)
        gram[...] -= dot(top, top, ((0,), (0,)))
        work[...] -= dot(top, solved, ((0,), (0,)))

        @pl.when(far_of(chip))
        def _():
            for parity in range(2):
                pl.when(core == parity)(lambda parity=parity: far_copy(index, parity).start())

        @pl.when(jnp.logical_not(far_of(chip)))
        def _():
            near_copy(index, 0).start()
            near_copy(index, 1).start()

        @pl.when(index % 2 == 1)
        def _():
            send_slabs(index // 2, BLOCK)

        return carry

    lax.fori_loop(0, steps, step, 0)
    if steps % 2 == 1:
        send_slabs(groups - 1, nb)

    def times(a, b):
        return lax.dot_general(
            a, b, (((1,), (1,)), ((), ())), preferred_element_type=jnp.float32
        )

    def core_copy(place, goal, slot):
        return remote(
            stage.at[place, goal], stage_in.at[slot], core_send.at[place, goal],
            core_recv.at[slot], {"col": goal},
        )

    def send_core(place, slot, value):
        value = (value * shrink).astype(stage.dtype)
        for goal in range(col_count):
            stage[place, goal, :rank_rows] = value[goal * rank_rows : (goal + 1) * rank_rows]

            @pl.when(goal != col)
            def _(goal=goal):
                core_copy(place, goal, slot).start()

            @pl.when(goal == col)
            def _(goal=goal):
                stage_in[slot] = stage[place, goal]

    def wait_tile(place, source):
        @pl.when(source == col)
        def _():
            pltpu.make_async_copy(
                front_hbm.at[pl.ds(0, rows), pl.ds(0, rows)], tile.at[place],
                tile_recv.at[place],
            ).wait()

        @pl.when(source != col)
        def _():
            remote(
                front_hbm.at[pl.ds(0, rows), pl.ds(0, rows)], tile.at[place], tile_send.at[0],
                tile_recv.at[place], {"col": source},
            ).wait_recv()

    @pl.when(jnp.logical_not(far_of(chip)))
    def _():
        wait_tile(0, 2 * row + col // tile_leaves)
        for index in range(steps):
            near_copy(index, 0).wait_recv()
            near_copy(index, 1).wait_recv()
        product = (times(near_high[...], tile[0]) + times(near_low[...], tile[0])) * shrink
        rounded = product.astype(jnp.bfloat16)
        rest = (product - rounded.astype(jnp.float32)).astype(jnp.bfloat16)
        send_core(
            0, col,
            times(high[...], rounded) + (times(low[...], rounded) + times(high[...], rest)),
        )

    for pair in range(chips):

        @pl.when(at_home & far_of(pair) & (core == pair % 2))
        def _(pair=pair):
            for parity in range(2):
                for index in range(steps):
                    span = pl.ds(index * nb, nb)
                    remote(
                        high.at[span], far.at[parity, span], far_send.at[index],
                        far_recv.at[parity, index], {"col": 2 * pair + parity},
                    ).wait_recv()
            for parity in range(2):
                slot = 2 * pair + parity
                wait_tile(1 + parity, 2 * row + slot // tile_leaves)
                product = times(far[1 - parity], tile[1 + parity]) * shrink
                send_core(1 + parity, slot, times(far[parity], product.astype(jnp.bfloat16)))

    for group in range(groups):
        for shift in range(1, col_count):
            slab_copy(group, shift, -1).wait_recv()
    for slot in range(col_count):
        for group in range(groups):
            count = min(BLOCK, probes - group * BLOCK)
            basis_ref[
                slot * per_leaf : (slot + 1) * per_leaf, :, group * BLOCK : group * BLOCK + count
            ] = slab_in[group, slot, :, :, :count]
    for slot in range(col_count):
        pair = slot // 2
        source = jnp.where(far_of(pair), 2 * row + pair % 2, slot)

        @pl.when(source != col)
        def _(slot=slot, source=source):
            remote(
                stage.at[0, 0], stage_in.at[slot], core_send.at[0, 0], core_recv.at[slot],
                {"col": source},
            ).wait_recv()

        core_ref[slot] = stage_in[slot, :rank_rows].astype(jnp.float32)

    def settle(copy, away):
        if away:
            copy.wait_send()

    each_tile(settle)

    @pl.when(far_of(chip))
    def _():
        for index in range(steps):
            far_copy(index, 0).wait_send()

    @pl.when(jnp.logical_not(far_of(chip)))
    def _():
        for index in range(steps):
            near_copy(index, 0).wait_send()
            near_copy(index, 1).wait_send()
        for goal in range(col_count):
            pl.when(goal != col)(lambda goal=goal: core_copy(0, goal, col).wait_send())

    for group in range(groups):
        for shift in range(1, col_count):
            slab_copy(group, shift).wait_send()
    for pair in range(chips):

        @pl.when(at_home & far_of(pair) & (core == pair % 2))
        def _(pair=pair):
            for parity in range(2):
                for goal in range(col_count):
                    pl.when(goal != col)(
                        lambda goal=goal, parity=parity: core_copy(
                            1 + parity, goal, 2 * pair + parity
                        ).wait_send()
                    )


def finish(yt, front, row_count, col_count):
    probes, rows = yt.shape
    steps = probes // PIVOTS
    per_leaf = rows // BLOCK
    blocks = front.shape[0] // BLOCK
    groups = -(-probes // BLOCK)
    rank_rows = probes // col_count
    padded = -(-rank_rows // 16) * 16
    f32, bf16 = jnp.float32, jnp.bfloat16
    dma = pltpu.SemaphoreType.DMA
    slab = pltpu.VMEM((groups, col_count, per_leaf, BLOCK // col_count, BLOCK), bf16)
    dims = (row_count, col_count, front.shape[1] // LEAF)
    return pl.pallas_call(
        functools.partial(finish_kernel, dims),
        out_shape=(
            jax.ShapeDtypeStruct((blocks, BLOCK // col_count, probes), bf16),
            jax.ShapeDtypeStruct((col_count, rank_rows, probes), f32),
        ),
        in_specs=[
            pl.BlockSpec(memory_space=pltpu.VMEM),
            pl.BlockSpec(memory_space=pl.ANY),
        ],
        out_specs=(
            pl.BlockSpec(memory_space=pltpu.VMEM),
            pl.BlockSpec(memory_space=pltpu.VMEM),
        ),
        scratch_shapes=[
            pltpu.VMEM((probes, probes), f32),
            pltpu.VMEM((probes, rows), f32),
            pltpu.VMEM((probes, rows), f32),
            pltpu.VMEM((probes, rows), bf16),
            pltpu.VMEM((probes, rows), bf16),
            pltpu.VMEM((probes, rows), bf16),
            pltpu.VMEM((probes, rows), bf16),
            pltpu.VMEM((2, probes, rows), bf16),
            pltpu.VMEM((3, rows, rows), bf16),
            slab,
            slab,
            pltpu.VMEM((3, col_count, padded, probes), bf16),
            pltpu.VMEM((col_count, padded, probes), bf16),
            dma((dims[2],)),
            dma((3,)),
            dma((2, steps)),
            dma((2, steps)),
            dma((steps,)),
            dma((2, steps)),
            dma((groups, col_count)),
            dma((groups, col_count)),
            dma((3, col_count)),
            dma((col_count,)),
        ],
        compiler_params=pltpu.CompilerParams(
            collective_id=1, has_side_effects=True, vmem_limit_bytes=56 << 20
        ),
        cost_estimate=pl.CostEstimate(
            flops=40 * probes * probes * rows,
            bytes_accessed=6 * probes * rows,
            transcendentals=0,
        ),
        name="finish",
    )(yt, front)


def general(parent_front, child_update, parent_test, child_test, child_map):
    row_count = lax.axis_size("row")
    col_count = lax.axis_size("col")
    row_index = lax.axis_index("row")
    col_index = lax.axis_index("col")
    slab = BLOCK // col_count
    own_blocks = parent_front.shape[0] // BLOCK
    probes = parent_test.shape[1]
    per_leaf = LEAF // BLOCK
    leaf_count = own_blocks // per_leaf
    col_leaves = parent_front.shape[1] // LEAF
    shrink = 1.0 / math.sqrt(LEAF)

    tie = lax.optimization_barrier
    pair_index = col_index // 2
    parity = col_index % 2
    half = own_blocks // 2 * BLOCK
    sign = jnp.reshape(parity, (1,)).astype(jnp.int32)
    fronts, tests = parent_front[None], parent_test[None]
    kid_rows = child_update.shape[1]

    def send_tile(position, front):
        sibling = col_index * col_leaves + position
        row_start = jnp.bitwise_xor(sibling, 1) % leaf_count * LEAF
        tile = lax.dynamic_slice(front, (row_start, position * LEAF), (LEAF, LEAF))
        routes = []
        for row in range(row_count):
            for slot in range(leaf_count):
                other = (row * leaf_count + slot) ^ 1
                if other % col_leaves == position:
                    routes.append(
                        (row * col_count + other // col_leaves, row * col_count + slot)
                    )
        return lax.ppermute(tile, ("row", "col"), routes)

    pieces = {position: send_tile(position, parent_front) for position in range(0, col_leaves, 2)}

    jobs = (
        (child_update, child_test, 0, 0, kid_rows),
        (child_update, child_test, 1, 0, kid_rows),
        (fronts, tests, 0, 0, half),
        (fronts, tests, 0, half, half),
    )
    sums = []
    for front, test, which, first_row, rows in jobs:
        halves = probe(front, test, which, first_row, rows, col_count, sign)
        kept, swapped = swap_pair(halves, col_count)
        sums.append(send_pairs(kept, swapped, col_count, pair_index))
    (first_own, first_came), (second_own, second_came) = sums[:2]
    (upper_own, upper_came), (lower_own, lower_came) = sums[2:]

    kid_share = jnp.stack([add_up(first_own, first_came), add_up(second_own, second_came)])
    all_kids = lax.all_gather(kid_share, "row", axis=1, tiled=True)
    own_share = jnp.concatenate([add_up(upper_own, upper_came), add_up(lower_own, lower_came)])

    targets = jnp.arange(own_blocks, dtype=jnp.int32)
    mapped = child_map - row_index * own_blocks
    onehot = (mapped[:, None, :] == targets[None, :, None]).astype(jnp.float32)
    sample = own_share + jnp.einsum("cpn,cnsr->psr", onehot, all_kids, precision=HIGH)

    by_leaf = sample.reshape(leaf_count, per_leaf * slab, probes)
    by_leaf = jnp.pad(by_leaf, ((0, col_count - leaf_count), (0, 0), (0, 0)))
    leaf_rows = lax.all_to_all(by_leaf, "col", 0, 0, tiled=True).reshape(LEAF, probes)

    leaf_rows, front = tie((leaf_rows, parent_front))
    for position in range(1, col_leaves, 2):
        pieces[position] = send_tile(position, front)
    wanted = jnp.bitwise_xor(col_index, 1) % col_leaves
    front_tile = pieces[0]
    for position in range(1, col_leaves):
        front_tile = jnp.where(wanted == position, pieces[position], front_tile)

    basis_t = leaf_basis_of(leaf_rows.T)
    basis = basis_t.T
    slabs = lax.all_to_all(
        basis.reshape(col_count, per_leaf * slab, probes), "col", 0, 0, tiled=True
    )
    leaf_basis = slabs[:leaf_count].reshape(own_blocks, slab, probes)

    natural = (
        basis.reshape(col_count, per_leaf, slab, probes)
        .transpose(1, 0, 2, 3)
        .reshape(LEAF, probes)
    )
    sibling_basis = lax.ppermute(natural, "col", [(c, c ^ 1) for c in range(col_count)])
    product = jnp.dot(front_tile, sibling_basis, preferred_element_type=jnp.float32) * shrink
    core = (
        lax.dot_general(
            natural,
            product.astype(jnp.bfloat16),
            (((0,), (0,)), ((), ())),
            preferred_element_type=jnp.float32,
        )
        * shrink
    )
    cores = lax.all_to_all(
        core.reshape(col_count, probes // col_count, probes), "col", 0, 0, tiled=True
    )
    return (leaf_basis, cores[:leaf_count])


def fits(parent_front, child_update, row_count, col_count):
    leaf_count = parent_front.shape[0] // LEAF
    return (
        leaf_count == col_count
        and row_count * 2 == col_count
        and child_update.shape[0] * child_update.shape[1] // LEAF % 4 == 0
        and all(
            sum(abs(pair - row) > 1 and pair % 2 == core for pair in range(row_count)) < 2
            for row in range(row_count)
            for core in range(2)
        )
        and parent_front.shape[1] // LEAF * 2 == leaf_count
        and col_count % 2 == 0
        and parent_front.shape[1] % LEAF == 0
        and child_update.shape[1] % LEAF == 0
        and 2 * parent_front.shape[1] * LEAF * 2 < 16 << 20
    )


def picks_of(child_map, row_index, row_count, own_blocks):
    kid_count, kid_blocks = child_map.shape
    each = kid_blocks // row_count
    at = jnp.arange(kid_blocks, dtype=jnp.int32)
    which = jnp.arange(kid_count, dtype=jnp.int32)
    value = (at // each * own_blocks + at % each)[None, :] + which[:, None] * each
    targets = jnp.arange(own_blocks, dtype=jnp.int32)
    match = (child_map - row_index * own_blocks)[:, None, :] == targets[None, :, None]
    found = jnp.max(jnp.where(match, value[:, None, :], -1), axis=2)
    return jnp.where(found < 0, row_count * own_blocks, found)


def local(parent_front, child_update, parent_test, child_test, child_map):
    row_count = lax.axis_size("row")
    col_count = lax.axis_size("col")
    if not fits(parent_front, child_update, row_count, col_count):
        return general(parent_front, child_update, parent_test, child_test, child_map)
    row_index = lax.axis_index("row")
    own_blocks = parent_front.shape[0] // BLOCK
    picks = picks_of(child_map, row_index, row_count, own_blocks)
    yt = sample_of(
        picks, child_test.transpose(0, 2, 1), parent_test.T, child_update, parent_front,
        row_count, col_count,
    )
    return tuple(finish(yt, parent_front, row_count, col_count))


def solution(mesh):
    in_specs = (P("row", "col"), P(None, "row", "col"), P("col", None), P(None, "col", None), P())
    out_specs = (P("row", "col", None), P("row", "col", None))
    return jax.shard_map(local, mesh=mesh, in_specs=in_specs, out_specs=out_specs, check_vma=False)
```

```python
import functools
import math

import jax
import jax.numpy as jnp
from jax import lax
from jax.experimental import pallas as pl
from jax.experimental.pallas import tpu as pltpu
from jax.sharding import PartitionSpec as P


LEAF = 896
BLOCK = 128
PIVOTS = 64
GROUP = 8

HIGH = lax.Precision.HIGHEST
MESH = pl.DeviceIdType.MESH


def dot(a, b, dims):
    return lax.dot_general(
        a, b, (dims, ((), ())), precision=HIGH, preferred_element_type=jnp.float32
    )


def inverse_factor(tile, nb):
    ridx = lax.broadcasted_iota(jnp.int32, tile.shape, 0)
    lane = lax.broadcasted_iota(jnp.int32, tile.shape, 1)
    for j in range(0, nb, GROUP):
        cols = [
            jnp.broadcast_to(tile[:, nb + j + k : nb + j + k + 1], tile.shape)
            for k in range(GROUP)
        ]
        rows = [tile[j + k : j + k + 1, :] for k in range(GROUP)]
        for k in range(GROUP):
            at = j + k
            factor = jnp.where(ridx > at, cols[k] * (1.0 / cols[k][at : at + 1, :]), 0.0)
            for m in range(k + 1, GROUP):
                cols[m] = cols[m] - factor * cols[m][at : at + 1, :]
                rows[m] = rows[m] - factor[j + m : j + m + 1, :] * rows[k]
            cols[k] = factor
        for k in range(GROUP):
            tile = tile - cols[k] * rows[k]
    pivots = jnp.sum(jnp.where(lane == ridx + nb, tile, 0.0), axis=1, keepdims=True)
    return tile[:, :nb] * lax.rsqrt(pivots)


def basis_kernel(scale, yt_ref, qt_ref, gram_ref, work_ref):
    nb = PIVOTS
    probes = yt_ref.shape[0]
    work_ref[...] = yt_ref[...]
    gram_ref[...] = dot(yt_ref[...], yt_ref[...], ((1,), (1,)))

    def step(index, carry):
        start = pl.multiple_of(index * nb, nb)
        panel = gram_ref[pl.ds(start, nb), :]
        source = lax.broadcasted_iota(jnp.int32, (probes, 2 * nb), 0)
        lane = lax.broadcasted_iota(jnp.int32, (probes, 2 * nb), 1)
        pick = jnp.where((lane >= nb) & (source == lane - nb + start), 1.0, 0.0)
        eye = jnp.where(
            lax.broadcasted_iota(jnp.int32, (nb, 2 * nb), 0)
            == lax.broadcasted_iota(jnp.int32, (nb, 2 * nb), 1),
            1.0,
            0.0,
        )
        inverse = inverse_factor(dot(panel, pick, ((1,), (0,))) + eye, nb)
        top = dot(inverse, panel, ((1,), (0,)))
        solved = dot(inverse, work_ref[pl.ds(start, nb), :], ((1,), (0,)))
        qt_ref[pl.ds(start, nb), :] = (solved * scale).astype(qt_ref.dtype)
        gram_ref[...] -= dot(top, top, ((0,), (0,)))
        work_ref[...] -= dot(top, solved, ((0,), (0,)))
        return carry

    lax.fori_loop(0, probes // nb, step, 0)


def leaf_basis_of(yt):
    probes, rows = yt.shape
    return pl.pallas_call(
        functools.partial(basis_kernel, math.sqrt(LEAF)),
        out_shape=jax.ShapeDtypeStruct((probes, rows), jnp.bfloat16),
        in_specs=[pl.BlockSpec(memory_space=pltpu.VMEM)],
        out_specs=pl.BlockSpec(memory_space=pltpu.VMEM),
        scratch_shapes=[
            pltpu.VMEM((probes, probes), jnp.float32),
            pltpu.VMEM((probes, rows), jnp.float32),
        ],
        compiler_params=pltpu.CompilerParams(vmem_limit_bytes=40 << 20),
        cost_estimate=pl.CostEstimate(
            flops=40 * probes * probes * rows,
            bytes_accessed=6 * probes * rows,
            transcendentals=0,
        ),
        name="leaf_basis",
    )(yt)


def probe_kernel(parity_ref, front_ref, test_ref, kept_ref, sent_ref):
    total = jnp.dot(front_ref[...], test_ref[...], preferred_element_type=jnp.float32)
    blocks, pairs, slab, probes = kept_ref.shape
    view = total.reshape(blocks * pairs, 2, slab, probes)
    even = parity_ref[0] == 0
    kept_ref[...] = jnp.where(even, view[:, 0], view[:, 1]).reshape(kept_ref.shape)
    sent_ref[...] = jnp.where(even, view[:, 1], view[:, 0]).reshape(sent_ref.shape)


def probe(front, test, which, first_row, rows, col_count, parity):
    depth, probes = test.shape[1:]
    tile = max(t for t in range(BLOCK, 4 * BLOCK + 1, BLOCK) if rows % t == 0)
    pairs, slab = col_count // 2, BLOCK // col_count
    half = jax.ShapeDtypeStruct((rows // BLOCK, pairs, slab, probes), jnp.float32)
    out_spec = pl.BlockSpec((tile // BLOCK, pairs, slab, probes), lambda i, p: (i, 0, 0, 0))
    skip = first_row // tile
    return pl.pallas_call(
        probe_kernel,
        out_shape=(half, half),
        grid_spec=pltpu.PrefetchScalarGridSpec(
            num_scalar_prefetch=1,
            grid=(rows // tile,),
            in_specs=[
                pl.BlockSpec((None, tile, depth), lambda i, p: (which, skip + i, 0)),
                pl.BlockSpec((None, depth, probes), lambda i, p: (which, 0, 0)),
            ],
            out_specs=(out_spec, out_spec),
        ),
        compiler_params=pltpu.CompilerParams(vmem_limit_bytes=40 << 20),
        cost_estimate=pl.CostEstimate(
            flops=2 * rows * depth * probes,
            bytes_accessed=2 * rows * depth + 2 * depth * probes + 4 * rows * probes,
            transcendentals=0,
        ),
        name="probe",
    )(parity, front, test)


def swap_pair(halves, col_count):
    kept, sent = halves
    return kept, lax.ppermute(sent, "col", [(c, c ^ 1) for c in range(col_count)])


def send_pairs(kept, swapped, col_count, pair_index):
    pairs = col_count // 2

    def piece(pair):
        return lax.dynamic_index_in_dim(kept, pair, 1, False) + lax.dynamic_index_in_dim(
            swapped, pair, 1, False
        )

    came = [
        lax.ppermute(
            piece((pair_index + shift) % pairs).astype(jnp.bfloat16),
            "col",
            [(c, (c + 2 * shift) % col_count) for c in range(col_count)],
        )
        for shift in range(1, pairs)
    ]
    return piece(pair_index), came


def add_up(own, came):
    for term in came:
        own = own + term.astype(jnp.float32)
    return own


def spread(total, parts, grain):
    base = total // grain
    cuts = [base * (i + 1) // parts * grain for i in range(parts)]
    starts = [0] + cuts[:-1]
    return [(s, e - s) for s, e in zip(starts, cuts)]


def sample_kernel(
    dims,
    picks_ref,
    kid_test_hbm,
    test_hbm,
    kids_hbm,
    front_hbm,
    yt_ref,
    kid_test,
    test,
    ring,
    parts,
    kid_sum,
    sums,
    kid_in,
    kid_in_two,
    came,
    came_two,
    kids,
    merged,
    landed,
    load_sem,
    test_sem,
    swap_send,
    swap_recv,
    kid_send,
    kid_recv,
    kid_recv_two,
    line_send,
    line_recv,
    line_recv_two,
    row_send,
    row_recv,
    leaf_send,
    leaf_recv,
):
    row_count, col_count, kid_tiles, kid_each, order, slots, subs = dims
    chips = col_count // 2
    probes, rows = yt_ref.shape
    half = probes // 2
    per_leaf = rows // BLOCK
    blocks = merged.shape[0]
    pieces = slots
    row, col = lax.axis_index("row"), lax.axis_index("col")
    chip, core = col // 2, col % 2
    sibling = {"col": chip * 2 + 1 - core}

    def remote(src, dst, send, recv, target):
        return pltpu.make_async_remote_copy(
            src_ref=src, dst_ref=dst, send_sem=send, recv_sem=recv,
            device_id=target, device_id_type=MESH,
        )

    barrier = pltpu.get_barrier_semaphore()
    for shift in range(1, col_count):
        pl.semaphore_signal(
            barrier, inc=1, device_id={"col": (col + shift) % col_count}, device_id_type=MESH
        )
    for shift in range(1, row_count):
        pl.semaphore_signal(
            barrier, inc=1, device_id={"row": (row + shift) % row_count}, device_id_type=MESH
        )

    kid_depth = kid_test.shape[2]

    def pair_at(at):
        return jnp.where(at % 2 == 0, chips - 1 - at // 2, at // 2)

    def load_kid(index):
        index = jnp.asarray(index, jnp.int32)
        start = pl.multiple_of(index % kid_each * rows, rows)
        return pltpu.make_async_copy(
            kids_hbm.at[index // kid_each, pl.ds(start, rows)],
            ring.at[index % 2, :, pl.ds(0, kid_depth)],
            load_sem.at[index % 2],
        )

    def load_front(index):
        index = jnp.asarray(index, jnp.int32)
        leaf = 2 * pair_at(index // 2) + jnp.where(index % 2 == 0, 1 - core, core)
        return pltpu.make_async_copy(
            front_hbm.at[pl.ds(pl.multiple_of(leaf * rows, rows), rows)],
            ring.at[index % 2],
            load_sem.at[index % 2],
        )

    kid_test_load = pltpu.make_async_copy(kid_test_hbm, kid_test, test_sem.at[0])
    test_load = pltpu.make_async_copy(test_hbm, test, test_sem.at[1])
    load_kid(0).start()
    kid_test_load.start()
    load_kid(1).start()
    test_load.start()
    kid_test_load.wait()

    def product(left, right):
        return lax.dot_general(
            left, right, (((1,), (1,)), ((), ())), preferred_element_type=jnp.float32
        )

    def kid_swap(tile):
        away = pl.ds(pl.multiple_of((1 - core) * half, half), half)
        return remote(
            parts.at[tile % 4, away], kid_sum.at[tile],
            swap_send.at[tile], swap_recv.at[tile], sibling,
        )

    def swap(at):
        return remote(
            parts.at[2 * at % 4], sums.at[pair_at(at)],
            swap_send.at[kid_tiles + at], swap_recv.at[kid_tiles + at], sibling,
        )

    def kid_combine(tile):
        kid_swap(tile).wait_recv()
        own = pl.ds(pl.multiple_of(core * half, half), half)
        kid_sum[tile] += parts[tile % 4, own]

    def combine(at):
        swap(at).wait_recv()
        sums[pair_at(at)] += parts[(2 * at + 1) % 4]

    def kid_hop(tile, goal, right, last, target):
        start, size = pieces[goal]
        span = pl.ds(start, size)
        two = last and not right
        dst = kid_in_two.at[tile, pl.ds(0, size)] if two else kid_in.at[tile, span]
        sem = kid_recv_two.at[tile] if two else kid_recv.at[tile, goal]
        return remote(
            kid_in.at[tile, span], dst, kid_send.at[tile, goal], sem, {"col": target}
        )

    def kid_push(tile, goal, here):
        start, size = pieces[goal]
        span = pl.ds(start, size)
        right = goal > here
        last = goal == here + 1 if right else goal == here - 1
        kid_in[tile, span] = kid_sum[tile, span].astype(jnp.bfloat16)
        kid_hop(tile, goal, right, last, col + 2 if right else col - 2).start()

    def kid_take(tile, goal, here, right):
        start, size = pieces[goal]
        span = pl.ds(start, size)
        last = goal == here
        kid_hop(tile, goal, right, last, col - 2 if right else col + 2).wait_recv()
        if last and not right:
            kid_sum[tile, span] += kid_in_two[tile, :size].astype(jnp.float32)
        else:
            kid_sum[tile, span] += kid_in[tile, span].astype(jnp.float32)

    def kid_share(tile, shift, here, toward=1):
        size = pieces[here][1]
        other = (row + toward * shift + row_count) % row_count
        owner = row if toward == 1 else other
        span = kids.at[pl.ds(owner * blocks + tile * per_leaf, per_leaf), pl.ds(0, size)]
        return remote(
            span, span, row_send.at[tile, shift - 1], row_recv.at[tile, shift - 1],
            {"row": other},
        )

    def on_chip(here, body):
        pl.when(chip == here)(body)

    def each_chip(body):
        for here in range(chips):
            on_chip(here, functools.partial(body, here))

    end = chips - 1

    def kid_head(tile):
        def right():
            for goal in reversed(range(1, chips)):
                kid_push(tile, goal, 0)

        def left():
            for goal in range(end):
                kid_push(tile, goal, end)

        on_chip(0, right)
        on_chip(end, left)

    def kid_stage(stage, tile):
        def right():
            for goal in reversed(range(stage + 1, chips)):
                kid_take(tile, goal, stage, True)
                kid_push(tile, goal, stage)

        def left():
            for goal in range(end - stage):
                kid_take(tile, goal, end - stage, False)
                kid_push(tile, goal, end - stage)

        def final(here):
            if here > 0:
                kid_take(tile, here, here, True)
            if here < end:
                kid_take(tile, here, here, False)
            start, size = pieces[here]
            for block in range(per_leaf):
                kids[row * blocks + tile * per_leaf + block, :size] = kid_sum[
                    tile, start : start + size, block * BLOCK : (block + 1) * BLOCK
                ]
            for shift in range(1, row_count):
                kid_share(tile, shift, here).start()

        if stage < end:
            on_chip(stage, right)
            on_chip(end - stage, left)
        for here in range(chips):
            if max(here, end - here) == stage:
                on_chip(here, functools.partial(final, here))

    sub = probes // subs

    def hop(pair, piece, right, last, target):
        span = pl.ds(pl.multiple_of(piece * sub, sub), sub)
        two = last and not right
        dst = came_two.at[span] if two else came.at[pair, span]
        sem = line_recv_two.at[piece] if two else line_recv.at[pair, piece]
        return remote(
            came.at[pair, span], dst, line_send.at[pair, piece], sem, {"col": target}
        )

    def push(pair, piece, here):
        span = pl.ds(pl.multiple_of(piece * sub, sub), sub)
        right = pair > here
        last = pair == here + 1 if right else pair == here - 1
        came[pair, span] = sums[pair, span].astype(jnp.bfloat16)
        hop(pair, piece, right, last, col + 2 if right else col - 2).start()

    def take(pair, piece, here, right):
        span = pl.ds(pl.multiple_of(piece * sub, sub), sub)
        last = pair == here
        hop(pair, piece, right, last, col - 2 if right else col + 2).wait_recv()
        if last and not right:
            sums[pair, span] += came_two[span].astype(jnp.float32)
        else:
            sums[pair, span] += came[pair, span].astype(jnp.float32)

    def head(pair, here):
        def body():
            def one(piece, carry):
                push(pair, piece, here)
                return carry

            lax.fori_loop(0, subs, one, 0)

        on_chip(here, body)

    def stage_of(stage, pair, piece):
        def right():
            take(pair, piece, stage, True)
            push(pair, piece, stage)

        def left():
            take(pair, piece, end - stage, False)
            push(pair, piece, end - stage)

        def final():
            if pair > 0:
                take(pair, piece, pair, True)
            if pair < end:
                take(pair, piece, pair, False)

        if pair > stage and stage < end:
            on_chip(stage, right)
        if pair < end - stage and stage < end:
            on_chip(end - stage, left)
        if max(pair, end - pair) == stage:
            on_chip(pair, final)

    def chain(pairs):
        deepest = max(max(pair, end - pair) for pair in pairs)

        def one(turn, carry):
            for stage in range(1, deepest + 1):
                at = turn - (stage - 1)

                @pl.when((at >= 0) & (at < subs))
                def _(stage=stage, at=at):
                    for pair in pairs:
                        stage_of(stage, pair, at)

            return carry

        lax.fori_loop(0, subs + deepest - 1, one, 0)

    kids[row_count * blocks] = jnp.zeros(kids.shape[1:], kids.dtype)

    def kid_turn(tile, carry):
        pl.when(tile >= 4)(lambda: kid_swap(tile - 4).wait_send())
        load_kid(tile).wait()
        parts[tile % 4] = product(kid_test[tile // kid_each], ring[tile % 2, :, :kid_depth])
        pl.when(tile + 2 < kid_tiles)(lambda: load_kid(tile + 2).start())
        pl.when(tile + 2 >= kid_tiles)(lambda: load_front(tile + 2 - kid_tiles).start())

        @pl.when(tile == 0)
        def _():
            pl.semaphore_wait(barrier, col_count - 1 + row_count - 1)

        kid_swap(tile).start()

        @pl.when(tile > 0)
        def _():
            kid_combine(tile - 1)
            kid_head(tile - 1)

        return carry

    lax.fori_loop(0, kid_tiles, kid_turn, 0)
    test_load.wait()
    turns = 2 * chips

    def turn_of(index, carry):
        at = index // 2

        @pl.when(index < 4)
        def _():
            kid_swap(kid_tiles + index - 4).wait_send()

        @pl.when((index >= 4) & (index % 2 == 0))
        def _():
            swap(at - 2).wait_send()

        load_front(index).wait()
        parts[index % 4] = product(test[...], ring[index % 2])
        pl.when(index + 2 < turns)(lambda: load_front(index + 2).start())

        @pl.when(index % 2 == 0)
        def _():
            swap(at).start()

        @pl.when(index == 0)
        def _():
            kid_combine(kid_tiles - 1)
            kid_head(kid_tiles - 1)

        @pl.when((index % 2 == 0) & (index > 0))
        def _():
            combine(at - 1)

        for spot in range(chips - 1):

            @pl.when(index == 2 * spot + 2)
            def _(spot=spot):
                if order[spot] > 0:
                    head(order[spot], 0)
                if order[spot] < end and spot < chips - 2:
                    head(order[spot], end)

        for stage in range(1, chips):
            tile = index - (stage - 1)
            pl.when((tile >= 0) & (tile < kid_tiles))(
                functools.partial(kid_stage, stage, tile)
            )
        return carry

    lax.fori_loop(0, turns, turn_of, 0)
    combine(chips - 1)
    if order[-1] > 0:
        head(order[-1], 0)
    for pair in (order[-1], order[-2]):
        if pair < end:
            head(pair, end)

    def tail_turn(index, carry):
        for stage in range(1, chips):
            tile = index - (stage - 1)
            pl.when((tile >= 0) & (tile < kid_tiles))(
                functools.partial(kid_stage, stage, tile)
            )
        return carry

    lax.fori_loop(turns, kid_tiles + chips - 2, tail_turn, 0)
    chain(order[:2])
    chain(order[2:])

    def leaf_move(shift, here):
        size = pieces[here][1]
        goal = (col + shift) % col_count
        return remote(
            merged.at[pl.ds(goal * per_leaf, per_leaf), pl.ds(0, size)],
            landed.at[col, :, pl.ds(0, size)],
            leaf_send.at[shift - 1], leaf_recv.at[shift - 1], {"col": goal},
        )

    def merge(here):
        size = pieces[here][1]

        def arrive(tile, carry):
            for shift in range(1, row_count):
                kid_share(tile, shift, here, -1).wait_recv()
            return carry

        lax.fori_loop(0, kid_tiles, arrive, 0)

        def one(block, carry):
            first = kids[picks_ref[0, block], :size]
            second = kids[picks_ref[1, block], :size]
            merged[block, :size] = (first + second).astype(jnp.bfloat16)
            return carry

        lax.fori_loop(0, blocks, one, 0)
        for shift in range(1, col_count):
            leaf_move(shift, here).start()
        landed[col, :, :size] = merged[pl.ds(col * per_leaf, per_leaf), :size]

    each_chip(merge)

    def land():
        for shift in range(1, col_count):
            source = (col - shift + col_count) % col_count
            far = source // 2
            for there in range(chips):

                def wait(there=there):
                    size = pieces[there][1]
                    remote(
                        merged.at[pl.ds(0, per_leaf), pl.ds(0, size)],
                        landed.at[source, :, pl.ds(0, size)],
                        leaf_send.at[shift - 1], leaf_recv.at[shift - 1], {"col": source},
                    ).wait_recv()

                pl.when(far == there)(wait)

    land()
    for source in range(col_count):
        start, size = pieces[source // 2]
        start += source % 2 * half
        for block in range(per_leaf):
            lanes = pl.ds(block * BLOCK, BLOCK)
            yt_ref[pl.ds(start, size), lanes] = (
                sums[chip, pl.ds(start, size), lanes]
                + landed[source, block, :size].astype(jnp.float32)
            )

    def drain(here):
        def one(tile, carry):
            for goal in range(chips):
                if goal != here:
                    kid_hop(tile, goal, goal > here, False, col).wait_send()
            for shift in range(1, row_count):
                kid_share(tile, shift, here).wait_send()
            return carry

        lax.fori_loop(0, kid_tiles, one, 0)
        for pair in range(chips):
            if pair != here:
                for piece in range(subs):
                    hop(pair, piece, pair > here, False, col).wait_send()
        for shift in range(1, col_count):
            leaf_move(shift, here).wait_send()

    each_chip(drain)
    for at in range(chips - 2, chips):
        swap(at).wait_send()


def sample_of(picks, kid_test, test, kids, front, row_count, col_count):
    depth = front.shape[1]
    probes = test.shape[0]
    kid_rows, kid_depth = kids.shape[1:]
    chips = col_count // 2
    half = probes // 2
    kid_each = kid_rows // LEAF
    kid_tiles = kids.shape[0] * kid_each
    per_leaf = LEAF // BLOCK
    blocks = front.shape[0] // BLOCK
    subs = 4
    pieces = spread(half, chips, 16)
    most = max(size for _, size in pieces)
    low, high, order = 0, chips - 1, []
    while low <= high:
        order += [high] if low == high else [high, low]
        low, high = low + 1, high - 1
    f32, bf16 = jnp.float32, jnp.bfloat16
    dims = (row_count, col_count, kid_tiles, kid_each, tuple(order), tuple(pieces), subs)
    any_spec = pl.BlockSpec(memory_space=pl.ANY)
    dma = pltpu.SemaphoreType.DMA
    return pl.pallas_call(
        functools.partial(sample_kernel, dims),
        out_shape=jax.ShapeDtypeStruct((probes, LEAF), f32),
        in_specs=[pl.BlockSpec(memory_space=pltpu.SMEM)] + [any_spec] * 4,
        out_specs=pl.BlockSpec(memory_space=pltpu.VMEM),
        scratch_shapes=[
            pltpu.VMEM((kids.shape[0], probes, kid_depth), bf16),
            pltpu.VMEM((probes, depth), bf16),
            pltpu.VMEM((2, LEAF, depth), bf16),
            pltpu.VMEM((4, probes, LEAF), f32),
            pltpu.VMEM((kid_tiles, half, LEAF), f32),
            pltpu.VMEM((chips, probes, LEAF), f32),
            pltpu.VMEM((kid_tiles, half, LEAF), bf16),
            pltpu.VMEM((kid_tiles, most, LEAF), bf16),
            pltpu.VMEM((chips, probes, LEAF), bf16),
            pltpu.VMEM((probes, LEAF), bf16),
            pltpu.VMEM((row_count * blocks + 1, most, BLOCK), f32),
            pltpu.VMEM((blocks, most, BLOCK), bf16),
            pltpu.VMEM((col_count, per_leaf, most, BLOCK), bf16),
            dma((2,)),
            dma((2,)),
            dma((kid_tiles + chips,)),
            dma((kid_tiles + chips,)),
            dma((kid_tiles, chips)),
            dma((kid_tiles, chips)),
            dma((kid_tiles,)),
            dma((chips, subs)),
            dma((chips, subs)),
            dma((subs,)),
            dma((kid_tiles, row_count - 1)),
            dma((kid_tiles, row_count - 1)),
            dma((col_count - 1,)),
            dma((col_count - 1,)),
        ],
        compiler_params=pltpu.CompilerParams(
            collective_id=0, has_side_effects=True, vmem_limit_bytes=67043328
        ),
        cost_estimate=pl.CostEstimate(
            flops=4 * front.shape[0] * depth * probes,
            bytes_accessed=4 * front.shape[0] * depth,
            transcendentals=0,
        ),
        name="sample",
    )(picks, kid_test, test, kids, front)


def parts_of(x):
    high = x.astype(jnp.bfloat16).astype(jnp.float32)
    rest = x - high
    middle = rest.astype(jnp.bfloat16).astype(jnp.float32)
    return high, middle, rest - middle


def left_parts(x, axis):
    high, middle, low = parts_of(x)
    stacked = jnp.concatenate([high, high, middle, middle, high, low], axis=axis)
    return stacked.astype(jnp.bfloat16)


def right_parts(x):
    high, middle, low = parts_of(x)
    stacked = jnp.concatenate([high, middle, high, middle, low, high], axis=0)
    return stacked.astype(jnp.bfloat16)


def fast_dot(a, b, dims):
    return lax.dot_general(a, b, (dims, ((), ())), preferred_element_type=jnp.float32)


def finish_kernel(
    dims,
    yt_ref,
    front_hbm,
    basis_ref,
    core_ref,
    gram,
    work,
    exact,
    high,
    low,
    near_high,
    near_low,
    far,
    tile,
    slab,
    slab_in,
    stage,
    stage_in,
    tile_send,
    tile_recv,
    near_send,
    near_recv,
    far_send,
    far_recv,
    slab_send,
    slab_recv,
    core_send,
    core_recv,
):
    _, col_count, tile_leaves = dims
    nb = PIVOTS
    chips = col_count // 2
    probes, rows = yt_ref.shape
    per_leaf = rows // BLOCK
    rank_rows = probes // col_count
    groups = slab.shape[0]
    steps = probes // nb
    scale = math.sqrt(LEAF)
    shrink = 1.0 / scale
    row, col = lax.axis_index("row"), lax.axis_index("col")
    chip, core = col // 2, col % 2
    sibling = {"col": chip * 2 + 1 - core}
    at_home = chip == row

    def far_of(pair):
        return (pair >= row + 2) | (pair + 2 <= row)

    def remote(src, dst, send, recv, target):
        return pltpu.make_async_remote_copy(
            src_ref=src, dst_ref=dst, send_sem=send, recv_sem=recv,
            device_id=target, device_id_type=MESH,
        )

    barrier = pltpu.get_barrier_semaphore()
    for shift in range(1, col_count):
        pl.semaphore_signal(
            barrier, inc=1, device_id={"col": (col + shift) % col_count}, device_id_type=MESH
        )
    pl.semaphore_wait(barrier, col_count - 1)

    def tile_source(position):
        slot = core * tile_leaves + (position ^ 1)
        return front_hbm.at[
            pl.ds(pl.multiple_of(slot * rows, rows), rows), pl.ds(position * rows, rows)
        ]

    def each_tile(act):
        for position in range(tile_leaves):
            parity = (position ^ 1) % 2
            pair = (core * tile_leaves + (position ^ 1)) // 2
            slot = pair * 2 + parity
            is_far = far_of(pair)
            goal = jnp.where(is_far, 2 * row + pair % 2, slot)
            for place, chosen in ((0, jnp.logical_not(is_far)), (1 + parity, is_far)):
                here = at_home & chosen & (goal == col)
                there = at_home & chosen & (goal != col)

                def stay(place=place, position=position):
                    act(
                        pltpu.make_async_copy(
                            tile_source(position), tile.at[place], tile_recv.at[place]
                        ),
                        False,
                    )

                def go(place=place, position=position, goal=goal):
                    act(
                        remote(
                            tile_source(position), tile.at[place], tile_send.at[position],
                            tile_recv.at[place], {"col": goal},
                        ),
                        True,
                    )

                pl.when(here)(stay)
                pl.when(there)(go)

    each_tile(lambda copy, away: copy.start())

    work[...] = yt_ref[...]
    one, two, three = (part.astype(jnp.bfloat16) for part in parts_of(yt_ref[...]))
    both = ((1,), (1,))
    small = fast_dot(two, two, both) + fast_dot(one, three, both) + fast_dot(three, one, both)
    middle = fast_dot(one, two, both) + fast_dot(two, one, both)
    wide = gram.shape[1]
    gram[:, :probes] = fast_dot(one, one, both) + (middle + small)
    if wide > probes:
        gram[:, probes:] = jnp.zeros((probes, wide - probes), jnp.float32)

    def near_copy(step, which):
        span = pl.ds(pl.multiple_of(step * nb, nb), nb)
        src, dst = ((high, near_high), (low, near_low))[which]
        return remote(
            src.at[span], dst.at[span], near_send.at[which, step], near_recv.at[which, step],
            sibling,
        )

    def far_copy(step, parity):
        span = pl.ds(pl.multiple_of(step * nb, nb), nb)
        return remote(
            high.at[span], far.at[parity, span], far_send.at[step], far_recv.at[parity, step],
            {"col": 2 * row + chip % 2},
        )

    def slab_copy(group, shift, toward=1):
        other = (col + toward * shift + col_count) % col_count
        owner = col if toward == 1 else other
        return remote(
            slab.at[group, other], slab_in.at[group, owner],
            slab_send.at[group, shift], slab_recv.at[group, shift], {"col": other},
        )

    per_slab = BLOCK // col_count

    def send_slabs(group, count):
        start = pl.multiple_of(group * BLOCK, BLOCK)
        for block in range(per_leaf):
            turned = exact[pl.ds(start, count), block * BLOCK : (block + 1) * BLOCK].T
            for goal in range(col_count):
                slab[group, goal, block, :, :count] = turned[
                    goal * per_slab : (goal + 1) * per_slab
                ].astype(slab.dtype)
        for shift in range(1, col_count):
            ready = jnp.logical_not(far_of(chip) & ((col + shift) % col_count // 2 == row))
            pl.when(ready)(lambda shift=shift: slab_copy(group, shift).start())
        slab_in[group, col] = slab[group, col]

    def step(index, carry):
        start = pl.multiple_of(index * nb, nb)
        panel = gram[pl.ds(start, nb), :]
        square = gram[pl.ds(start, nb), pl.ds(pl.multiple_of(index // 2 * 2 * nb, 2 * nb), 2 * nb)]
        square = jnp.where(index % 2 == 0, pltpu.roll(square, nb, 1), square)
        lane = lax.broadcasted_iota(jnp.int32, square.shape, 1)
        eye = jnp.where(lax.broadcasted_iota(jnp.int32, square.shape, 0) == lane, 1.0, 0.0)
        inverse = inverse_factor(jnp.where(lane >= nb, square, eye), nb)
        inverse_parts = left_parts(inverse, 1)
        top = fast_dot(inverse_parts, right_parts(panel), ((1,), (0,)))
        solved = fast_dot(inverse_parts, right_parts(work[pl.ds(start, nb), :]), ((1,), (0,)))
        scaled = solved * scale
        rounded = scaled.astype(high.dtype)
        exact[pl.ds(start, nb), :] = scaled
        high[pl.ds(start, nb), :] = rounded
        low[pl.ds(start, nb), :] = (scaled - rounded.astype(jnp.float32)).astype(low.dtype)
        top_parts = left_parts(top[:, :probes], 0)
        gram[...] -= fast_dot(top_parts, right_parts(top), ((0,), (0,)))
        work[...] -= fast_dot(top_parts, right_parts(solved), ((0,), (0,)))

        @pl.when(far_of(chip))
        def _():
            for parity in range(2):
                pl.when(core == parity)(lambda parity=parity: far_copy(index, parity).start())

        @pl.when(jnp.logical_not(far_of(chip)))
        def _():
            near_copy(index, 0).start()
            near_copy(index, 1).start()

        @pl.when(index % 2 == 1)
        def _():
            send_slabs(index // 2, BLOCK)

        return carry

    lax.fori_loop(0, steps, step, 0)
    if steps % 2 == 1:
        send_slabs(groups - 1, nb)
    for shift in range(1, col_count):

        @pl.when(far_of(chip) & ((col + shift) % col_count // 2 == row))
        def _(shift=shift):
            for group in range(groups):
                slab_copy(group, shift).start()


    def times(a, b):
        return lax.dot_general(
            a, b, (((1,), (1,)), ((), ())), preferred_element_type=jnp.float32
        )

    def core_copy(place, goal, slot):
        return remote(
            stage.at[place, goal], stage_in.at[slot], core_send.at[place, goal],
            core_recv.at[slot], {"col": goal},
        )

    def send_core(place, slot, value):
        value = (value * shrink).astype(stage.dtype)
        for goal in range(col_count):
            stage[place, goal, :rank_rows] = value[goal * rank_rows : (goal + 1) * rank_rows]

            @pl.when(goal != col)
            def _(goal=goal):
                core_copy(place, goal, slot).start()

            @pl.when(goal == col)
            def _(goal=goal):
                stage_in[slot] = stage[place, goal]

    def wait_tile(place, source):
        @pl.when(source == col)
        def _():
            pltpu.make_async_copy(
                front_hbm.at[pl.ds(0, rows), pl.ds(0, rows)], tile.at[place],
                tile_recv.at[place],
            ).wait()

        @pl.when(source != col)
        def _():
            remote(
                front_hbm.at[pl.ds(0, rows), pl.ds(0, rows)], tile.at[place], tile_send.at[0],
                tile_recv.at[place], {"col": source},
            ).wait_recv()

    @pl.when(jnp.logical_not(far_of(chip)))
    def _():
        wait_tile(0, 2 * row + col // tile_leaves)
        for index in range(steps):
            near_copy(index, 0).wait_recv()
            near_copy(index, 1).wait_recv()
        product = (times(near_high[...], tile[0]) + times(near_low[...], tile[0])) * shrink
        rounded = product.astype(jnp.bfloat16)
        rest = (product - rounded.astype(jnp.float32)).astype(jnp.bfloat16)
        send_core(
            0, col,
            times(high[...], rounded) + (times(low[...], rounded) + times(high[...], rest)),
        )

    for pair in range(chips):

        @pl.when(at_home & far_of(pair) & (core == pair % 2))
        def _(pair=pair):
            for parity in range(2):
                for index in range(steps):
                    span = pl.ds(index * nb, nb)
                    remote(
                        high.at[span], far.at[parity, span], far_send.at[index],
                        far_recv.at[parity, index], {"col": 2 * pair + parity},
                    ).wait_recv()
            for parity in range(2):
                slot = 2 * pair + parity
                wait_tile(1 + parity, 2 * row + slot // tile_leaves)
                product = times(far[1 - parity], tile[1 + parity]) * shrink
                send_core(1 + parity, slot, times(far[parity], product.astype(jnp.bfloat16)))

    for group in range(groups):
        for shift in range(1, col_count):
            slab_copy(group, shift, -1).wait_recv()
    for slot in range(col_count):
        for group in range(groups):
            count = min(BLOCK, probes - group * BLOCK)
            basis_ref[
                slot * per_leaf : (slot + 1) * per_leaf, :, group * BLOCK : group * BLOCK + count
            ] = slab_in[group, slot, :, :, :count]
    for slot in range(col_count):
        pair = slot // 2
        source = jnp.where(far_of(pair), 2 * row + pair % 2, slot)

        @pl.when(source != col)
        def _(slot=slot, source=source):
            remote(
                stage.at[0, 0], stage_in.at[slot], core_send.at[0, 0], core_recv.at[slot],
                {"col": source},
            ).wait_recv()

        core_ref[slot] = stage_in[slot, :rank_rows].astype(jnp.float32)

    def settle(copy, away):
        if away:
            copy.wait_send()

    each_tile(settle)

    @pl.when(far_of(chip))
    def _():
        for index in range(steps):
            far_copy(index, 0).wait_send()

    @pl.when(jnp.logical_not(far_of(chip)))
    def _():
        for index in range(steps):
            near_copy(index, 0).wait_send()
            near_copy(index, 1).wait_send()
        for goal in range(col_count):
            pl.when(goal != col)(lambda goal=goal: core_copy(0, goal, col).wait_send())

    for group in range(groups):
        for shift in range(1, col_count):
            slab_copy(group, shift).wait_send()
    for pair in range(chips):

        @pl.when(at_home & far_of(pair) & (core == pair % 2))
        def _(pair=pair):
            for parity in range(2):
                for goal in range(col_count):
                    pl.when(goal != col)(
                        lambda goal=goal, parity=parity: core_copy(
                            1 + parity, goal, 2 * pair + parity
                        ).wait_send()
                    )


def finish(yt, front, row_count, col_count):
    probes, rows = yt.shape
    steps = probes // PIVOTS
    per_leaf = rows // BLOCK
    blocks = front.shape[0] // BLOCK
    groups = -(-probes // BLOCK)
    rank_rows = probes // col_count
    padded = -(-rank_rows // 16) * 16
    f32, bf16 = jnp.float32, jnp.bfloat16
    dma = pltpu.SemaphoreType.DMA
    slab = pltpu.VMEM((groups, col_count, per_leaf, BLOCK // col_count, BLOCK), bf16)
    dims = (row_count, col_count, front.shape[1] // LEAF)
    return pl.pallas_call(
        functools.partial(finish_kernel, dims),
        out_shape=(
            jax.ShapeDtypeStruct((blocks, BLOCK // col_count, probes), bf16),
            jax.ShapeDtypeStruct((col_count, rank_rows, probes), f32),
        ),
        in_specs=[
            pl.BlockSpec(memory_space=pltpu.VMEM),
            pl.BlockSpec(memory_space=pl.ANY),
        ],
        out_specs=(
            pl.BlockSpec(memory_space=pltpu.VMEM),
            pl.BlockSpec(memory_space=pltpu.VMEM),
        ),
        scratch_shapes=[
            pltpu.VMEM((probes, groups * BLOCK), f32),
            pltpu.VMEM((probes, rows), f32),
            pltpu.VMEM((probes, rows), f32),
            pltpu.VMEM((probes, rows), bf16),
            pltpu.VMEM((probes, rows), bf16),
            pltpu.VMEM((probes, rows), bf16),
            pltpu.VMEM((probes, rows), bf16),
            pltpu.VMEM((2, probes, rows), bf16),
            pltpu.VMEM((3, rows, rows), bf16),
            slab,
            slab,
            pltpu.VMEM((3, col_count, padded, probes), bf16),
            pltpu.VMEM((col_count, padded, probes), bf16),
            dma((dims[2],)),
            dma((3,)),
            dma((2, steps)),
            dma((2, steps)),
            dma((steps,)),
            dma((2, steps)),
            dma((groups, col_count)),
            dma((groups, col_count)),
            dma((3, col_count)),
            dma((col_count,)),
        ],
        compiler_params=pltpu.CompilerParams(
            collective_id=1, has_side_effects=True, vmem_limit_bytes=56 << 20
        ),
        cost_estimate=pl.CostEstimate(
            flops=40 * probes * probes * rows,
            bytes_accessed=6 * probes * rows,
            transcendentals=0,
        ),
        name="finish",
    )(yt, front)


def general(parent_front, child_update, parent_test, child_test, child_map):
    row_count = lax.axis_size("row")
    col_count = lax.axis_size("col")
    row_index = lax.axis_index("row")
    col_index = lax.axis_index("col")
    slab = BLOCK // col_count
    own_blocks = parent_front.shape[0] // BLOCK
    probes = parent_test.shape[1]
    per_leaf = LEAF // BLOCK
    leaf_count = own_blocks // per_leaf
    col_leaves = parent_front.shape[1] // LEAF
    shrink = 1.0 / math.sqrt(LEAF)

    tie = lax.optimization_barrier
    pair_index = col_index // 2
    parity = col_index % 2
    half = own_blocks // 2 * BLOCK
    sign = jnp.reshape(parity, (1,)).astype(jnp.int32)
    fronts, tests = parent_front[None], parent_test[None]
    kid_rows = child_update.shape[1]

    def send_tile(position, front):
        sibling = col_index * col_leaves + position
        row_start = jnp.bitwise_xor(sibling, 1) % leaf_count * LEAF
        tile = lax.dynamic_slice(front, (row_start, position * LEAF), (LEAF, LEAF))
        routes = []
        for row in range(row_count):
            for slot in range(leaf_count):
                other = (row * leaf_count + slot) ^ 1
                if other % col_leaves == position:
                    routes.append(
                        (row * col_count + other // col_leaves, row * col_count + slot)
                    )
        return lax.ppermute(tile, ("row", "col"), routes)

    pieces = {position: send_tile(position, parent_front) for position in range(0, col_leaves, 2)}

    jobs = (
        (child_update, child_test, 0, 0, kid_rows),
        (child_update, child_test, 1, 0, kid_rows),
        (fronts, tests, 0, 0, half),
        (fronts, tests, 0, half, half),
    )
    sums = []
    for front, test, which, first_row, rows in jobs:
        halves = probe(front, test, which, first_row, rows, col_count, sign)
        kept, swapped = swap_pair(halves, col_count)
        sums.append(send_pairs(kept, swapped, col_count, pair_index))
    (first_own, first_came), (second_own, second_came) = sums[:2]
    (upper_own, upper_came), (lower_own, lower_came) = sums[2:]

    kid_share = jnp.stack([add_up(first_own, first_came), add_up(second_own, second_came)])
    all_kids = lax.all_gather(kid_share, "row", axis=1, tiled=True)
    own_share = jnp.concatenate([add_up(upper_own, upper_came), add_up(lower_own, lower_came)])

    targets = jnp.arange(own_blocks, dtype=jnp.int32)
    mapped = child_map - row_index * own_blocks
    onehot = (mapped[:, None, :] == targets[None, :, None]).astype(jnp.float32)
    sample = own_share + jnp.einsum("cpn,cnsr->psr", onehot, all_kids, precision=HIGH)

    by_leaf = sample.reshape(leaf_count, per_leaf * slab, probes)
    by_leaf = jnp.pad(by_leaf, ((0, col_count - leaf_count), (0, 0), (0, 0)))
    leaf_rows = lax.all_to_all(by_leaf, "col", 0, 0, tiled=True).reshape(LEAF, probes)

    leaf_rows, front = tie((leaf_rows, parent_front))
    for position in range(1, col_leaves, 2):
        pieces[position] = send_tile(position, front)
    wanted = jnp.bitwise_xor(col_index, 1) % col_leaves
    front_tile = pieces[0]
    for position in range(1, col_leaves):
        front_tile = jnp.where(wanted == position, pieces[position], front_tile)

    basis_t = leaf_basis_of(leaf_rows.T)
    basis = basis_t.T
    slabs = lax.all_to_all(
        basis.reshape(col_count, per_leaf * slab, probes), "col", 0, 0, tiled=True
    )
    leaf_basis = slabs[:leaf_count].reshape(own_blocks, slab, probes)

    natural = (
        basis.reshape(col_count, per_leaf, slab, probes)
        .transpose(1, 0, 2, 3)
        .reshape(LEAF, probes)
    )
    sibling_basis = lax.ppermute(natural, "col", [(c, c ^ 1) for c in range(col_count)])
    product = jnp.dot(front_tile, sibling_basis, preferred_element_type=jnp.float32) * shrink
    core = (
        lax.dot_general(
            natural,
            product.astype(jnp.bfloat16),
            (((0,), (0,)), ((), ())),
            preferred_element_type=jnp.float32,
        )
        * shrink
    )
    cores = lax.all_to_all(
        core.reshape(col_count, probes // col_count, probes), "col", 0, 0, tiled=True
    )
    return (leaf_basis, cores[:leaf_count])


def fits(parent_front, child_update, row_count, col_count):
    leaf_count = parent_front.shape[0] // LEAF
    return (
        leaf_count == col_count
        and row_count * 2 == col_count
        and child_update.shape[0] * child_update.shape[1] // LEAF % 4 == 0
        and all(
            sum(abs(pair - row) > 1 and pair % 2 == core for pair in range(row_count)) < 2
            for row in range(row_count)
            for core in range(2)
        )
        and parent_front.shape[1] // LEAF * 2 == leaf_count
        and col_count % 2 == 0
        and parent_front.shape[1] % LEAF == 0
        and 2 * PIVOTS == BLOCK
        and child_update.shape[1] % LEAF == 0
        and 2 * parent_front.shape[1] * LEAF * 2 < 16 << 20
    )


def picks_of(child_map, row_index, row_count, own_blocks):
    kid_count, kid_blocks = child_map.shape
    each = kid_blocks // row_count
    at = jnp.arange(kid_blocks, dtype=jnp.int32)
    which = jnp.arange(kid_count, dtype=jnp.int32)
    value = (at // each * own_blocks + at % each)[None, :] + which[:, None] * each
    targets = jnp.arange(own_blocks, dtype=jnp.int32)
    match = (child_map - row_index * own_blocks)[:, None, :] == targets[None, :, None]
    found = jnp.max(jnp.where(match, value[:, None, :], -1), axis=2)
    return jnp.where(found < 0, row_count * own_blocks, found)


def local(parent_front, child_update, parent_test, child_test, child_map):
    row_count = lax.axis_size("row")
    col_count = lax.axis_size("col")
    if not fits(parent_front, child_update, row_count, col_count):
        return general(parent_front, child_update, parent_test, child_test, child_map)
    row_index = lax.axis_index("row")
    own_blocks = parent_front.shape[0] // BLOCK
    picks = picks_of(child_map, row_index, row_count, own_blocks)
    yt = sample_of(
        picks, child_test.transpose(0, 2, 1), parent_test.T, child_update, parent_front,
        row_count, col_count,
    )
    return tuple(finish(yt, parent_front, row_count, col_count))


def solution(mesh):
    in_specs = (P("row", "col"), P(None, "row", "col"), P("col", None), P(None, "col", None), P())
    out_specs = (P("row", "col", None), P("row", "col", None))
    return jax.shard_map(local, mesh=mesh, in_specs=in_specs, out_specs=out_specs, check_vma=False)
```

```python
import functools
import math

import jax
import jax.numpy as jnp
from jax import lax
from jax.experimental import pallas as pl
from jax.experimental.pallas import tpu as pltpu
from jax.sharding import PartitionSpec as P


LEAF = 896
BLOCK = 128
PIVOTS = 64
GROUP = 8

HIGH = lax.Precision.HIGHEST
MESH = pl.DeviceIdType.MESH


def dot(a, b, dims):
    return lax.dot_general(
        a, b, (dims, ((), ())), precision=HIGH, preferred_element_type=jnp.float32
    )


def inverse_factor(tile, nb):
    ridx = lax.broadcasted_iota(jnp.int32, tile.shape, 0)
    lane = lax.broadcasted_iota(jnp.int32, tile.shape, 1)
    for j in range(0, nb, GROUP):
        cols = [
            jnp.broadcast_to(tile[:, nb + j + k : nb + j + k + 1], tile.shape)
            for k in range(GROUP)
        ]
        rows = [tile[j + k : j + k + 1, :] for k in range(GROUP)]
        for k in range(GROUP):
            at = j + k
            factor = jnp.where(ridx > at, cols[k] * (1.0 / cols[k][at : at + 1, :]), 0.0)
            for m in range(k + 1, GROUP):
                cols[m] = cols[m] - factor * cols[m][at : at + 1, :]
                rows[m] = rows[m] - factor[j + m : j + m + 1, :] * rows[k]
            cols[k] = factor
        for k in range(GROUP):
            tile = tile - cols[k] * rows[k]
    pivots = jnp.sum(jnp.where(lane == ridx + nb, tile, 0.0), axis=1, keepdims=True)
    return tile[:, :nb] * lax.rsqrt(pivots)


def basis_kernel(scale, yt_ref, qt_ref, gram_ref, work_ref):
    nb = PIVOTS
    probes = yt_ref.shape[0]
    work_ref[...] = yt_ref[...]
    gram_ref[...] = dot(yt_ref[...], yt_ref[...], ((1,), (1,)))

    def step(index, carry):
        start = pl.multiple_of(index * nb, nb)
        panel = gram_ref[pl.ds(start, nb), :]
        source = lax.broadcasted_iota(jnp.int32, (probes, 2 * nb), 0)
        lane = lax.broadcasted_iota(jnp.int32, (probes, 2 * nb), 1)
        pick = jnp.where((lane >= nb) & (source == lane - nb + start), 1.0, 0.0)
        eye = jnp.where(
            lax.broadcasted_iota(jnp.int32, (nb, 2 * nb), 0)
            == lax.broadcasted_iota(jnp.int32, (nb, 2 * nb), 1),
            1.0,
            0.0,
        )
        inverse = inverse_factor(dot(panel, pick, ((1,), (0,))) + eye, nb)
        top = dot(inverse, panel, ((1,), (0,)))
        solved = dot(inverse, work_ref[pl.ds(start, nb), :], ((1,), (0,)))
        qt_ref[pl.ds(start, nb), :] = (solved * scale).astype(qt_ref.dtype)
        gram_ref[...] -= dot(top, top, ((0,), (0,)))
        work_ref[...] -= dot(top, solved, ((0,), (0,)))
        return carry

    lax.fori_loop(0, probes // nb, step, 0)


def leaf_basis_of(yt):
    probes, rows = yt.shape
    return pl.pallas_call(
        functools.partial(basis_kernel, math.sqrt(LEAF)),
        out_shape=jax.ShapeDtypeStruct((probes, rows), jnp.bfloat16),
        in_specs=[pl.BlockSpec(memory_space=pltpu.VMEM)],
        out_specs=pl.BlockSpec(memory_space=pltpu.VMEM),
        scratch_shapes=[
            pltpu.VMEM((probes, probes), jnp.float32),
            pltpu.VMEM((probes, rows), jnp.float32),
        ],
        compiler_params=pltpu.CompilerParams(vmem_limit_bytes=40 << 20),
        cost_estimate=pl.CostEstimate(
            flops=40 * probes * probes * rows,
            bytes_accessed=6 * probes * rows,
            transcendentals=0,
        ),
        name="leaf_basis",
    )(yt)


def probe_kernel(parity_ref, front_ref, test_ref, kept_ref, sent_ref):
    total = jnp.dot(front_ref[...], test_ref[...], preferred_element_type=jnp.float32)
    blocks, pairs, slab, probes = kept_ref.shape
    view = total.reshape(blocks * pairs, 2, slab, probes)
    even = parity_ref[0] == 0
    kept_ref[...] = jnp.where(even, view[:, 0], view[:, 1]).reshape(kept_ref.shape)
    sent_ref[...] = jnp.where(even, view[:, 1], view[:, 0]).reshape(sent_ref.shape)


def probe(front, test, which, first_row, rows, col_count, parity):
    depth, probes = test.shape[1:]
    tile = max(t for t in range(BLOCK, 4 * BLOCK + 1, BLOCK) if rows % t == 0)
    pairs, slab = col_count // 2, BLOCK // col_count
    half = jax.ShapeDtypeStruct((rows // BLOCK, pairs, slab, probes), jnp.float32)
    out_spec = pl.BlockSpec((tile // BLOCK, pairs, slab, probes), lambda i, p: (i, 0, 0, 0))
    skip = first_row // tile
    return pl.pallas_call(
        probe_kernel,
        out_shape=(half, half),
        grid_spec=pltpu.PrefetchScalarGridSpec(
            num_scalar_prefetch=1,
            grid=(rows // tile,),
            in_specs=[
                pl.BlockSpec((None, tile, depth), lambda i, p: (which, skip + i, 0)),
                pl.BlockSpec((None, depth, probes), lambda i, p: (which, 0, 0)),
            ],
            out_specs=(out_spec, out_spec),
        ),
        compiler_params=pltpu.CompilerParams(vmem_limit_bytes=40 << 20),
        cost_estimate=pl.CostEstimate(
            flops=2 * rows * depth * probes,
            bytes_accessed=2 * rows * depth + 2 * depth * probes + 4 * rows * probes,
            transcendentals=0,
        ),
        name="probe",
    )(parity, front, test)


def swap_pair(halves, col_count):
    kept, sent = halves
    return kept, lax.ppermute(sent, "col", [(c, c ^ 1) for c in range(col_count)])


def send_pairs(kept, swapped, col_count, pair_index):
    pairs = col_count // 2

    def piece(pair):
        return lax.dynamic_index_in_dim(kept, pair, 1, False) + lax.dynamic_index_in_dim(
            swapped, pair, 1, False
        )

    came = [
        lax.ppermute(
            piece((pair_index + shift) % pairs).astype(jnp.bfloat16),
            "col",
            [(c, (c + 2 * shift) % col_count) for c in range(col_count)],
        )
        for shift in range(1, pairs)
    ]
    return piece(pair_index), came


def add_up(own, came):
    for term in came:
        own = own + term.astype(jnp.float32)
    return own


def parts_of(x):
    high = x.astype(jnp.bfloat16).astype(jnp.float32)
    rest = x - high
    middle = rest.astype(jnp.bfloat16).astype(jnp.float32)
    return high, middle, rest - middle


def left_parts(x, axis):
    high, middle, low = parts_of(x)
    stacked = jnp.concatenate([high, high, middle, middle, high, low], axis=axis)
    return stacked.astype(jnp.bfloat16)


def right_parts(x):
    high, middle, low = parts_of(x)
    stacked = jnp.concatenate([high, middle, high, middle, low, high], axis=0)
    return stacked.astype(jnp.bfloat16)


def fast_dot(a, b, dims):
    return lax.dot_general(a, b, (dims, ((), ())), preferred_element_type=jnp.float32)


def finishing(
    dims, tile_at, far_at, front_hbm, basis_ref, core_ref, gram, work, exact, high, low,
    near_high, near_low, slab, slab_in, stage, stage_in, sems,
):
    groups, _, slab_rows, _ = slab_in.shape

    (
        tile_send, tile_recv, near_send, near_recv, far_send, far_recv, slab_send, slab_recv,
        core_send, core_recv,
    ) = sems
    _, col_count, tile_leaves = dims
    nb = PIVOTS
    chips = col_count // 2
    probes, rows = work.shape
    per_leaf = rows // BLOCK
    rank_rows = probes // col_count
    steps = probes // nb
    scale = math.sqrt(LEAF)
    shrink = 1.0 / scale
    row, col = lax.axis_index("row"), lax.axis_index("col")
    chip, core = col // 2, col % 2
    sibling = {"col": chip * 2 + 1 - core}
    at_home = chip == row

    def far_of(pair):
        return (pair >= row + 2) | (pair + 2 <= row)

    def remote(src, dst, send, recv, target):
        return pltpu.make_async_remote_copy(
            src_ref=src, dst_ref=dst, send_sem=send, recv_sem=recv,
            device_id=target, device_id_type=MESH,
        )

    def tile_source(position):
        slot = core * tile_leaves + (position ^ 1)
        return front_hbm.at[
            pl.ds(pl.multiple_of(slot * rows, rows), rows), pl.ds(position * rows, rows)
        ]

    def each_tile(act):
        for position in range(tile_leaves):
            parity = (position ^ 1) % 2
            pair = (core * tile_leaves + (position ^ 1)) // 2
            slot = pair * 2 + parity
            is_far = far_of(pair)
            goal = jnp.where(is_far, 2 * row + pair % 2, slot)
            for place, chosen in ((0, jnp.logical_not(is_far)), (1 + parity, is_far)):
                here = at_home & chosen & (goal == col)
                there = at_home & chosen & (goal != col)

                def stay(place=place, position=position):
                    act(
                        pltpu.make_async_copy(
                            tile_source(position), tile_at(place), tile_recv.at[place]
                        ),
                        False,
                    )

                def go(place=place, position=position, goal=goal):
                    act(
                        remote(
                            tile_source(position), tile_at(place), tile_send.at[position],
                            tile_recv.at[place], {"col": goal},
                        ),
                        True,
                    )

                pl.when(here)(stay)
                pl.when(there)(go)

    def start_tiles():
        each_tile(lambda copy, away: copy.start())

    def run():
        one, two, three = (part.astype(jnp.bfloat16) for part in parts_of(work[...]))
        both = ((1,), (1,))
        small = fast_dot(two, two, both) + fast_dot(one, three, both) + fast_dot(three, one, both)
        middle = fast_dot(one, two, both) + fast_dot(two, one, both)
        wide = gram.shape[1]
        gram[:, :probes] = fast_dot(one, one, both) + (middle + small)
        if wide > probes:
            gram[:, probes:] = jnp.zeros((probes, wide - probes), jnp.float32)

        def near_copy(step, which):
            span = pl.ds(pl.multiple_of(step * nb, nb), nb)
            src, dst = ((high, near_high), (low, near_low))[which]
            return remote(
                src.at[span], dst.at[span], near_send.at[which, step], near_recv.at[which, step],
                sibling,
            )

        def far_copy(step, parity):
            span = pl.ds(pl.multiple_of(step * nb, nb), nb)
            return remote(
                high.at[span], far_at(parity).at[span], far_send.at[step], far_recv.at[parity, step],
                {"col": 2 * row + chip % 2},
            )

        def slab_at(group, goal):
            return slab.at[
                pl.ds(pl.multiple_of(jnp.asarray(group * slab_rows, jnp.int32), 16), slab_rows),
                pl.ds(pl.multiple_of(jnp.asarray(goal * BLOCK, jnp.int32), BLOCK), BLOCK),
            ]

        def slab_copy(group, shift, toward=1):
            other = (col + toward * shift + col_count) % col_count
            owner = col if toward == 1 else other
            return remote(
                slab_at(group, other), slab_in.at[group, owner],
                slab_send.at[group, shift], slab_recv.at[group, shift], {"col": other},
            )

        per_slab = BLOCK // col_count

        def send_slabs(group, count):
            start = pl.multiple_of(group * BLOCK, BLOCK)
            for block in range(per_leaf):
                turned = exact[pl.ds(start, count), block * BLOCK : (block + 1) * BLOCK].T
                for goal in range(col_count):
                    place = slab_at(group, goal).at[
                        pl.ds(block * per_slab, per_slab), pl.ds(0, count)
                    ]
                    place[...] = turned[
                        goal * per_slab : (goal + 1) * per_slab
                    ].astype(slab.dtype)
            for shift in range(1, col_count):
                ready = jnp.logical_not(far_of(chip) & ((col + shift) % col_count // 2 == row))
                pl.when(ready)(lambda shift=shift: slab_copy(group, shift).start())
            slab_in[group, col] = slab_at(group, col)[...]

        def step(index, carry):
            start = pl.multiple_of(index * nb, nb)
            panel = gram[pl.ds(start, nb), :]
            square = gram[pl.ds(start, nb), pl.ds(pl.multiple_of(index // 2 * 2 * nb, 2 * nb), 2 * nb)]
            square = jnp.where(index % 2 == 0, pltpu.roll(square, nb, 1), square)
            lane = lax.broadcasted_iota(jnp.int32, square.shape, 1)
            eye = jnp.where(lax.broadcasted_iota(jnp.int32, square.shape, 0) == lane, 1.0, 0.0)
            inverse = inverse_factor(jnp.where(lane >= nb, square, eye), nb)
            inverse_parts = left_parts(inverse, 1)
            top = fast_dot(inverse_parts, right_parts(panel), ((1,), (0,)))
            solved = fast_dot(inverse_parts, right_parts(work[pl.ds(start, nb), :]), ((1,), (0,)))
            scaled = solved * scale
            rounded = scaled.astype(high.dtype)
            exact[pl.ds(start, nb), :] = scaled
            high[pl.ds(start, nb), :] = rounded
            low[pl.ds(start, nb), :] = (scaled - rounded.astype(jnp.float32)).astype(low.dtype)
            top_parts = left_parts(top[:, :probes], 0)
            gram[...] -= fast_dot(top_parts, right_parts(top), ((0,), (0,)))
            work[...] -= fast_dot(top_parts, right_parts(solved), ((0,), (0,)))

            @pl.when(far_of(chip))
            def _():
                for parity in range(2):
                    pl.when(core == parity)(lambda parity=parity: far_copy(index, parity).start())

            @pl.when(jnp.logical_not(far_of(chip)))
            def _():
                near_copy(index, 0).start()
                near_copy(index, 1).start()

            @pl.when(index % 2 == 1)
            def _():
                send_slabs(index // 2, BLOCK)

            return carry

        lax.fori_loop(0, steps, step, 0)
        if steps % 2 == 1:
            send_slabs(groups - 1, nb)
        for shift in range(1, col_count):

            @pl.when(far_of(chip) & ((col + shift) % col_count // 2 == row))
            def _(shift=shift):
                for group in range(groups):
                    slab_copy(group, shift).start()


        def times(a, b):
            return lax.dot_general(
                a, b, (((1,), (1,)), ((), ())), preferred_element_type=jnp.float32
            )

        def core_copy(place, goal, slot):
            return remote(
                stage.at[place, goal], stage_in.at[slot], core_send.at[place, goal],
                core_recv.at[slot], {"col": goal},
            )

        def send_core(place, slot, value):
            value = (value * shrink).astype(stage.dtype)
            for goal in range(col_count):
                stage[place, goal, :rank_rows] = value[goal * rank_rows : (goal + 1) * rank_rows]

                @pl.when(goal != col)
                def _(goal=goal):
                    core_copy(place, goal, slot).start()

                @pl.when(goal == col)
                def _(goal=goal):
                    stage_in[slot] = stage[place, goal]

        def wait_tile(place, source):
            @pl.when(source == col)
            def _():
                pltpu.make_async_copy(
                    front_hbm.at[pl.ds(0, rows), pl.ds(0, rows)], tile_at(place),
                    tile_recv.at[place],
                ).wait()

            @pl.when(source != col)
            def _():
                remote(
                    front_hbm.at[pl.ds(0, rows), pl.ds(0, rows)], tile_at(place), tile_send.at[0],
                    tile_recv.at[place], {"col": source},
                ).wait_recv()

        @pl.when(jnp.logical_not(far_of(chip)))
        def _():
            wait_tile(0, 2 * row + col // tile_leaves)
            for index in range(steps):
                near_copy(index, 0).wait_recv()
                near_copy(index, 1).wait_recv()
            product = (times(near_high[...], tile_at(0)[...]) + times(near_low[...], tile_at(0)[...])) * shrink
            rounded = product.astype(jnp.bfloat16)
            rest = (product - rounded.astype(jnp.float32)).astype(jnp.bfloat16)
            send_core(
                0, col,
                times(high[...], rounded) + (times(low[...], rounded) + times(high[...], rest)),
            )

        for pair in range(chips):

            @pl.when(at_home & far_of(pair) & (core == pair % 2))
            def _(pair=pair):
                for parity in range(2):
                    for index in range(steps):
                        span = pl.ds(index * nb, nb)
                        remote(
                            high.at[span], far_at(parity).at[span], far_send.at[index],
                            far_recv.at[parity, index], {"col": 2 * pair + parity},
                        ).wait_recv()
                for parity in range(2):
                    slot = 2 * pair + parity
                    wait_tile(1 + parity, 2 * row + slot // tile_leaves)
                    product = times(far_at(1 - parity)[...], tile_at(1 + parity)[...]) * shrink
                    send_core(1 + parity, slot, times(far_at(parity)[...], product.astype(jnp.bfloat16)))

        for group in range(groups):
            for shift in range(1, col_count):
                slab_copy(group, shift, -1).wait_recv()
        for slot in range(col_count):
            for group in range(groups):
                count = min(BLOCK, probes - group * BLOCK)
                basis_ref[
                    slot * per_leaf : (slot + 1) * per_leaf, :, group * BLOCK : group * BLOCK + count
                ] = slab_in[group, slot].reshape(per_leaf, per_slab, BLOCK)[:, :, :count]
        for slot in range(col_count):
            pair = slot // 2
            source = jnp.where(far_of(pair), 2 * row + pair % 2, slot)

            @pl.when(source != col)
            def _(slot=slot, source=source):
                remote(
                    stage.at[0, 0], stage_in.at[slot], core_send.at[0, 0], core_recv.at[slot],
                    {"col": source},
                ).wait_recv()

            core_ref[slot] = stage_in[slot, :rank_rows].astype(jnp.float32)

        def settle(copy, away):
            if away:
                copy.wait_send()

        each_tile(settle)

        @pl.when(far_of(chip))
        def _():
            for index in range(steps):
                far_copy(index, 0).wait_send()

        @pl.when(jnp.logical_not(far_of(chip)))
        def _():
            for index in range(steps):
                near_copy(index, 0).wait_send()
                near_copy(index, 1).wait_send()
            for goal in range(col_count):
                pl.when(goal != col)(lambda goal=goal: core_copy(0, goal, col).wait_send())

        for group in range(groups):
            for shift in range(1, col_count):
                slab_copy(group, shift).wait_send()
        for pair in range(chips):

            @pl.when(at_home & far_of(pair) & (core == pair % 2))
            def _(pair=pair):
                for parity in range(2):
                    for goal in range(col_count):
                        pl.when(goal != col)(
                            lambda goal=goal, parity=parity: core_copy(
                                1 + parity, goal, 2 * pair + parity
                            ).wait_send()
                        )

    return start_tiles, run


def spread(total, parts, grain):
    base = total // grain
    cuts = [base * (i + 1) // parts * grain for i in range(parts)]
    starts = [0] + cuts[:-1]
    return [(s, e - s) for s, e in zip(starts, cuts)]


def sample_kernel(
    dims,
    picks_ref,
    kid_test_hbm,
    test_hbm,
    kids_hbm,
    front_hbm,
    basis_ref,
    core_ref,
    kid_test,
    test,
    ring,
    parts,
    kid_sum,
    sums,
    kid_in,
    kid_in_two,
    came,
    came_two,
    kids,
    load_sem,
    test_sem,
    swap_send,
    swap_recv,
    kid_send,
    kid_recv,
    kid_recv_two,
    line_send,
    line_recv,
    line_recv_two,
    row_send,
    row_recv,
    leaf_send,
    leaf_recv,
    slab_in,
    stage_out,
    stage_in,
    ready,
    *sems,
):
    row_count, col_count, kid_tiles, kid_each, order, slots, subs = dims
    chips = col_count // 2
    probes, rows = parts.shape[1:]
    half = probes // 2
    per_leaf = rows // BLOCK
    blocks = front_hbm.shape[0] // BLOCK
    most = kids.shape[1]
    pieces = slots
    row, col = lax.axis_index("row"), lax.axis_index("col")
    chip, core = col // 2, col % 2
    sibling = {"col": chip * 2 + 1 - core}

    def remote(src, dst, send, recv, target):
        return pltpu.make_async_remote_copy(
            src_ref=src, dst_ref=dst, send_sem=send, recv_sem=recv,
            device_id=target, device_id_type=MESH,
        )

    barrier = pltpu.get_barrier_semaphore()
    for shift in range(1, col_count):
        pl.semaphore_signal(
            barrier, inc=1, device_id={"col": (col + shift) % col_count}, device_id_type=MESH
        )
    for shift in range(1, row_count):
        pl.semaphore_signal(
            barrier, inc=1, device_id={"row": (row + shift) % row_count}, device_id_type=MESH
        )

    kid_depth = kid_test.shape[2]

    def pair_at(at):
        return jnp.where(at % 2 == 0, chips - 1 - at // 2, at // 2)

    def load_kid(index):
        index = jnp.asarray(index, jnp.int32)
        start = pl.multiple_of(index % kid_each * rows, rows)
        return pltpu.make_async_copy(
            kids_hbm.at[index // kid_each, pl.ds(start, rows)],
            ring.at[index % 2, :, pl.ds(0, kid_depth)],
            load_sem.at[index % 2],
        )

    def load_front(index):
        index = jnp.asarray(index, jnp.int32)
        leaf = 2 * pair_at(index // 2) + jnp.where(index % 2 == 0, 1 - core, core)
        return pltpu.make_async_copy(
            front_hbm.at[pl.ds(pl.multiple_of(leaf * rows, rows), rows)],
            ring.at[index % 2],
            load_sem.at[index % 2],
        )

    kid_test_load = pltpu.make_async_copy(kid_test_hbm, kid_test, test_sem.at[0])
    test_load = pltpu.make_async_copy(test_hbm, test, test_sem.at[1])
    load_kid(0).start()
    kid_test_load.start()
    load_kid(1).start()
    test_load.start()
    kid_test_load.wait()

    def product(left, right):
        return lax.dot_general(
            left, right, (((1,), (1,)), ((), ())), preferred_element_type=jnp.float32
        )

    def kid_swap(tile):
        away = pl.ds(pl.multiple_of((1 - core) * half, half), half)
        return remote(
            parts.at[tile % 4, away], kid_sum.at[tile],
            swap_send.at[tile], swap_recv.at[tile], sibling,
        )

    def swap(at):
        return remote(
            parts.at[2 * at % 4], sums.at[pair_at(at)],
            swap_send.at[kid_tiles + at], swap_recv.at[kid_tiles + at], sibling,
        )

    def kid_combine(tile):
        kid_swap(tile).wait_recv()
        own = pl.ds(pl.multiple_of(core * half, half), half)
        kid_sum[tile] += parts[tile % 4, own]

    def combine(at):
        swap(at).wait_recv()
        sums[pair_at(at)] += parts[(2 * at + 1) % 4]

    def kid_hop(tile, goal, right, last, target):
        start, size = pieces[goal]
        span = pl.ds(start, size)
        two = last and not right
        dst = kid_in_two.at[tile, pl.ds(0, size)] if two else kid_in.at[tile, span]
        sem = kid_recv_two.at[tile] if two else kid_recv.at[tile, goal]
        return remote(
            kid_in.at[tile, span], dst, kid_send.at[tile, goal], sem, {"col": target}
        )

    def kid_push(tile, goal, here):
        start, size = pieces[goal]
        span = pl.ds(start, size)
        right = goal > here
        last = goal == here + 1 if right else goal == here - 1
        kid_in[tile, span] = kid_sum[tile, span].astype(jnp.bfloat16)
        kid_hop(tile, goal, right, last, col + 2 if right else col - 2).start()

    def kid_take(tile, goal, here, right):
        start, size = pieces[goal]
        span = pl.ds(start, size)
        last = goal == here
        kid_hop(tile, goal, right, last, col - 2 if right else col + 2).wait_recv()
        if last and not right:
            kid_sum[tile, span] += kid_in_two[tile, :size].astype(jnp.float32)
        else:
            kid_sum[tile, span] += kid_in[tile, span].astype(jnp.float32)

    def kid_share(tile, shift, here, toward=1):
        size = pieces[here][1]
        other = (row + toward * shift + row_count) % row_count
        owner = row if toward == 1 else other
        span = kids.at[pl.ds(owner * blocks + tile * per_leaf, per_leaf), pl.ds(0, size)]
        return remote(
            span, span, row_send.at[tile, shift - 1], row_recv.at[tile, shift - 1],
            {"row": other},
        )

    def on_chip(here, body):
        pl.when(chip == here)(body)

    def each_chip(body):
        for here in range(chips):
            on_chip(here, functools.partial(body, here))

    end = chips - 1

    def kid_head(tile):
        def right():
            for goal in reversed(range(1, chips)):
                kid_push(tile, goal, 0)

        def left():
            for goal in range(end):
                kid_push(tile, goal, end)

        on_chip(0, right)
        on_chip(end, left)

    def kid_stage(stage, tile):
        def right():
            for goal in reversed(range(stage + 1, chips)):
                kid_take(tile, goal, stage, True)
                kid_push(tile, goal, stage)

        def left():
            for goal in range(end - stage):
                kid_take(tile, goal, end - stage, False)
                kid_push(tile, goal, end - stage)

        def final(here):
            if here > 0:
                kid_take(tile, here, here, True)
            if here < end:
                kid_take(tile, here, here, False)
            start, size = pieces[here]
            for block in range(per_leaf):
                kids[row * blocks + tile * per_leaf + block, :size] = kid_sum[
                    tile, start : start + size, block * BLOCK : (block + 1) * BLOCK
                ]
            for shift in range(1, row_count):
                kid_share(tile, shift, here).start()

        if stage < end:
            on_chip(stage, right)
            on_chip(end - stage, left)
        for here in range(chips):
            if max(here, end - here) == stage:
                on_chip(here, functools.partial(final, here))

    sub = probes // subs

    def hop(pair, piece, right, last, target):
        span = pl.ds(pl.multiple_of(piece * sub, sub), sub)
        two = last and not right
        dst = came_two.at[span] if two else came.at[pair, span]
        sem = line_recv_two.at[piece] if two else line_recv.at[pair, piece]
        return remote(
            came.at[pair, span], dst, line_send.at[pair, piece], sem, {"col": target}
        )

    def push(pair, piece, here):
        span = pl.ds(pl.multiple_of(piece * sub, sub), sub)
        right = pair > here
        last = pair == here + 1 if right else pair == here - 1
        came[pair, span] = sums[pair, span].astype(jnp.bfloat16)
        hop(pair, piece, right, last, col + 2 if right else col - 2).start()

    def take(pair, piece, here, right):
        span = pl.ds(pl.multiple_of(piece * sub, sub), sub)
        last = pair == here
        hop(pair, piece, right, last, col - 2 if right else col + 2).wait_recv()
        if last and not right:
            sums[pair, span] += came_two[span].astype(jnp.float32)
        else:
            sums[pair, span] += came[pair, span].astype(jnp.float32)

    def head(pair, here):
        def body():
            def one(piece, carry):
                push(pair, piece, here)
                return carry

            lax.fori_loop(0, subs, one, 0)

        on_chip(here, body)

    def stage_of(stage, pair, piece):
        def right():
            take(pair, piece, stage, True)
            push(pair, piece, stage)

        def left():
            take(pair, piece, end - stage, False)
            push(pair, piece, end - stage)

        def final():
            if pair > 0:
                take(pair, piece, pair, True)
            if pair < end:
                take(pair, piece, pair, False)

        if pair > stage and stage < end:
            on_chip(stage, right)
        if pair < end - stage and stage < end:
            on_chip(end - stage, left)
        if max(pair, end - pair) == stage:
            on_chip(pair, final)

    def chain(pairs):
        deepest = max(max(pair, end - pair) for pair in pairs)

        def one(turn, carry):
            for stage in range(1, deepest + 1):
                at = turn - (stage - 1)

                @pl.when((at >= 0) & (at < subs))
                def _(stage=stage, at=at):
                    for pair in pairs:
                        stage_of(stage, pair, at)

            return carry

        lax.fori_loop(0, subs + deepest - 1, one, 0)

    kids[row_count * blocks] = jnp.zeros(kids.shape[1:], kids.dtype)

    def kid_turn(tile, carry):
        pl.when(tile >= 4)(lambda: kid_swap(tile - 4).wait_send())
        load_kid(tile).wait()
        parts[tile % 4] = product(kid_test[tile // kid_each], ring[tile % 2, :, :kid_depth])
        pl.when(tile + 2 < kid_tiles)(lambda: load_kid(tile + 2).start())
        pl.when(tile + 2 >= kid_tiles)(lambda: load_front(tile + 2 - kid_tiles).start())

        @pl.when(tile == 0)
        def _():
            pl.semaphore_wait(barrier, col_count - 1 + row_count - 1)

        kid_swap(tile).start()

        @pl.when(tile > 0)
        def _():
            kid_combine(tile - 1)
            kid_head(tile - 1)

        return carry

    lax.fori_loop(0, kid_tiles, kid_turn, 0)
    test_load.wait()
    turns = 2 * chips

    def turn_of(index, carry):
        at = index // 2

        @pl.when(index < 4)
        def _():
            kid_swap(kid_tiles + index - 4).wait_send()

        @pl.when((index >= 4) & (index % 2 == 0))
        def _():
            swap(at - 2).wait_send()

        load_front(index).wait()
        parts[index % 4] = product(test[...], ring[index % 2])
        pl.when(index + 2 < turns)(lambda: load_front(index + 2).start())

        @pl.when(index % 2 == 0)
        def _():
            swap(at).start()

        @pl.when(index == 0)
        def _():
            kid_combine(kid_tiles - 1)
            kid_head(kid_tiles - 1)

        @pl.when((index % 2 == 0) & (index > 0))
        def _():
            combine(at - 1)

        for spot in range(chips - 1):

            @pl.when(index == 2 * spot + 2)
            def _(spot=spot):
                if order[spot] > 0:
                    head(order[spot], 0)
                if order[spot] < end and spot < chips - 2:
                    head(order[spot], end)

        for stage in range(1, chips):
            tile = index - (stage - 1)
            pl.when((tile >= 0) & (tile < kid_tiles))(
                functools.partial(kid_stage, stage, tile)
            )
        return carry

    lax.fori_loop(0, turns, turn_of, 0)
    combine(chips - 1)
    for at in range(chips - 2, chips):
        swap(at).wait_send()
    for shift in range(1, col_count):
        pl.semaphore_signal(
            ready, inc=1, device_id={"col": (col + shift) % col_count}, device_id_type=MESH
        )
    if order[-1] > 0:
        head(order[-1], 0)
    for pair in (order[-1], order[-2]):
        if pair < end:
            head(pair, end)

    def tail_turn(index, carry):
        for stage in range(1, chips):
            tile = index - (stage - 1)
            pl.when((tile >= 0) & (tile < kid_tiles))(
                functools.partial(kid_stage, stage, tile)
            )
        return carry

    lax.fori_loop(turns, kid_tiles + chips - 2, tail_turn, 0)
    chain(order[:2])
    chain(order[2:])

    landing = pl.ds(2 * rows, rows)
    leaving = 3 * rows

    def leaf_move(shift, here):
        start, size = pieces[here]
        goal = (col + shift) % col_count
        src = pl.ds(pl.multiple_of(goal * most, most), size)
        dst = pl.ds(pl.multiple_of(core * half + start, 16), size)
        return remote(
            ring.at[1, src, pl.ds(leaving, rows)], ring.at[1, dst, landing],
            leaf_send.at[shift - 1], leaf_recv.at[shift - 1], {"col": goal},
        )

    def merge(here):
        size = pieces[here][1]

        def arrive(tile, carry):
            for shift in range(1, row_count):
                kid_share(tile, shift, here, -1).wait_recv()
            return carry

        lax.fori_loop(0, kid_tiles, arrive, 0)

        def one(block, carry):
            first = kids[picks_ref[0, block], :size]
            second = kids[picks_ref[1, block], :size]
            goal = block // per_leaf
            lane = pl.multiple_of(leaving + block % per_leaf * BLOCK, BLOCK)
            ring[1, pl.ds(pl.multiple_of(goal * most, most), size), pl.ds(lane, BLOCK)] = (
                first + second
            ).astype(jnp.bfloat16)
            return carry

        lax.fori_loop(0, blocks, one, 0)
        for shift in range(1, col_count):
            leaf_move(shift, here).start()
        start = pieces[here][0]
        dst = pl.ds(pl.multiple_of(core * half + start, 16), size)
        src = pl.ds(pl.multiple_of(col * most, most), size)
        ring[1, dst, landing] = ring[1, src, pl.ds(leaving, rows)]

    pl.semaphore_wait(ready, col_count - 1)
    each_chip(merge)
    work = parts.at[1]
    start_tiles, run = finishing(
        (row_count, col_count, test.shape[1] // rows),
        lambda place: ring.at[0, :, pl.ds(place * rows, rows)],
        lambda parity: ring.at[1, pl.ds(parity * probes, probes), pl.ds(0, rows)],
        front_hbm,
        basis_ref,
        core_ref,
        parts.at[3, :, pl.ds(0, slab_in.shape[0] * BLOCK)],
        work,
        parts.at[0],
        ring.at[1, pl.ds(0, probes), pl.ds(rows, rows)],
        ring.at[1, pl.ds(probes, probes), pl.ds(rows, rows)],
        ring.at[0, pl.ds(0, probes), pl.ds(3 * rows, rows)],
        ring.at[0, pl.ds(probes, probes), pl.ds(3 * rows, rows)],
        test,
        slab_in,
        stage_out,
        stage_in,
        sems,
    )
    start_tiles()

    def land():
        for shift in range(1, col_count):
            source = (col - shift + col_count) % col_count
            far = source // 2
            for there in range(chips):

                def wait(there=there):
                    start, size = pieces[there]
                    dst = pl.ds(pl.multiple_of(source % 2 * half + start, 16), size)
                    remote(
                        ring.at[1, pl.ds(0, size), pl.ds(leaving, rows)],
                        ring.at[1, dst, landing],
                        leaf_send.at[shift - 1], leaf_recv.at[shift - 1], {"col": source},
                    ).wait_recv()

                pl.when(far == there)(wait)

    land()
    work[...] = sums[chip] + ring[1, :probes, 2 * rows : 3 * rows].astype(jnp.float32)

    def drain(here):
        def one(tile, carry):
            for goal in range(chips):
                if goal != here:
                    kid_hop(tile, goal, goal > here, False, col).wait_send()
            for shift in range(1, row_count):
                kid_share(tile, shift, here).wait_send()
            return carry

        lax.fori_loop(0, kid_tiles, one, 0)
        for pair in range(chips):
            if pair != here:
                for piece in range(subs):
                    hop(pair, piece, pair > here, False, col).wait_send()
        for shift in range(1, col_count):
            leaf_move(shift, here).wait_send()

    run()
    each_chip(drain)


def sample_of(picks, kid_test, test, kids, front, row_count, col_count):
    depth = front.shape[1]
    probes = test.shape[0]
    kid_rows, kid_depth = kids.shape[1:]
    chips = col_count // 2
    half = probes // 2
    kid_each = kid_rows // LEAF
    kid_tiles = kids.shape[0] * kid_each
    per_leaf = LEAF // BLOCK
    blocks = front.shape[0] // BLOCK
    subs = 4
    pieces = spread(half, chips, 16)
    most = max(size for _, size in pieces)
    low, high, order = 0, chips - 1, []
    while low <= high:
        order += [high] if low == high else [high, low]
        low, high = low + 1, high - 1
    f32, bf16 = jnp.float32, jnp.bfloat16
    steps = probes // PIVOTS
    groups = -(-probes // BLOCK)
    rank_rows = probes // col_count
    padded = -(-rank_rows // 16) * 16
    slab = pltpu.VMEM((groups, col_count, per_leaf * (BLOCK // col_count), BLOCK), bf16)
    dims = (row_count, col_count, kid_tiles, kid_each, tuple(order), tuple(pieces), subs)
    any_spec = pl.BlockSpec(memory_space=pl.ANY)
    dma = pltpu.SemaphoreType.DMA
    return pl.pallas_call(
        functools.partial(sample_kernel, dims),
        out_shape=(
            jax.ShapeDtypeStruct((blocks, BLOCK // col_count, probes), bf16),
            jax.ShapeDtypeStruct((col_count, rank_rows, probes), f32),
        ),
        in_specs=[pl.BlockSpec(memory_space=pltpu.SMEM)] + [any_spec] * 4,
        out_specs=(
            pl.BlockSpec(memory_space=pltpu.VMEM),
            pl.BlockSpec(memory_space=pltpu.VMEM),
        ),
        scratch_shapes=[
            pltpu.VMEM((kids.shape[0], probes, kid_depth), bf16),
            pltpu.VMEM((probes, depth), bf16),
            pltpu.VMEM((2, LEAF, depth), bf16),
            pltpu.VMEM((4, probes, LEAF), f32),
            pltpu.VMEM((kid_tiles, half, LEAF), f32),
            pltpu.VMEM((chips, probes, LEAF), f32),
            pltpu.VMEM((kid_tiles, half, LEAF), bf16),
            pltpu.VMEM((kid_tiles, most, LEAF), bf16),
            pltpu.VMEM((chips, probes, LEAF), bf16),
            pltpu.VMEM((probes, LEAF), bf16),
            pltpu.VMEM((row_count * blocks + 1, most, BLOCK), f32),
            dma((2,)),
            dma((2,)),
            dma((kid_tiles + chips,)),
            dma((kid_tiles + chips,)),
            dma((kid_tiles, chips)),
            dma((kid_tiles, chips)),
            dma((kid_tiles,)),
            dma((chips, subs)),
            dma((chips, subs)),
            dma((subs,)),
            dma((kid_tiles, row_count - 1)),
            dma((kid_tiles, row_count - 1)),
            dma((col_count - 1,)),
            dma((col_count - 1,)),
            slab,
            pltpu.VMEM((3, col_count, padded, probes), bf16),
            pltpu.VMEM((col_count, padded, probes), bf16),
            pltpu.SemaphoreType.REGULAR,
            dma((depth // LEAF,)),
            dma((3,)),
            dma((2, steps)),
            dma((2, steps)),
            dma((steps,)),
            dma((2, steps)),
            dma((groups, col_count)),
            dma((groups, col_count)),
            dma((3, col_count)),
            dma((col_count,)),
        ],
        compiler_params=pltpu.CompilerParams(
            collective_id=0, has_side_effects=True, vmem_limit_bytes=67043328
        ),
        cost_estimate=pl.CostEstimate(
            flops=4 * front.shape[0] * depth * probes,
            bytes_accessed=4 * front.shape[0] * depth,
            transcendentals=0,
        ),
        name="sample",
    )(picks, kid_test, test, kids, front)


def general(parent_front, child_update, parent_test, child_test, child_map):
    row_count = lax.axis_size("row")
    col_count = lax.axis_size("col")
    row_index = lax.axis_index("row")
    col_index = lax.axis_index("col")
    slab = BLOCK // col_count
    own_blocks = parent_front.shape[0] // BLOCK
    probes = parent_test.shape[1]
    per_leaf = LEAF // BLOCK
    leaf_count = own_blocks // per_leaf
    col_leaves = parent_front.shape[1] // LEAF
    shrink = 1.0 / math.sqrt(LEAF)

    tie = lax.optimization_barrier
    pair_index = col_index // 2
    parity = col_index % 2
    half = own_blocks // 2 * BLOCK
    sign = jnp.reshape(parity, (1,)).astype(jnp.int32)
    fronts, tests = parent_front[None], parent_test[None]
    kid_rows = child_update.shape[1]

    def send_tile(position, front):
        sibling = col_index * col_leaves + position
        row_start = jnp.bitwise_xor(sibling, 1) % leaf_count * LEAF
        tile = lax.dynamic_slice(front, (row_start, position * LEAF), (LEAF, LEAF))
        routes = []
        for row in range(row_count):
            for slot in range(leaf_count):
                other = (row * leaf_count + slot) ^ 1
                if other % col_leaves == position:
                    routes.append(
                        (row * col_count + other // col_leaves, row * col_count + slot)
                    )
        return lax.ppermute(tile, ("row", "col"), routes)

    pieces = {position: send_tile(position, parent_front) for position in range(0, col_leaves, 2)}

    jobs = (
        (child_update, child_test, 0, 0, kid_rows),
        (child_update, child_test, 1, 0, kid_rows),
        (fronts, tests, 0, 0, half),
        (fronts, tests, 0, half, half),
    )
    sums = []
    for front, test, which, first_row, rows in jobs:
        halves = probe(front, test, which, first_row, rows, col_count, sign)
        kept, swapped = swap_pair(halves, col_count)
        sums.append(send_pairs(kept, swapped, col_count, pair_index))
    (first_own, first_came), (second_own, second_came) = sums[:2]
    (upper_own, upper_came), (lower_own, lower_came) = sums[2:]

    kid_share = jnp.stack([add_up(first_own, first_came), add_up(second_own, second_came)])
    all_kids = lax.all_gather(kid_share, "row", axis=1, tiled=True)
    own_share = jnp.concatenate([add_up(upper_own, upper_came), add_up(lower_own, lower_came)])

    targets = jnp.arange(own_blocks, dtype=jnp.int32)
    mapped = child_map - row_index * own_blocks
    onehot = (mapped[:, None, :] == targets[None, :, None]).astype(jnp.float32)
    sample = own_share + jnp.einsum("cpn,cnsr->psr", onehot, all_kids, precision=HIGH)

    by_leaf = sample.reshape(leaf_count, per_leaf * slab, probes)
    by_leaf = jnp.pad(by_leaf, ((0, col_count - leaf_count), (0, 0), (0, 0)))
    leaf_rows = lax.all_to_all(by_leaf, "col", 0, 0, tiled=True).reshape(LEAF, probes)

    leaf_rows, front = tie((leaf_rows, parent_front))
    for position in range(1, col_leaves, 2):
        pieces[position] = send_tile(position, front)
    wanted = jnp.bitwise_xor(col_index, 1) % col_leaves
    front_tile = pieces[0]
    for position in range(1, col_leaves):
        front_tile = jnp.where(wanted == position, pieces[position], front_tile)

    basis_t = leaf_basis_of(leaf_rows.T)
    basis = basis_t.T
    slabs = lax.all_to_all(
        basis.reshape(col_count, per_leaf * slab, probes), "col", 0, 0, tiled=True
    )
    leaf_basis = slabs[:leaf_count].reshape(own_blocks, slab, probes)

    natural = (
        basis.reshape(col_count, per_leaf, slab, probes)
        .transpose(1, 0, 2, 3)
        .reshape(LEAF, probes)
    )
    sibling_basis = lax.ppermute(natural, "col", [(c, c ^ 1) for c in range(col_count)])
    product = jnp.dot(front_tile, sibling_basis, preferred_element_type=jnp.float32) * shrink
    core = (
        lax.dot_general(
            natural,
            product.astype(jnp.bfloat16),
            (((0,), (0,)), ((), ())),
            preferred_element_type=jnp.float32,
        )
        * shrink
    )
    cores = lax.all_to_all(
        core.reshape(col_count, probes // col_count, probes), "col", 0, 0, tiled=True
    )
    return (leaf_basis, cores[:leaf_count])


def fits(parent_front, child_update, parent_test, row_count, col_count):
    leaf_count = parent_front.shape[0] // LEAF
    return (
        leaf_count == col_count
        and row_count * 2 == col_count
        and child_update.shape[0] * child_update.shape[1] // LEAF % 4 == 0
        and all(
            sum(abs(pair - row) > 1 and pair % 2 == core for pair in range(row_count)) < 2
            for row in range(row_count)
            for core in range(2)
        )
        and parent_front.shape[1] // LEAF * 2 == leaf_count
        and col_count % 2 == 0
        and parent_front.shape[1] % LEAF == 0
        and 2 * PIVOTS == BLOCK
        and parent_front.shape[1] >= 4 * LEAF
        and LEAF // col_count * -(-parent_test.shape[1] // BLOCK) <= parent_test.shape[1]
        and parent_test.shape[1] * 2 <= LEAF
        and child_update.shape[1] % LEAF == 0
        and 2 * parent_front.shape[1] * LEAF * 2 < 16 << 20
    )


def picks_of(child_map, row_index, row_count, own_blocks):
    kid_count, kid_blocks = child_map.shape
    each = kid_blocks // row_count
    at = jnp.arange(kid_blocks, dtype=jnp.int32)
    which = jnp.arange(kid_count, dtype=jnp.int32)
    value = (at // each * own_blocks + at % each)[None, :] + which[:, None] * each
    targets = jnp.arange(own_blocks, dtype=jnp.int32)
    match = (child_map - row_index * own_blocks)[:, None, :] == targets[None, :, None]
    found = jnp.max(jnp.where(match, value[:, None, :], -1), axis=2)
    return jnp.where(found < 0, row_count * own_blocks, found)


def local(parent_front, child_update, parent_test, child_test, child_map):
    row_count = lax.axis_size("row")
    col_count = lax.axis_size("col")
    if not fits(parent_front, child_update, parent_test, row_count, col_count):
        return general(parent_front, child_update, parent_test, child_test, child_map)
    row_index = lax.axis_index("row")
    own_blocks = parent_front.shape[0] // BLOCK
    picks = picks_of(child_map, row_index, row_count, own_blocks)
    outs = sample_of(
        picks, child_test.transpose(0, 2, 1), parent_test.T, child_update, parent_front,
        row_count, col_count,
    )
    return tuple(outs)


def solution(mesh):
    in_specs = (P("row", "col"), P(None, "row", "col"), P("col", None), P(None, "col", None), P())
    out_specs = (P("row", "col", None), P("row", "col", None))
    return jax.shard_map(local, mesh=mesh, in_specs=in_specs, out_specs=out_specs, check_vma=False)
```

```python
import functools
import math

import jax
import jax.numpy as jnp
from jax import lax
from jax.experimental import pallas as pl
from jax.experimental.pallas import tpu as pltpu
from jax.sharding import PartitionSpec as P


LEAF = 896
BLOCK = 128
PIVOTS = 64
GROUP = 8

HIGH = lax.Precision.HIGHEST
MESH = pl.DeviceIdType.MESH


def dot(a, b, dims):
    return lax.dot_general(
        a, b, (dims, ((), ())), precision=HIGH, preferred_element_type=jnp.float32
    )


def inverse_factor(tile, nb):
    ridx = lax.broadcasted_iota(jnp.int32, tile.shape, 0)
    lane = lax.broadcasted_iota(jnp.int32, tile.shape, 1)
    for j in range(0, nb, GROUP):
        cols = [
            jnp.broadcast_to(tile[:, nb + j + k : nb + j + k + 1], tile.shape)
            for k in range(GROUP)
        ]
        rows = [tile[j + k : j + k + 1, :] for k in range(GROUP)]
        for k in range(GROUP):
            at = j + k
            factor = jnp.where(ridx > at, cols[k] * (1.0 / cols[k][at : at + 1, :]), 0.0)
            for m in range(k + 1, GROUP):
                cols[m] = cols[m] - factor * cols[m][at : at + 1, :]
                rows[m] = rows[m] - factor[j + m : j + m + 1, :] * rows[k]
            cols[k] = factor
        for k in range(GROUP):
            tile = tile - cols[k] * rows[k]
    pivots = jnp.sum(jnp.where(lane == ridx + nb, tile, 0.0), axis=1, keepdims=True)
    return tile[:, :nb] * lax.rsqrt(pivots)


def basis_kernel(scale, yt_ref, qt_ref, gram_ref, work_ref):
    nb = PIVOTS
    probes = yt_ref.shape[0]
    work_ref[...] = yt_ref[...]
    gram_ref[...] = dot(yt_ref[...], yt_ref[...], ((1,), (1,)))

    def step(index, carry):
        start = pl.multiple_of(index * nb, nb)
        panel = gram_ref[pl.ds(start, nb), :]
        source = lax.broadcasted_iota(jnp.int32, (probes, 2 * nb), 0)
        lane = lax.broadcasted_iota(jnp.int32, (probes, 2 * nb), 1)
        pick = jnp.where((lane >= nb) & (source == lane - nb + start), 1.0, 0.0)
        eye = jnp.where(
            lax.broadcasted_iota(jnp.int32, (nb, 2 * nb), 0)
            == lax.broadcasted_iota(jnp.int32, (nb, 2 * nb), 1),
            1.0,
            0.0,
        )
        inverse = inverse_factor(dot(panel, pick, ((1,), (0,))) + eye, nb)
        top = dot(inverse, panel, ((1,), (0,)))
        solved = dot(inverse, work_ref[pl.ds(start, nb), :], ((1,), (0,)))
        qt_ref[pl.ds(start, nb), :] = (solved * scale).astype(qt_ref.dtype)
        gram_ref[...] -= dot(top, top, ((0,), (0,)))
        work_ref[...] -= dot(top, solved, ((0,), (0,)))
        return carry

    lax.fori_loop(0, probes // nb, step, 0)


def leaf_basis_of(yt):
    probes, rows = yt.shape
    return pl.pallas_call(
        functools.partial(basis_kernel, math.sqrt(LEAF)),
        out_shape=jax.ShapeDtypeStruct((probes, rows), jnp.bfloat16),
        in_specs=[pl.BlockSpec(memory_space=pltpu.VMEM)],
        out_specs=pl.BlockSpec(memory_space=pltpu.VMEM),
        scratch_shapes=[
            pltpu.VMEM((probes, probes), jnp.float32),
            pltpu.VMEM((probes, rows), jnp.float32),
        ],
        compiler_params=pltpu.CompilerParams(vmem_limit_bytes=40 << 20),
        cost_estimate=pl.CostEstimate(
            flops=40 * probes * probes * rows,
            bytes_accessed=6 * probes * rows,
            transcendentals=0,
        ),
        name="leaf_basis",
    )(yt)


def probe_kernel(parity_ref, front_ref, test_ref, kept_ref, sent_ref):
    total = jnp.dot(front_ref[...], test_ref[...], preferred_element_type=jnp.float32)
    blocks, pairs, slab, probes = kept_ref.shape
    view = total.reshape(blocks * pairs, 2, slab, probes)
    even = parity_ref[0] == 0
    kept_ref[...] = jnp.where(even, view[:, 0], view[:, 1]).reshape(kept_ref.shape)
    sent_ref[...] = jnp.where(even, view[:, 1], view[:, 0]).reshape(sent_ref.shape)


def probe(front, test, which, first_row, rows, col_count, parity):
    depth, probes = test.shape[1:]
    tile = max(t for t in range(BLOCK, 4 * BLOCK + 1, BLOCK) if rows % t == 0)
    pairs, slab = col_count // 2, BLOCK // col_count
    half = jax.ShapeDtypeStruct((rows // BLOCK, pairs, slab, probes), jnp.float32)
    out_spec = pl.BlockSpec((tile // BLOCK, pairs, slab, probes), lambda i, p: (i, 0, 0, 0))
    skip = first_row // tile
    return pl.pallas_call(
        probe_kernel,
        out_shape=(half, half),
        grid_spec=pltpu.PrefetchScalarGridSpec(
            num_scalar_prefetch=1,
            grid=(rows // tile,),
            in_specs=[
                pl.BlockSpec((None, tile, depth), lambda i, p: (which, skip + i, 0)),
                pl.BlockSpec((None, depth, probes), lambda i, p: (which, 0, 0)),
            ],
            out_specs=(out_spec, out_spec),
        ),
        compiler_params=pltpu.CompilerParams(vmem_limit_bytes=40 << 20),
        cost_estimate=pl.CostEstimate(
            flops=2 * rows * depth * probes,
            bytes_accessed=2 * rows * depth + 2 * depth * probes + 4 * rows * probes,
            transcendentals=0,
        ),
        name="probe",
    )(parity, front, test)


def swap_pair(halves, col_count):
    kept, sent = halves
    return kept, lax.ppermute(sent, "col", [(c, c ^ 1) for c in range(col_count)])


def send_pairs(kept, swapped, col_count, pair_index):
    pairs = col_count // 2

    def piece(pair):
        return lax.dynamic_index_in_dim(kept, pair, 1, False) + lax.dynamic_index_in_dim(
            swapped, pair, 1, False
        )

    came = [
        lax.ppermute(
            piece((pair_index + shift) % pairs).astype(jnp.bfloat16),
            "col",
            [(c, (c + 2 * shift) % col_count) for c in range(col_count)],
        )
        for shift in range(1, pairs)
    ]
    return piece(pair_index), came


def add_up(own, came):
    for term in came:
        own = own + term.astype(jnp.float32)
    return own


def parts_of(x):
    high = x.astype(jnp.bfloat16).astype(jnp.float32)
    rest = x - high
    middle = rest.astype(jnp.bfloat16).astype(jnp.float32)
    return high, middle, rest - middle


def left_parts(x, axis):
    high, middle, low = parts_of(x)
    stacked = jnp.concatenate([high, high, middle, middle, high, low], axis=axis)
    return stacked.astype(jnp.bfloat16)


def right_parts(x):
    high, middle, low = parts_of(x)
    stacked = jnp.concatenate([high, middle, high, middle, low, high], axis=0)
    return stacked.astype(jnp.bfloat16)


def fast_dot(a, b, dims):
    return lax.dot_general(a, b, (dims, ((), ())), preferred_element_type=jnp.float32)


def finishing(
    dims, tile_at, far_at, front_hbm, basis_ref, core_ref, gram, work, exact, high, low,
    near_high, near_low, slab, slab_in, stage, stage_in, sems,
):
    groups, _, slab_rows, _ = slab_in.shape

    (
        tile_send, tile_recv, near_send, near_recv, far_send, far_recv, slab_send, slab_recv,
        core_send, core_recv,
    ) = sems
    _, col_count, tile_leaves = dims
    nb = PIVOTS
    chips = col_count // 2
    probes, rows = work.shape
    per_leaf = rows // BLOCK
    rank_rows = probes // col_count
    whole = probes // BLOCK * BLOCK
    fold = -(-rank_rows // 16) * 8
    packed = stage_in.shape[1]
    steps = probes // nb
    scale = math.sqrt(LEAF)
    shrink = 1.0 / scale
    row, col = lax.axis_index("row"), lax.axis_index("col")
    chip, core = col // 2, col % 2
    sibling = {"col": chip * 2 + 1 - core}
    at_home = chip == row

    def far_of(pair):
        return (pair >= row + 2) | (pair + 2 <= row)

    def remote(src, dst, send, recv, target):
        return pltpu.make_async_remote_copy(
            src_ref=src, dst_ref=dst, send_sem=send, recv_sem=recv,
            device_id=target, device_id_type=MESH,
        )

    def tile_source(position):
        slot = core * tile_leaves + (position ^ 1)
        return front_hbm.at[
            pl.ds(pl.multiple_of(slot * rows, rows), rows), pl.ds(position * rows, rows)
        ]

    def each_tile(act):
        for position in range(tile_leaves):
            parity = (position ^ 1) % 2
            pair = (core * tile_leaves + (position ^ 1)) // 2
            slot = pair * 2 + parity
            is_far = far_of(pair)
            goal = jnp.where(is_far, 2 * row + pair % 2, slot)
            for place, chosen in ((0, jnp.logical_not(is_far)), (1 + parity, is_far)):
                here = at_home & chosen & (goal == col)
                there = at_home & chosen & (goal != col)

                def stay(place=place, position=position):
                    act(
                        pltpu.make_async_copy(
                            tile_source(position), tile_at(place), tile_recv.at[place]
                        ),
                        False,
                    )

                def go(place=place, position=position, goal=goal):
                    act(
                        remote(
                            tile_source(position), tile_at(place), tile_send.at[position],
                            tile_recv.at[place], {"col": goal},
                        ),
                        True,
                    )

                pl.when(here)(stay)
                pl.when(there)(go)

    def start_tiles():
        each_tile(lambda copy, away: copy.start())

    def run():
        one, two, three = (part.astype(jnp.bfloat16) for part in parts_of(work[...]))
        both = ((1,), (1,))
        small = fast_dot(two, two, both) + fast_dot(one, three, both) + fast_dot(three, one, both)
        middle = fast_dot(one, two, both) + fast_dot(two, one, both)
        wide = gram.shape[1]
        gram[:, :probes] = fast_dot(one, one, both) + (middle + small)
        if wide > probes:
            gram[:, probes:] = jnp.zeros((probes, wide - probes), jnp.float32)

        def near_copy(step, which):
            span = pl.ds(pl.multiple_of(step * nb, nb), nb)
            src, dst = ((high, near_high), (low, near_low))[which]
            return remote(
                src.at[span], dst.at[span], near_send.at[which, step], near_recv.at[which, step],
                sibling,
            )

        def far_copy(step, parity):
            span = pl.ds(pl.multiple_of(step * nb, nb), nb)
            return remote(
                high.at[span], far_at(parity).at[span], far_send.at[step], far_recv.at[parity, step],
                {"col": 2 * row + chip % 2},
            )

        def slab_at(group, goal):
            return slab.at[
                pl.ds(pl.multiple_of(jnp.asarray(group * slab_rows, jnp.int32), 16), slab_rows),
                pl.ds(pl.multiple_of(jnp.asarray(goal * BLOCK, jnp.int32), BLOCK), BLOCK),
            ]

        def slab_copy(group, shift, toward=1):
            other = (col + toward * shift + col_count) % col_count
            owner = col if toward == 1 else other
            return remote(
                slab_at(group, other), slab_in.at[group, owner],
                slab_send.at[group, shift], slab_recv.at[group, shift], {"col": other},
            )

        per_slab = BLOCK // col_count

        def send_slabs(group, count):
            start = pl.multiple_of(group * BLOCK, BLOCK)
            for block in range(per_leaf):
                turned = exact[pl.ds(start, count), block * BLOCK : (block + 1) * BLOCK].T
                for goal in range(col_count):
                    place = slab_at(group, goal).at[
                        pl.ds(block * per_slab, per_slab), pl.ds(0, count)
                    ]
                    place[...] = turned[
                        goal * per_slab : (goal + 1) * per_slab
                    ].astype(slab.dtype)
            for shift in range(1, col_count):
                ready = jnp.logical_not(far_of(chip) & ((col + shift) % col_count // 2 == row))
                pl.when(ready)(lambda shift=shift: slab_copy(group, shift).start())
            slab_in[group, col] = slab_at(group, col)[...]

        def step(index, carry):
            start = pl.multiple_of(index * nb, nb)
            panel = gram[pl.ds(start, nb), :]
            square = gram[pl.ds(start, nb), pl.ds(pl.multiple_of(index // 2 * 2 * nb, 2 * nb), 2 * nb)]
            square = jnp.where(index % 2 == 0, pltpu.roll(square, nb, 1), square)
            lane = lax.broadcasted_iota(jnp.int32, square.shape, 1)
            eye = jnp.where(lax.broadcasted_iota(jnp.int32, square.shape, 0) == lane, 1.0, 0.0)
            inverse = inverse_factor(jnp.where(lane >= nb, square, eye), nb)
            inverse_parts = left_parts(inverse, 1)
            top = fast_dot(inverse_parts, right_parts(panel), ((1,), (0,)))
            solved = fast_dot(inverse_parts, right_parts(work[pl.ds(start, nb), :]), ((1,), (0,)))
            scaled = solved * scale
            rounded = scaled.astype(high.dtype)
            exact[pl.ds(start, nb), :] = scaled
            high[pl.ds(start, nb), :] = rounded
            low[pl.ds(start, nb), :] = (scaled - rounded.astype(jnp.float32)).astype(low.dtype)
            top_parts = left_parts(top[:, :probes], 0)
            gram[...] -= fast_dot(top_parts, right_parts(top), ((0,), (0,)))
            work[...] -= fast_dot(top_parts, right_parts(solved), ((0,), (0,)))

            @pl.when(far_of(chip))
            def _():
                for parity in range(2):
                    pl.when(core == parity)(lambda parity=parity: far_copy(index, parity).start())

            @pl.when(jnp.logical_not(far_of(chip)))
            def _():
                near_copy(index, 0).start()
                near_copy(index, 1).start()

            @pl.when(index % 2 == 1)
            def _():
                send_slabs(index // 2, BLOCK)

            return carry

        lax.fori_loop(0, steps, step, 0)
        if steps % 2 == 1:
            send_slabs(groups - 1, nb)

        def times(a, b):
            return lax.dot_general(
                a, b, (((1,), (1,)), ((), ())), preferred_element_type=jnp.float32
            )

        def core_copy(place, goal, slot):
            return remote(
                stage.at[place, goal], stage_in.at[slot], core_send.at[place, goal],
                core_recv.at[slot], {"col": goal},
            )

        def send_core(place, slot, value):
            value = value * shrink
            for goal in range(col_count):
                piece = value[goal * rank_rows : (goal + 1) * rank_rows]
                columns = [piece[:, at : at + BLOCK] for at in range(0, whole, BLOCK)]
                last = jnp.concatenate(
                    [piece[:fold, whole:], piece[rank_rows - fold :, whole:]], axis=1
                )
                filler = jnp.zeros((packed - len(columns) * rank_rows - fold, BLOCK), jnp.float32)
                stage[place, goal] = jnp.concatenate(columns + [last, filler], axis=0).astype(
                    stage.dtype
                )

                @pl.when(goal != col)
                def _(goal=goal):
                    core_copy(place, goal, slot).start()

                @pl.when(goal == col)
                def _(goal=goal):
                    stage_in[slot] = stage[place, goal]

        def wait_tile(place, source):
            @pl.when(source == col)
            def _():
                pltpu.make_async_copy(
                    front_hbm.at[pl.ds(0, rows), pl.ds(0, rows)], tile_at(place),
                    tile_recv.at[place],
                ).wait()

            @pl.when(source != col)
            def _():
                remote(
                    front_hbm.at[pl.ds(0, rows), pl.ds(0, rows)], tile_at(place), tile_send.at[0],
                    tile_recv.at[place], {"col": source},
                ).wait_recv()

        @pl.when(jnp.logical_not(far_of(chip)))
        def _():
            wait_tile(0, 2 * row + col // tile_leaves)
            for index in range(steps):
                near_copy(index, 0).wait_recv()
                near_copy(index, 1).wait_recv()
            product = (times(near_high[...], tile_at(0)[...]) + times(near_low[...], tile_at(0)[...])) * shrink
            rounded = product.astype(jnp.bfloat16)
            rest = (product - rounded.astype(jnp.float32)).astype(jnp.bfloat16)
            send_core(
                0, col,
                times(high[...], rounded) + (times(low[...], rounded) + times(high[...], rest)),
            )

        for pair in range(chips):

            @pl.when(at_home & far_of(pair) & (core == pair % 2))
            def _(pair=pair):
                for parity in range(2):
                    for index in range(steps):
                        span = pl.ds(index * nb, nb)
                        remote(
                            high.at[span], far_at(parity).at[span], far_send.at[index],
                            far_recv.at[parity, index], {"col": 2 * pair + parity},
                        ).wait_recv()
                for parity in range(2):
                    slot = 2 * pair + parity
                    wait_tile(1 + parity, 2 * row + slot // tile_leaves)
                    product = times(far_at(1 - parity)[...], tile_at(1 + parity)[...]) * shrink
                    send_core(1 + parity, slot, times(far_at(parity)[...], product.astype(jnp.bfloat16)))

        def late(shift):
            other = (col - shift + col_count) % col_count
            return at_home & far_of(other // 2)

        for shift in range(1, col_count):

            @pl.when(jnp.logical_not(late(shift)))
            def _(shift=shift):
                for group in range(groups):
                    slab_copy(group, shift, -1).wait_recv()

        for shift in range(1, col_count):

            @pl.when(far_of(chip) & ((col + shift) % col_count // 2 == row))
            def _(shift=shift):
                for group in range(groups):
                    slab_copy(group, shift).start()

        for shift in range(1, col_count):

            @pl.when(late(shift))
            def _(shift=shift):
                for group in range(groups):
                    slab_copy(group, shift, -1).wait_recv()

        for slot in range(col_count):
            for group in range(groups):
                count = min(BLOCK, probes - group * BLOCK)
                basis_ref[
                    slot * per_leaf : (slot + 1) * per_leaf, :, group * BLOCK : group * BLOCK + count
                ] = slab_in[group, slot].reshape(per_leaf, per_slab, BLOCK)[:, :, :count]
        for slot in range(col_count):
            pair = slot // 2
            source = jnp.where(far_of(pair), 2 * row + pair % 2, slot)

            @pl.when(source != col)
            def _(slot=slot, source=source):
                remote(
                    stage.at[0, 0], stage_in.at[slot], core_send.at[0, 0], core_recv.at[slot],
                    {"col": source},
                ).wait_recv()

            came = stage_in[slot].astype(jnp.float32)
            for at in range(0, whole, BLOCK):
                first = at // BLOCK * rank_rows
                core_ref[slot, :, at : at + BLOCK] = came[first : first + rank_rows]
            last = came[whole // BLOCK * rank_rows :][:fold]
            core_ref[slot, :fold, whole:] = last[:, : probes - whole]
            core_ref[slot, fold:, whole:] = last[2 * fold - rank_rows :, probes - whole :]

        def settle(copy, away):
            if away:
                copy.wait_send()

        each_tile(settle)

        @pl.when(far_of(chip))
        def _():
            for index in range(steps):
                far_copy(index, 0).wait_send()

        @pl.when(jnp.logical_not(far_of(chip)))
        def _():
            for index in range(steps):
                near_copy(index, 0).wait_send()
                near_copy(index, 1).wait_send()
            for goal in range(col_count):
                pl.when(goal != col)(lambda goal=goal: core_copy(0, goal, col).wait_send())

        for group in range(groups):
            for shift in range(1, col_count):
                slab_copy(group, shift).wait_send()
        for pair in range(chips):

            @pl.when(at_home & far_of(pair) & (core == pair % 2))
            def _(pair=pair):
                for parity in range(2):
                    for goal in range(col_count):
                        pl.when(goal != col)(
                            lambda goal=goal, parity=parity: core_copy(
                                1 + parity, goal, 2 * pair + parity
                            ).wait_send()
                        )

    return start_tiles, run


def spread(total, parts, grain):
    base = total // grain
    cuts = [base * (i + 1) // parts * grain for i in range(parts)]
    starts = [0] + cuts[:-1]
    return [(s, e - s) for s, e in zip(starts, cuts)]


def sample_kernel(
    dims,
    picks_ref,
    kid_test_hbm,
    test_hbm,
    kids_hbm,
    front_hbm,
    basis_ref,
    core_ref,
    kid_test,
    test,
    ring,
    parts,
    kid_sum,
    sums,
    kid_in,
    kid_in_two,
    came,
    came_two,
    kids,
    load_sem,
    test_sem,
    swap_send,
    swap_recv,
    kid_send,
    kid_recv,
    kid_recv_two,
    line_send,
    line_recv,
    line_recv_two,
    row_send,
    row_recv,
    leaf_send,
    leaf_recv,
    slab_in,
    stage_out,
    stage_in,
    ready,
    *sems,
):
    row_count, col_count, kid_tiles, kid_each, order, slots, subs = dims
    chips = col_count // 2
    probes, rows = parts.shape[1:]
    half = probes // 2
    per_leaf = rows // BLOCK
    blocks = front_hbm.shape[0] // BLOCK
    most = kids.shape[1]
    pieces = slots
    row, col = lax.axis_index("row"), lax.axis_index("col")
    chip, core = col // 2, col % 2
    sibling = {"col": chip * 2 + 1 - core}

    def remote(src, dst, send, recv, target):
        return pltpu.make_async_remote_copy(
            src_ref=src, dst_ref=dst, send_sem=send, recv_sem=recv,
            device_id=target, device_id_type=MESH,
        )

    barrier = pltpu.get_barrier_semaphore()
    for shift in range(1, col_count):
        pl.semaphore_signal(
            barrier, inc=1, device_id={"col": (col + shift) % col_count}, device_id_type=MESH
        )
    for shift in range(1, row_count):
        pl.semaphore_signal(
            barrier, inc=1, device_id={"row": (row + shift) % row_count}, device_id_type=MESH
        )

    kid_depth = kid_test.shape[2]

    def pair_at(at):
        return jnp.where(at % 2 == 0, chips - 1 - at // 2, at // 2)

    def load_kid(index):
        index = jnp.asarray(index, jnp.int32)
        start = pl.multiple_of(index % kid_each * rows, rows)
        return pltpu.make_async_copy(
            kids_hbm.at[index // kid_each, pl.ds(start, rows)],
            ring.at[index % 2, :, pl.ds(0, kid_depth)],
            load_sem.at[index % 2],
        )

    def load_front(index):
        index = jnp.asarray(index, jnp.int32)
        leaf = 2 * pair_at(index // 2) + jnp.where(index % 2 == 0, 1 - core, core)
        return pltpu.make_async_copy(
            front_hbm.at[pl.ds(pl.multiple_of(leaf * rows, rows), rows)],
            ring.at[index % 2],
            load_sem.at[index % 2],
        )

    kid_test_load = pltpu.make_async_copy(kid_test_hbm, kid_test, test_sem.at[0])
    test_load = pltpu.make_async_copy(test_hbm, test, test_sem.at[1])
    load_kid(0).start()
    kid_test_load.start()
    load_kid(1).start()
    test_load.start()
    kid_test_load.wait()

    def product(left, right):
        return lax.dot_general(
            left, right, (((1,), (1,)), ((), ())), preferred_element_type=jnp.float32
        )

    def kid_swap(tile):
        away = pl.ds(pl.multiple_of((1 - core) * half, half), half)
        return remote(
            parts.at[tile % 4, away], kid_sum.at[tile],
            swap_send.at[tile], swap_recv.at[tile], sibling,
        )

    def swap(at):
        return remote(
            parts.at[2 * at % 4], sums.at[pair_at(at)],
            swap_send.at[kid_tiles + at], swap_recv.at[kid_tiles + at], sibling,
        )

    def kid_combine(tile):
        kid_swap(tile).wait_recv()
        own = pl.ds(pl.multiple_of(core * half, half), half)
        kid_sum[tile] += parts[tile % 4, own]

    def combine(at):
        swap(at).wait_recv()
        sums[pair_at(at)] += parts[(2 * at + 1) % 4]

    def kid_hop(tile, goal, right, last, target):
        start, size = pieces[goal]
        span = pl.ds(start, size)
        two = last and not right
        dst = kid_in_two.at[tile, pl.ds(0, size)] if two else kid_in.at[tile, span]
        sem = kid_recv_two.at[tile] if two else kid_recv.at[tile, goal]
        return remote(
            kid_in.at[tile, span], dst, kid_send.at[tile, goal], sem, {"col": target}
        )

    def kid_push(tile, goal, here):
        start, size = pieces[goal]
        span = pl.ds(start, size)
        right = goal > here
        last = goal == here + 1 if right else goal == here - 1
        kid_in[tile, span] = kid_sum[tile, span].astype(jnp.bfloat16)
        kid_hop(tile, goal, right, last, col + 2 if right else col - 2).start()

    def kid_take(tile, goal, here, right):
        start, size = pieces[goal]
        span = pl.ds(start, size)
        last = goal == here
        kid_hop(tile, goal, right, last, col - 2 if right else col + 2).wait_recv()
        if last and not right:
            kid_sum[tile, span] += kid_in_two[tile, :size].astype(jnp.float32)
        else:
            kid_sum[tile, span] += kid_in[tile, span].astype(jnp.float32)

    def kid_share(tile, shift, here, toward=1):
        size = pieces[here][1]
        other = (row + toward * shift + row_count) % row_count
        owner = row if toward == 1 else other
        span = kids.at[pl.ds(owner * blocks + tile * per_leaf, per_leaf), pl.ds(0, size)]
        return remote(
            span, span, row_send.at[tile, shift - 1], row_recv.at[tile, shift - 1],
            {"row": other},
        )

    def on_chip(here, body):
        pl.when(chip == here)(body)

    def each_chip(body):
        for here in range(chips):
            on_chip(here, functools.partial(body, here))

    end = chips - 1

    def kid_head(tile):
        def right():
            for goal in reversed(range(1, chips)):
                kid_push(tile, goal, 0)

        def left():
            for goal in range(end):
                kid_push(tile, goal, end)

        on_chip(0, right)
        on_chip(end, left)

    def kid_stage(stage, tile):
        def right():
            for goal in reversed(range(stage + 1, chips)):
                kid_take(tile, goal, stage, True)
                kid_push(tile, goal, stage)

        def left():
            for goal in range(end - stage):
                kid_take(tile, goal, end - stage, False)
                kid_push(tile, goal, end - stage)

        def final(here):
            if here > 0:
                kid_take(tile, here, here, True)
            if here < end:
                kid_take(tile, here, here, False)
            start, size = pieces[here]
            for block in range(per_leaf):
                kids[row * blocks + tile * per_leaf + block, :size] = kid_sum[
                    tile, start : start + size, block * BLOCK : (block + 1) * BLOCK
                ].astype(kids.dtype)
            for shift in range(1, row_count):
                kid_share(tile, shift, here).start()

        if stage < end:
            on_chip(stage, right)
            on_chip(end - stage, left)
        for here in range(chips):
            if max(here, end - here) == stage:
                on_chip(here, functools.partial(final, here))

    sub = probes // subs

    def hop(pair, piece, right, last, target):
        span = pl.ds(pl.multiple_of(piece * sub, sub), sub)
        two = last and not right
        dst = came_two.at[span] if two else came.at[pair, span]
        sem = line_recv_two.at[piece] if two else line_recv.at[pair, piece]
        return remote(
            came.at[pair, span], dst, line_send.at[pair, piece], sem, {"col": target}
        )

    def push(pair, piece, here):
        span = pl.ds(pl.multiple_of(piece * sub, sub), sub)
        right = pair > here
        last = pair == here + 1 if right else pair == here - 1
        came[pair, span] = sums[pair, span].astype(jnp.bfloat16)
        hop(pair, piece, right, last, col + 2 if right else col - 2).start()

    def take(pair, piece, here, right):
        span = pl.ds(pl.multiple_of(piece * sub, sub), sub)
        last = pair == here
        hop(pair, piece, right, last, col - 2 if right else col + 2).wait_recv()
        if last and not right:
            sums[pair, span] += came_two[span].astype(jnp.float32)
        else:
            sums[pair, span] += came[pair, span].astype(jnp.float32)

    def head(pair, here):
        def body():
            def one(piece, carry):
                push(pair, piece, here)
                return carry

            lax.fori_loop(0, subs, one, 0)

        on_chip(here, body)

    def stage_of(stage, pair, piece):
        def right():
            take(pair, piece, stage, True)
            push(pair, piece, stage)

        def left():
            take(pair, piece, end - stage, False)
            push(pair, piece, end - stage)

        def final():
            if pair > 0:
                take(pair, piece, pair, True)
            if pair < end:
                take(pair, piece, pair, False)

        if pair > stage and stage < end:
            on_chip(stage, right)
        if pair < end - stage and stage < end:
            on_chip(end - stage, left)
        if max(pair, end - pair) == stage:
            on_chip(pair, final)

    def chain(pairs):
        deepest = max(max(pair, end - pair) for pair in pairs)

        def one(turn, carry):
            for stage in range(1, deepest + 1):
                at = turn - (stage - 1)

                @pl.when((at >= 0) & (at < subs))
                def _(stage=stage, at=at):
                    for pair in pairs:
                        stage_of(stage, pair, at)

            return carry

        lax.fori_loop(0, subs + deepest - 1, one, 0)

    kids[row_count * blocks] = jnp.zeros(kids.shape[1:], kids.dtype)

    def kid_turn(tile, carry):
        pl.when(tile >= 4)(lambda: kid_swap(tile - 4).wait_send())
        load_kid(tile).wait()
        parts[tile % 4] = product(kid_test[tile // kid_each], ring[tile % 2, :, :kid_depth])
        pl.when(tile + 2 < kid_tiles)(lambda: load_kid(tile + 2).start())
        pl.when(tile + 2 >= kid_tiles)(lambda: load_front(tile + 2 - kid_tiles).start())

        @pl.when(tile == 0)
        def _():
            pl.semaphore_wait(barrier, col_count - 1 + row_count - 1)

        kid_swap(tile).start()

        @pl.when(tile > 0)
        def _():
            kid_combine(tile - 1)
            kid_head(tile - 1)

        return carry

    lax.fori_loop(0, kid_tiles, kid_turn, 0)
    test_load.wait()
    turns = 2 * chips

    def turn_of(index, carry):
        at = index // 2

        @pl.when(index < 4)
        def _():
            kid_swap(kid_tiles + index - 4).wait_send()

        @pl.when((index >= 4) & (index % 2 == 0))
        def _():
            swap(at - 2).wait_send()

        load_front(index).wait()
        parts[index % 4] = product(test[...], ring[index % 2])
        pl.when(index + 2 < turns)(lambda: load_front(index + 2).start())

        @pl.when(index % 2 == 0)
        def _():
            swap(at).start()

        @pl.when(index == 0)
        def _():
            kid_combine(kid_tiles - 1)
            kid_head(kid_tiles - 1)

        @pl.when((index % 2 == 0) & (index > 0))
        def _():
            combine(at - 1)

        for spot in range(chips - 1):

            @pl.when(index == 2 * spot + 2)
            def _(spot=spot):
                if order[spot] > 0:
                    head(order[spot], 0)
                if order[spot] < end and spot < chips - 2:
                    head(order[spot], end)

        for stage in range(1, chips):
            tile = index - (stage - 1)
            pl.when((tile >= 0) & (tile < kid_tiles))(
                functools.partial(kid_stage, stage, tile)
            )
        return carry

    lax.fori_loop(0, turns, turn_of, 0)
    combine(chips - 1)
    for at in range(chips - 2, chips):
        swap(at).wait_send()
    for shift in range(1, col_count):
        pl.semaphore_signal(
            ready, inc=1, device_id={"col": (col + shift) % col_count}, device_id_type=MESH
        )
    if order[-1] > 0:
        head(order[-1], 0)
    for pair in (order[-1], order[-2]):
        if pair < end:
            head(pair, end)

    def tail_turn(index, carry):
        for stage in range(1, chips):
            tile = index - (stage - 1)
            pl.when((tile >= 0) & (tile < kid_tiles))(
                functools.partial(kid_stage, stage, tile)
            )
        return carry

    lax.fori_loop(turns, kid_tiles + chips - 2, tail_turn, 0)
    chain(order[:2])

    landing = pl.ds(2 * rows, rows)
    leaving = 3 * rows

    def leaf_move(shift, here):
        start, size = pieces[here]
        goal = (col + shift) % col_count
        src = pl.ds(pl.multiple_of(goal * most, most), size)
        dst = pl.ds(pl.multiple_of(core * half + start, 16), size)
        return remote(
            ring.at[1, src, pl.ds(leaving, rows)], ring.at[1, dst, landing],
            leaf_send.at[shift - 1], leaf_recv.at[shift - 1], {"col": goal},
        )

    def merge(here):
        size = pieces[here][1]

        def arrive(tile, carry):
            for shift in range(1, row_count):
                kid_share(tile, shift, here, -1).wait_recv()
            return carry

        lax.fori_loop(0, kid_tiles, arrive, 0)

        def one(block, carry):
            first = kids[picks_ref[0, block], :size].astype(jnp.float32)
            second = kids[picks_ref[1, block], :size].astype(jnp.float32)
            goal = block // per_leaf
            lane = pl.multiple_of(leaving + block % per_leaf * BLOCK, BLOCK)
            ring[1, pl.ds(pl.multiple_of(goal * most, most), size), pl.ds(lane, BLOCK)] = (
                first + second
            ).astype(jnp.bfloat16)
            return carry

        lax.fori_loop(0, blocks, one, 0)
        for shift in range(1, col_count):
            leaf_move(shift, here).start()
        start = pieces[here][0]
        dst = pl.ds(pl.multiple_of(core * half + start, 16), size)
        src = pl.ds(pl.multiple_of(col * most, most), size)
        ring[1, dst, landing] = ring[1, src, pl.ds(leaving, rows)]

    pl.semaphore_wait(ready, col_count - 1)
    each_chip(merge)
    chain(order[2:])
    work = parts.at[1]
    start_tiles, run = finishing(
        (row_count, col_count, test.shape[1] // rows),
        lambda place: ring.at[0, :, pl.ds(place * rows, rows)],
        lambda parity: ring.at[1, pl.ds(parity * probes, probes), pl.ds(0, rows)],
        front_hbm,
        basis_ref,
        core_ref,
        parts.at[3, :, pl.ds(0, slab_in.shape[0] * BLOCK)],
        work,
        parts.at[0],
        ring.at[1, pl.ds(0, probes), pl.ds(rows, rows)],
        ring.at[1, pl.ds(probes, probes), pl.ds(rows, rows)],
        ring.at[0, pl.ds(0, probes), pl.ds(3 * rows, rows)],
        ring.at[0, pl.ds(probes, probes), pl.ds(3 * rows, rows)],
        test,
        slab_in,
        stage_out,
        stage_in,
        sems,
    )
    start_tiles()

    def land():
        for shift in range(1, col_count):
            source = (col - shift + col_count) % col_count
            far = source // 2
            for there in range(chips):

                def wait(there=there):
                    start, size = pieces[there]
                    dst = pl.ds(pl.multiple_of(source % 2 * half + start, 16), size)
                    remote(
                        ring.at[1, pl.ds(0, size), pl.ds(leaving, rows)],
                        ring.at[1, dst, landing],
                        leaf_send.at[shift - 1], leaf_recv.at[shift - 1], {"col": source},
                    ).wait_recv()

                pl.when(far == there)(wait)

    land()
    work[...] = sums[chip] + ring[1, :probes, 2 * rows : 3 * rows].astype(jnp.float32)

    def drain(here):
        def one(tile, carry):
            for goal in range(chips):
                if goal != here:
                    kid_hop(tile, goal, goal > here, False, col).wait_send()
            for shift in range(1, row_count):
                kid_share(tile, shift, here).wait_send()
            return carry

        lax.fori_loop(0, kid_tiles, one, 0)
        for pair in range(chips):
            if pair != here:
                for piece in range(subs):
                    hop(pair, piece, pair > here, False, col).wait_send()
        for shift in range(1, col_count):
            leaf_move(shift, here).wait_send()

    run()
    each_chip(drain)


def sample_of(picks, kid_test, test, kids, front, row_count, col_count):
    depth = front.shape[1]
    probes = test.shape[0]
    kid_rows, kid_depth = kids.shape[1:]
    chips = col_count // 2
    half = probes // 2
    kid_each = kid_rows // LEAF
    kid_tiles = kids.shape[0] * kid_each
    per_leaf = LEAF // BLOCK
    blocks = front.shape[0] // BLOCK
    subs = 4
    pieces = spread(half, chips, 16)
    most = max(size for _, size in pieces)
    low, high, order = 0, chips - 1, []
    while low <= high:
        order += [high] if low == high else [high, low]
        low, high = low + 1, high - 1
    f32, bf16 = jnp.float32, jnp.bfloat16
    steps = probes // PIVOTS
    groups = -(-probes // BLOCK)
    rank_rows = probes // col_count
    packed = probes // BLOCK * rank_rows + -(-rank_rows // 16) * 8
    packed = -(-packed // 16) * 16
    slab = pltpu.VMEM((groups, col_count, per_leaf * (BLOCK // col_count), BLOCK), bf16)
    dims = (row_count, col_count, kid_tiles, kid_each, tuple(order), tuple(pieces), subs)
    any_spec = pl.BlockSpec(memory_space=pl.ANY)
    dma = pltpu.SemaphoreType.DMA
    return pl.pallas_call(
        functools.partial(sample_kernel, dims),
        out_shape=(
            jax.ShapeDtypeStruct((blocks, BLOCK // col_count, probes), bf16),
            jax.ShapeDtypeStruct((col_count, rank_rows, probes), f32),
        ),
        in_specs=[pl.BlockSpec(memory_space=pltpu.SMEM)] + [any_spec] * 4,
        out_specs=(
            pl.BlockSpec(memory_space=pltpu.VMEM),
            pl.BlockSpec(memory_space=pltpu.VMEM),
        ),
        scratch_shapes=[
            pltpu.VMEM((kids.shape[0], probes, kid_depth), bf16),
            pltpu.VMEM((probes, depth), bf16),
            pltpu.VMEM((2, LEAF, depth), bf16),
            pltpu.VMEM((4, probes, LEAF), f32),
            pltpu.VMEM((kid_tiles, half, LEAF), f32),
            pltpu.VMEM((chips, probes, LEAF), f32),
            pltpu.VMEM((kid_tiles, half, LEAF), bf16),
            pltpu.VMEM((kid_tiles, most, LEAF), bf16),
            pltpu.VMEM((chips, probes, LEAF), bf16),
            pltpu.VMEM((probes, LEAF), bf16),
            pltpu.VMEM((row_count * blocks + 1, most, BLOCK), bf16),
            dma((2,)),
            dma((2,)),
            dma((kid_tiles + chips,)),
            dma((kid_tiles + chips,)),
            dma((kid_tiles, chips)),
            dma((kid_tiles, chips)),
            dma((kid_tiles,)),
            dma((chips, subs)),
            dma((chips, subs)),
            dma((subs,)),
            dma((kid_tiles, row_count - 1)),
            dma((kid_tiles, row_count - 1)),
            dma((col_count - 1,)),
            dma((col_count - 1,)),
            slab,
            pltpu.VMEM((3, col_count, packed, BLOCK), bf16),
            pltpu.VMEM((col_count, packed, BLOCK), bf16),
            pltpu.SemaphoreType.REGULAR,
            dma((depth // LEAF,)),
            dma((3,)),
            dma((2, steps)),
            dma((2, steps)),
            dma((steps,)),
            dma((2, steps)),
            dma((groups, col_count)),
            dma((groups, col_count)),
            dma((3, col_count)),
            dma((col_count,)),
        ],
        compiler_params=pltpu.CompilerParams(
            collective_id=0, has_side_effects=True, vmem_limit_bytes=67043328
        ),
        cost_estimate=pl.CostEstimate(
            flops=4 * front.shape[0] * depth * probes,
            bytes_accessed=4 * front.shape[0] * depth,
            transcendentals=0,
        ),
        name="sample",
    )(picks, kid_test, test, kids, front)


def general(parent_front, child_update, parent_test, child_test, child_map):
    row_count = lax.axis_size("row")
    col_count = lax.axis_size("col")
    row_index = lax.axis_index("row")
    col_index = lax.axis_index("col")
    slab = BLOCK // col_count
    own_blocks = parent_front.shape[0] // BLOCK
    probes = parent_test.shape[1]
    per_leaf = LEAF // BLOCK
    leaf_count = own_blocks // per_leaf
    col_leaves = parent_front.shape[1] // LEAF
    shrink = 1.0 / math.sqrt(LEAF)

    tie = lax.optimization_barrier
    pair_index = col_index // 2
    parity = col_index % 2
    half = own_blocks // 2 * BLOCK
    sign = jnp.reshape(parity, (1,)).astype(jnp.int32)
    fronts, tests = parent_front[None], parent_test[None]
    kid_rows = child_update.shape[1]

    def send_tile(position, front):
        sibling = col_index * col_leaves + position
        row_start = jnp.bitwise_xor(sibling, 1) % leaf_count * LEAF
        tile = lax.dynamic_slice(front, (row_start, position * LEAF), (LEAF, LEAF))
        routes = []
        for row in range(row_count):
            for slot in range(leaf_count):
                other = (row * leaf_count + slot) ^ 1
                if other % col_leaves == position:
                    routes.append(
                        (row * col_count + other // col_leaves, row * col_count + slot)
                    )
        return lax.ppermute(tile, ("row", "col"), routes)

    pieces = {position: send_tile(position, parent_front) for position in range(0, col_leaves, 2)}

    jobs = (
        (child_update, child_test, 0, 0, kid_rows),
        (child_update, child_test, 1, 0, kid_rows),
        (fronts, tests, 0, 0, half),
        (fronts, tests, 0, half, half),
    )
    sums = []
    for front, test, which, first_row, rows in jobs:
        halves = probe(front, test, which, first_row, rows, col_count, sign)
        kept, swapped = swap_pair(halves, col_count)
        sums.append(send_pairs(kept, swapped, col_count, pair_index))
    (first_own, first_came), (second_own, second_came) = sums[:2]
    (upper_own, upper_came), (lower_own, lower_came) = sums[2:]

    kid_share = jnp.stack([add_up(first_own, first_came), add_up(second_own, second_came)])
    all_kids = lax.all_gather(kid_share, "row", axis=1, tiled=True)
    own_share = jnp.concatenate([add_up(upper_own, upper_came), add_up(lower_own, lower_came)])

    targets = jnp.arange(own_blocks, dtype=jnp.int32)
    mapped = child_map - row_index * own_blocks
    onehot = (mapped[:, None, :] == targets[None, :, None]).astype(jnp.float32)
    sample = own_share + jnp.einsum("cpn,cnsr->psr", onehot, all_kids, precision=HIGH)

    by_leaf = sample.reshape(leaf_count, per_leaf * slab, probes)
    by_leaf = jnp.pad(by_leaf, ((0, col_count - leaf_count), (0, 0), (0, 0)))
    leaf_rows = lax.all_to_all(by_leaf, "col", 0, 0, tiled=True).reshape(LEAF, probes)

    leaf_rows, front = tie((leaf_rows, parent_front))
    for position in range(1, col_leaves, 2):
        pieces[position] = send_tile(position, front)
    wanted = jnp.bitwise_xor(col_index, 1) % col_leaves
    front_tile = pieces[0]
    for position in range(1, col_leaves):
        front_tile = jnp.where(wanted == position, pieces[position], front_tile)

    basis_t = leaf_basis_of(leaf_rows.T)
    basis = basis_t.T
    slabs = lax.all_to_all(
        basis.reshape(col_count, per_leaf * slab, probes), "col", 0, 0, tiled=True
    )
    leaf_basis = slabs[:leaf_count].reshape(own_blocks, slab, probes)

    natural = (
        basis.reshape(col_count, per_leaf, slab, probes)
        .transpose(1, 0, 2, 3)
        .reshape(LEAF, probes)
    )
    sibling_basis = lax.ppermute(natural, "col", [(c, c ^ 1) for c in range(col_count)])
    product = jnp.dot(front_tile, sibling_basis, preferred_element_type=jnp.float32) * shrink
    core = (
        lax.dot_general(
            natural,
            product.astype(jnp.bfloat16),
            (((0,), (0,)), ((), ())),
            preferred_element_type=jnp.float32,
        )
        * shrink
    )
    cores = lax.all_to_all(
        core.reshape(col_count, probes // col_count, probes), "col", 0, 0, tiled=True
    )
    return (leaf_basis, cores[:leaf_count])


def fits(parent_front, child_update, parent_test, row_count, col_count):
    leaf_count = parent_front.shape[0] // LEAF
    return (
        leaf_count == col_count
        and row_count * 2 == col_count
        and child_update.shape[0] * child_update.shape[1] // LEAF % 4 == 0
        and all(
            sum(abs(pair - row) > 1 and pair % 2 == core for pair in range(row_count)) < 2
            for row in range(row_count)
            for core in range(2)
        )
        and parent_front.shape[1] // LEAF * 2 == leaf_count
        and col_count % 2 == 0
        and parent_front.shape[1] % LEAF == 0
        and 2 * PIVOTS == BLOCK
        and parent_front.shape[1] >= 4 * LEAF
        and LEAF // col_count * -(-parent_test.shape[1] // BLOCK) <= parent_test.shape[1]
        and parent_test.shape[1] * 2 <= LEAF
        and parent_test.shape[1] % BLOCK * 2 == BLOCK
        and parent_test.shape[1] % (8 * col_count) == 0
        and child_update.shape[1] % LEAF == 0
        and 2 * parent_front.shape[1] * LEAF * 2 < 16 << 20
    )


def picks_of(child_map, row_index, row_count, own_blocks):
    kid_count, kid_blocks = child_map.shape
    each = kid_blocks // row_count
    at = jnp.arange(kid_blocks, dtype=jnp.int32)
    which = jnp.arange(kid_count, dtype=jnp.int32)
    value = (at // each * own_blocks + at % each)[None, :] + which[:, None] * each
    targets = jnp.arange(own_blocks, dtype=jnp.int32)
    match = (child_map - row_index * own_blocks)[:, None, :] == targets[None, :, None]
    found = jnp.max(jnp.where(match, value[:, None, :], -1), axis=2)
    return jnp.where(found < 0, row_count * own_blocks, found)


def local(parent_front, child_update, parent_test, child_test, child_map):
    row_count = lax.axis_size("row")
    col_count = lax.axis_size("col")
    if not fits(parent_front, child_update, parent_test, row_count, col_count):
        return general(parent_front, child_update, parent_test, child_test, child_map)
    row_index = lax.axis_index("row")
    own_blocks = parent_front.shape[0] // BLOCK
    picks = picks_of(child_map, row_index, row_count, own_blocks)
    outs = sample_of(
        picks, child_test.transpose(0, 2, 1), parent_test.T, child_update, parent_front,
        row_count, col_count,
    )
    return tuple(outs)


def solution(mesh):
    in_specs = (P("row", "col"), P(None, "row", "col"), P("col", None), P(None, "col", None), P())
    out_specs = (P("row", "col", None), P("row", "col", None))
    return jax.shard_map(local, mesh=mesh, in_specs=in_specs, out_specs=out_specs, check_vma=False)
```

```python
import functools
import math

import jax
import jax.numpy as jnp
from jax import lax
from jax.experimental import pallas as pl
from jax.experimental.pallas import tpu as pltpu
from jax.sharding import PartitionSpec as P


LEAF = 896
BLOCK = 128
PIVOTS = 64
GROUP = 8

HIGH = lax.Precision.HIGHEST
MESH = pl.DeviceIdType.MESH


def dot(a, b, dims):
    return lax.dot_general(
        a, b, (dims, ((), ())), precision=HIGH, preferred_element_type=jnp.float32
    )


def inverse_factor(tile, nb):
    ridx = lax.broadcasted_iota(jnp.int32, tile.shape, 0)
    lane = lax.broadcasted_iota(jnp.int32, tile.shape, 1)
    for j in range(0, nb, GROUP):
        cols = [
            jnp.broadcast_to(tile[:, nb + j + k : nb + j + k + 1], tile.shape)
            for k in range(GROUP)
        ]
        rows = [tile[j + k : j + k + 1, :] for k in range(GROUP)]
        for k in range(GROUP):
            at = j + k
            factor = jnp.where(ridx > at, cols[k] * (1.0 / cols[k][at : at + 1, :]), 0.0)
            for m in range(k + 1, GROUP):
                cols[m] = cols[m] - factor * cols[m][at : at + 1, :]
                rows[m] = rows[m] - factor[j + m : j + m + 1, :] * rows[k]
            cols[k] = factor
        for k in range(GROUP):
            tile = tile - cols[k] * rows[k]
    pivots = jnp.sum(jnp.where(lane == ridx + nb, tile, 0.0), axis=1, keepdims=True)
    return tile[:, :nb] * lax.rsqrt(pivots)


def basis_kernel(scale, yt_ref, qt_ref, gram_ref, work_ref):
    nb = PIVOTS
    probes = yt_ref.shape[0]
    work_ref[...] = yt_ref[...]
    gram_ref[...] = dot(yt_ref[...], yt_ref[...], ((1,), (1,)))

    def step(index, carry):
        start = pl.multiple_of(index * nb, nb)
        panel = gram_ref[pl.ds(start, nb), :]
        source = lax.broadcasted_iota(jnp.int32, (probes, 2 * nb), 0)
        lane = lax.broadcasted_iota(jnp.int32, (probes, 2 * nb), 1)
        pick = jnp.where((lane >= nb) & (source == lane - nb + start), 1.0, 0.0)
        eye = jnp.where(
            lax.broadcasted_iota(jnp.int32, (nb, 2 * nb), 0)
            == lax.broadcasted_iota(jnp.int32, (nb, 2 * nb), 1),
            1.0,
            0.0,
        )
        inverse = inverse_factor(dot(panel, pick, ((1,), (0,))) + eye, nb)
        top = dot(inverse, panel, ((1,), (0,)))
        solved = dot(inverse, work_ref[pl.ds(start, nb), :], ((1,), (0,)))
        qt_ref[pl.ds(start, nb), :] = (solved * scale).astype(qt_ref.dtype)
        gram_ref[...] -= dot(top, top, ((0,), (0,)))
        work_ref[...] -= dot(top, solved, ((0,), (0,)))
        return carry

    lax.fori_loop(0, probes // nb, step, 0)


def leaf_basis_of(yt):
    probes, rows = yt.shape
    return pl.pallas_call(
        functools.partial(basis_kernel, math.sqrt(LEAF)),
        out_shape=jax.ShapeDtypeStruct((probes, rows), jnp.bfloat16),
        in_specs=[pl.BlockSpec(memory_space=pltpu.VMEM)],
        out_specs=pl.BlockSpec(memory_space=pltpu.VMEM),
        scratch_shapes=[
            pltpu.VMEM((probes, probes), jnp.float32),
            pltpu.VMEM((probes, rows), jnp.float32),
        ],
        compiler_params=pltpu.CompilerParams(vmem_limit_bytes=40 << 20),
        cost_estimate=pl.CostEstimate(
            flops=40 * probes * probes * rows,
            bytes_accessed=6 * probes * rows,
            transcendentals=0,
        ),
        name="leaf_basis",
    )(yt)


def probe_kernel(parity_ref, front_ref, test_ref, kept_ref, sent_ref):
    total = jnp.dot(front_ref[...], test_ref[...], preferred_element_type=jnp.float32)
    blocks, pairs, slab, probes = kept_ref.shape
    view = total.reshape(blocks * pairs, 2, slab, probes)
    even = parity_ref[0] == 0
    kept_ref[...] = jnp.where(even, view[:, 0], view[:, 1]).reshape(kept_ref.shape)
    sent_ref[...] = jnp.where(even, view[:, 1], view[:, 0]).reshape(sent_ref.shape)


def probe(front, test, which, first_row, rows, col_count, parity):
    depth, probes = test.shape[1:]
    tile = max(t for t in range(BLOCK, 4 * BLOCK + 1, BLOCK) if rows % t == 0)
    pairs, slab = col_count // 2, BLOCK // col_count
    half = jax.ShapeDtypeStruct((rows // BLOCK, pairs, slab, probes), jnp.float32)
    out_spec = pl.BlockSpec((tile // BLOCK, pairs, slab, probes), lambda i, p: (i, 0, 0, 0))
    skip = first_row // tile
    return pl.pallas_call(
        probe_kernel,
        out_shape=(half, half),
        grid_spec=pltpu.PrefetchScalarGridSpec(
            num_scalar_prefetch=1,
            grid=(rows // tile,),
            in_specs=[
                pl.BlockSpec((None, tile, depth), lambda i, p: (which, skip + i, 0)),
                pl.BlockSpec((None, depth, probes), lambda i, p: (which, 0, 0)),
            ],
            out_specs=(out_spec, out_spec),
        ),
        compiler_params=pltpu.CompilerParams(vmem_limit_bytes=40 << 20),
        cost_estimate=pl.CostEstimate(
            flops=2 * rows * depth * probes,
            bytes_accessed=2 * rows * depth + 2 * depth * probes + 4 * rows * probes,
            transcendentals=0,
        ),
        name="probe",
    )(parity, front, test)


def swap_pair(halves, col_count):
    kept, sent = halves
    return kept, lax.ppermute(sent, "col", [(c, c ^ 1) for c in range(col_count)])


def send_pairs(kept, swapped, col_count, pair_index):
    pairs = col_count // 2

    def piece(pair):
        return lax.dynamic_index_in_dim(kept, pair, 1, False) + lax.dynamic_index_in_dim(
            swapped, pair, 1, False
        )

    came = [
        lax.ppermute(
            piece((pair_index + shift) % pairs).astype(jnp.bfloat16),
            "col",
            [(c, (c + 2 * shift) % col_count) for c in range(col_count)],
        )
        for shift in range(1, pairs)
    ]
    return piece(pair_index), came


def add_up(own, came):
    for term in came:
        own = own + term.astype(jnp.float32)
    return own


def parts_of(x):
    high = x.astype(jnp.bfloat16).astype(jnp.float32)
    rest = x - high
    middle = rest.astype(jnp.bfloat16).astype(jnp.float32)
    return high, middle, rest - middle


def left_parts(x, axis):
    high, middle, low = parts_of(x)
    stacked = jnp.concatenate([high, high, middle, middle, high, low], axis=axis)
    return stacked.astype(jnp.bfloat16)


def right_parts(x):
    high, middle, low = parts_of(x)
    stacked = jnp.concatenate([high, middle, high, middle, low, high], axis=0)
    return stacked.astype(jnp.bfloat16)


def fast_dot(a, b, dims):
    return lax.dot_general(a, b, (dims, ((), ())), preferred_element_type=jnp.float32)


def finishing(
    dims, tile_at, far_at, front_hbm, basis_ref, core_ref, gram, work, exact, high, low,
    near_high, near_low, slab, slab_in, stage, stage_in, sems,
):
    groups, _, slab_rows, _ = slab_in.shape

    (
        tile_send, tile_recv, near_send, near_recv, far_send, far_recv, slab_send, slab_recv,
        core_send, core_recv,
    ) = sems
    _, col_count, tile_leaves = dims
    nb = PIVOTS
    chips = col_count // 2
    probes, rows = work.shape
    per_leaf = rows // BLOCK
    rank_rows = probes // col_count
    whole = probes // BLOCK * BLOCK
    fold = -(-rank_rows // 16) * 8
    packed = stage_in.shape[1]
    steps = probes // nb
    scale = math.sqrt(LEAF)
    shrink = 1.0 / scale
    row, col = lax.axis_index("row"), lax.axis_index("col")
    chip, core = col // 2, col % 2
    sibling = {"col": chip * 2 + 1 - core}
    at_home = chip == row

    def far_of(pair):
        return (pair >= row + 2) | (pair + 2 <= row)

    def remote(src, dst, send, recv, target):
        return pltpu.make_async_remote_copy(
            src_ref=src, dst_ref=dst, send_sem=send, recv_sem=recv,
            device_id=target, device_id_type=MESH,
        )

    def tile_source(position):
        slot = core * tile_leaves + (position ^ 1)
        return front_hbm.at[
            pl.ds(pl.multiple_of(slot * rows, rows), rows), pl.ds(position * rows, rows)
        ]

    def each_tile(act):
        for position in range(tile_leaves):
            parity = (position ^ 1) % 2
            pair = (core * tile_leaves + (position ^ 1)) // 2
            slot = pair * 2 + parity
            is_far = far_of(pair)
            goal = jnp.where(is_far, 2 * row + pair % 2, slot)
            for place, chosen in ((0, jnp.logical_not(is_far)), (1 + parity, is_far)):
                here = at_home & chosen & (goal == col)
                there = at_home & chosen & (goal != col)

                def stay(place=place, position=position):
                    act(
                        pltpu.make_async_copy(
                            tile_source(position), tile_at(place), tile_recv.at[place]
                        ),
                        False,
                    )

                def go(place=place, position=position, goal=goal):
                    act(
                        remote(
                            tile_source(position), tile_at(place), tile_send.at[position],
                            tile_recv.at[place], {"col": goal},
                        ),
                        True,
                    )

                pl.when(here)(stay)
                pl.when(there)(go)

    def start_tiles():
        each_tile(lambda copy, away: copy.start())

    def run():
        one, two, three = (part.astype(jnp.bfloat16) for part in parts_of(work[...]))
        both = ((1,), (1,))
        small = fast_dot(two, two, both) + fast_dot(one, three, both) + fast_dot(three, one, both)
        middle = fast_dot(one, two, both) + fast_dot(two, one, both)
        wide = gram.shape[1]
        gram[:, :probes] = fast_dot(one, one, both) + (middle + small)
        if wide > probes:
            gram[:, probes:] = jnp.zeros((probes, wide - probes), jnp.float32)

        def near_copy(step, which):
            span = pl.ds(pl.multiple_of(step * nb, nb), nb)
            src, dst = ((high, near_high), (low, near_low))[which]
            return remote(
                src.at[span], dst.at[span], near_send.at[which, step], near_recv.at[which, step],
                sibling,
            )

        def far_copy(step, parity):
            span = pl.ds(pl.multiple_of(step * nb, nb), nb)
            return remote(
                high.at[span], far_at(parity).at[span], far_send.at[step], far_recv.at[parity, step],
                {"col": 2 * row + chip % 2},
            )

        def slab_at(group, goal):
            return slab.at[
                pl.ds(pl.multiple_of(jnp.asarray(group * slab_rows, jnp.int32), 16), slab_rows),
                pl.ds(pl.multiple_of(jnp.asarray(goal * BLOCK, jnp.int32), BLOCK), BLOCK),
            ]

        def slab_copy(group, shift, toward=1):
            other = (col + toward * shift + col_count) % col_count
            owner = col if toward == 1 else other
            return remote(
                slab_at(group, other), slab_in.at[group, owner],
                slab_send.at[group, shift], slab_recv.at[group, shift], {"col": other},
            )

        per_slab = BLOCK // col_count

        def send_slabs(group, count):
            start = pl.multiple_of(group * BLOCK, BLOCK)
            for block in range(per_leaf):
                turned = exact[pl.ds(start, count), block * BLOCK : (block + 1) * BLOCK].T
                for goal in range(col_count):
                    place = slab_at(group, goal).at[
                        pl.ds(block * per_slab, per_slab), pl.ds(0, count)
                    ]
                    place[...] = turned[
                        goal * per_slab : (goal + 1) * per_slab
                    ].astype(slab.dtype)
            for shift in range(1, col_count):
                ready = jnp.logical_not(far_of(chip))
                pl.when(ready)(lambda shift=shift: slab_copy(group, shift).start())
            slab_in[group, col] = slab_at(group, col)[...]

        def step(index, carry):
            start = pl.multiple_of(index * nb, nb)
            panel = gram[pl.ds(start, nb), :]
            square = gram[pl.ds(start, nb), pl.ds(pl.multiple_of(index // 2 * 2 * nb, 2 * nb), 2 * nb)]
            square = jnp.where(index % 2 == 0, pltpu.roll(square, nb, 1), square)
            lane = lax.broadcasted_iota(jnp.int32, square.shape, 1)
            eye = jnp.where(lax.broadcasted_iota(jnp.int32, square.shape, 0) == lane, 1.0, 0.0)
            inverse = inverse_factor(jnp.where(lane >= nb, square, eye), nb)
            inverse_parts = left_parts(inverse, 1)
            top = fast_dot(inverse_parts, right_parts(panel), ((1,), (0,)))
            solved = fast_dot(inverse_parts, right_parts(work[pl.ds(start, nb), :]), ((1,), (0,)))
            scaled = solved * scale
            rounded = scaled.astype(high.dtype)
            exact[pl.ds(start, nb), :] = scaled
            high[pl.ds(start, nb), :] = rounded
            low[pl.ds(start, nb), :] = (scaled - rounded.astype(jnp.float32)).astype(low.dtype)
            top_parts = left_parts(top[:, :probes], 0)
            gram[...] -= fast_dot(top_parts, right_parts(top), ((0,), (0,)))
            work[...] -= fast_dot(top_parts, right_parts(solved), ((0,), (0,)))

            @pl.when(far_of(chip))
            def _():
                for parity in range(2):
                    pl.when(core == parity)(lambda parity=parity: far_copy(index, parity).start())

            @pl.when(jnp.logical_not(far_of(chip)))
            def _():
                near_copy(index, 0).start()
                near_copy(index, 1).start()

            @pl.when(index % 2 == 1)
            def _():
                send_slabs(index // 2, BLOCK)

            return carry

        lax.fori_loop(0, steps, step, 0)
        if steps % 2 == 1:
            send_slabs(groups - 1, nb)
        for to_home in (False, True):
            for shift in range(1, col_count):
                goes_home = (col + shift) % col_count // 2 == row

                @pl.when(far_of(chip) & (goes_home == to_home))
                def _(shift=shift):
                    for group in range(groups):
                        slab_copy(group, shift).start()

        def times(a, b):
            return lax.dot_general(
                a, b, (((1,), (1,)), ((), ())), preferred_element_type=jnp.float32
            )

        def core_copy(place, goal, slot):
            return remote(
                stage.at[place, goal], stage_in.at[slot], core_send.at[place, goal],
                core_recv.at[slot], {"col": goal},
            )

        def send_core(place, slot, value):
            value = value * shrink
            for goal in range(col_count):
                piece = value[goal * rank_rows : (goal + 1) * rank_rows]
                columns = [piece[:, at : at + BLOCK] for at in range(0, whole, BLOCK)]
                last = jnp.concatenate(
                    [piece[:fold, whole:], piece[rank_rows - fold :, whole:]], axis=1
                )
                filler = jnp.zeros((packed - len(columns) * rank_rows - fold, BLOCK), jnp.float32)
                stage[place, goal] = jnp.concatenate(columns + [last, filler], axis=0).astype(
                    stage.dtype
                )

                @pl.when(goal != col)
                def _(goal=goal):
                    core_copy(place, goal, slot).start()

                @pl.when(goal == col)
                def _(goal=goal):
                    stage_in[slot] = stage[place, goal]

        def wait_tile(place, source):
            @pl.when(source == col)
            def _():
                pltpu.make_async_copy(
                    front_hbm.at[pl.ds(0, rows), pl.ds(0, rows)], tile_at(place),
                    tile_recv.at[place],
                ).wait()

            @pl.when(source != col)
            def _():
                remote(
                    front_hbm.at[pl.ds(0, rows), pl.ds(0, rows)], tile_at(place), tile_send.at[0],
                    tile_recv.at[place], {"col": source},
                ).wait_recv()

        @pl.when(jnp.logical_not(far_of(chip)))
        def _():
            wait_tile(0, 2 * row + col // tile_leaves)
            for index in range(steps):
                near_copy(index, 0).wait_recv()
                near_copy(index, 1).wait_recv()
            product = (times(near_high[...], tile_at(0)[...]) + times(near_low[...], tile_at(0)[...])) * shrink
            rounded = product.astype(jnp.bfloat16)
            rest = (product - rounded.astype(jnp.float32)).astype(jnp.bfloat16)
            send_core(
                0, col,
                times(high[...], rounded) + (times(low[...], rounded) + times(high[...], rest)),
            )

        for pair in range(chips):

            @pl.when(at_home & far_of(pair) & (core == pair % 2))
            def _(pair=pair):
                for parity in range(2):
                    for index in range(steps):
                        span = pl.ds(index * nb, nb)
                        remote(
                            high.at[span], far_at(parity).at[span], far_send.at[index],
                            far_recv.at[parity, index], {"col": 2 * pair + parity},
                        ).wait_recv()
                for parity in range(2):
                    slot = 2 * pair + parity
                    wait_tile(1 + parity, 2 * row + slot // tile_leaves)
                    product = times(far_at(1 - parity)[...], tile_at(1 + parity)[...]) * shrink
                    send_core(1 + parity, slot, times(far_at(parity)[...], product.astype(jnp.bfloat16)))

        def late(shift):
            other = (col - shift + col_count) % col_count
            return at_home & far_of(other // 2)

        for shift in range(1, col_count):

            @pl.when(jnp.logical_not(late(shift)))
            def _(shift=shift):
                for group in range(groups):
                    slab_copy(group, shift, -1).wait_recv()

        for shift in range(1, col_count):

            @pl.when(late(shift))
            def _(shift=shift):
                for group in range(groups):
                    slab_copy(group, shift, -1).wait_recv()

        for slot in range(col_count):
            for group in range(groups):
                count = min(BLOCK, probes - group * BLOCK)
                basis_ref[
                    slot * per_leaf : (slot + 1) * per_leaf, :, group * BLOCK : group * BLOCK + count
                ] = slab_in[group, slot].reshape(per_leaf, per_slab, BLOCK)[:, :, :count].astype(
                    basis_ref.dtype
                )
        for slot in range(col_count):
            pair = slot // 2
            source = jnp.where(far_of(pair), 2 * row + pair % 2, slot)

            @pl.when(source != col)
            def _(slot=slot, source=source):
                remote(
                    stage.at[0, 0], stage_in.at[slot], core_send.at[0, 0], core_recv.at[slot],
                    {"col": source},
                ).wait_recv()

            came = stage_in[slot].astype(jnp.float32)
            for at in range(0, whole, BLOCK):
                first = at // BLOCK * rank_rows
                core_ref[slot, :, at : at + BLOCK] = came[first : first + rank_rows].astype(
                    core_ref.dtype
                )
            last = came[whole // BLOCK * rank_rows :][:fold]
            side = jnp.concatenate(
                [last[:, : probes - whole], last[2 * fold - rank_rows :, probes - whole :]], axis=0
            )
            core_ref[slot, :, whole:] = side.astype(core_ref.dtype)

        def settle(copy, away):
            if away:
                copy.wait_send()

        each_tile(settle)

        @pl.when(far_of(chip))
        def _():
            for index in range(steps):
                far_copy(index, 0).wait_send()

        @pl.when(jnp.logical_not(far_of(chip)))
        def _():
            for index in range(steps):
                near_copy(index, 0).wait_send()
                near_copy(index, 1).wait_send()
            for goal in range(col_count):
                pl.when(goal != col)(lambda goal=goal: core_copy(0, goal, col).wait_send())

        for group in range(groups):
            for shift in range(1, col_count):
                slab_copy(group, shift).wait_send()
        for pair in range(chips):

            @pl.when(at_home & far_of(pair) & (core == pair % 2))
            def _(pair=pair):
                for parity in range(2):
                    for goal in range(col_count):
                        pl.when(goal != col)(
                            lambda goal=goal, parity=parity: core_copy(
                                1 + parity, goal, 2 * pair + parity
                            ).wait_send()
                        )

    return start_tiles, run


def spread(total, parts, grain):
    base = total // grain
    cuts = [base * (i + 1) // parts * grain for i in range(parts)]
    starts = [0] + cuts[:-1]
    return [(s, e - s) for s, e in zip(starts, cuts)]


def sample_kernel(
    dims,
    picks_ref,
    kid_test_hbm,
    test_hbm,
    kids_hbm,
    front_hbm,
    basis_ref,
    core_ref,
    kid_test,
    test,
    ring,
    parts,
    kid_sum,
    sums,
    kid_in,
    kid_in_two,
    came,
    came_two,
    kids,
    load_sem,
    test_sem,
    swap_send,
    swap_recv,
    kid_send,
    kid_recv,
    kid_recv_two,
    line_send,
    line_recv,
    line_recv_two,
    row_send,
    row_recv,
    leaf_send,
    leaf_recv,
    slab_in,
    stage_out,
    stage_in,
    ready,
    *sems,
):
    row_count, col_count, kid_tiles, kid_each, order, slots, subs = dims
    chips = col_count // 2
    probes, rows = parts.shape[1:]
    half = probes // 2
    per_leaf = rows // BLOCK
    blocks = front_hbm.shape[0] // BLOCK
    most = kids.shape[1]
    pieces = slots
    row, col = lax.axis_index("row"), lax.axis_index("col")
    chip, core = col // 2, col % 2
    sibling = {"col": chip * 2 + 1 - core}

    def remote(src, dst, send, recv, target):
        return pltpu.make_async_remote_copy(
            src_ref=src, dst_ref=dst, send_sem=send, recv_sem=recv,
            device_id=target, device_id_type=MESH,
        )

    barrier = pltpu.get_barrier_semaphore()
    for shift in range(1, col_count):
        pl.semaphore_signal(
            barrier, inc=1, device_id={"col": (col + shift) % col_count}, device_id_type=MESH
        )
    for shift in range(1, row_count):
        pl.semaphore_signal(
            barrier, inc=1, device_id={"row": (row + shift) % row_count}, device_id_type=MESH
        )

    kid_depth = kid_test.shape[2]

    def pair_at(at):
        return jnp.where(at % 2 == 0, chips - 1 - at // 2, at // 2)

    def load_kid(index):
        index = jnp.asarray(index, jnp.int32)
        start = pl.multiple_of(index % kid_each * rows, rows)
        return pltpu.make_async_copy(
            kids_hbm.at[index // kid_each, pl.ds(start, rows)],
            ring.at[index % 2, :, pl.ds(0, kid_depth)],
            load_sem.at[index % 2],
        )

    def load_front(index):
        index = jnp.asarray(index, jnp.int32)
        leaf = 2 * pair_at(index // 2) + jnp.where(index % 2 == 0, 1 - core, core)
        return pltpu.make_async_copy(
            front_hbm.at[pl.ds(pl.multiple_of(leaf * rows, rows), rows)],
            ring.at[index % 2],
            load_sem.at[index % 2],
        )

    kid_test_load = pltpu.make_async_copy(kid_test_hbm, kid_test, test_sem.at[0])
    test_load = pltpu.make_async_copy(test_hbm, test, test_sem.at[1])
    load_kid(0).start()
    kid_test_load.start()
    load_kid(1).start()
    test_load.start()
    kid_test_load.wait()

    def product(left, right):
        return lax.dot_general(
            left, right, (((1,), (1,)), ((), ())), preferred_element_type=jnp.float32
        )

    def kid_swap(tile):
        away = pl.ds(pl.multiple_of((1 - core) * half, half), half)
        return remote(
            parts.at[tile % 4, away], kid_sum.at[tile],
            swap_send.at[tile], swap_recv.at[tile], sibling,
        )

    def swap(at):
        return remote(
            parts.at[2 * at % 4], sums.at[pair_at(at)],
            swap_send.at[kid_tiles + at], swap_recv.at[kid_tiles + at], sibling,
        )

    def kid_combine(tile):
        kid_swap(tile).wait_recv()
        own = pl.ds(pl.multiple_of(core * half, half), half)
        kid_sum[tile] += parts[tile % 4, own]

    def combine(at):
        swap(at).wait_recv()
        sums[pair_at(at)] += parts[(2 * at + 1) % 4]

    def kid_hop(tile, goal, right, last, target):
        start, size = pieces[goal]
        span = pl.ds(start, size)
        two = last and not right
        dst = kid_in_two.at[tile, pl.ds(0, size)] if two else kid_in.at[tile, span]
        sem = kid_recv_two.at[tile] if two else kid_recv.at[tile, goal]
        return remote(
            kid_in.at[tile, span], dst, kid_send.at[tile, goal], sem, {"col": target}
        )

    def kid_push(tile, goal, here):
        start, size = pieces[goal]
        span = pl.ds(start, size)
        right = goal > here
        last = goal == here + 1 if right else goal == here - 1
        kid_in[tile, span] = kid_sum[tile, span].astype(jnp.bfloat16)
        kid_hop(tile, goal, right, last, col + 2 if right else col - 2).start()

    def kid_take(tile, goal, here, right):
        start, size = pieces[goal]
        span = pl.ds(start, size)
        last = goal == here
        kid_hop(tile, goal, right, last, col - 2 if right else col + 2).wait_recv()
        if last and not right:
            kid_sum[tile, span] += kid_in_two[tile, :size].astype(jnp.float32)
        else:
            kid_sum[tile, span] += kid_in[tile, span].astype(jnp.float32)

    def kid_share(tile, shift, here, toward=1):
        size = pieces[here][1]
        other = (row + toward * shift + row_count) % row_count
        owner = row if toward == 1 else other
        span = kids.at[pl.ds(owner * blocks + tile * per_leaf, per_leaf), pl.ds(0, size)]
        return remote(
            span, span, row_send.at[tile, shift - 1], row_recv.at[tile, shift - 1],
            {"row": other},
        )

    def on_chip(here, body):
        pl.when(chip == here)(body)

    def each_chip(body):
        for here in range(chips):
            on_chip(here, functools.partial(body, here))

    end = chips - 1

    def kid_head(tile):
        def right():
            for goal in reversed(range(1, chips)):
                kid_push(tile, goal, 0)

        def left():
            for goal in range(end):
                kid_push(tile, goal, end)

        on_chip(0, right)
        on_chip(end, left)

    def kid_stage(stage, tile):
        def right():
            for goal in reversed(range(stage + 1, chips)):
                kid_take(tile, goal, stage, True)
                kid_push(tile, goal, stage)

        def left():
            for goal in range(end - stage):
                kid_take(tile, goal, end - stage, False)
                kid_push(tile, goal, end - stage)

        def final(here):
            if here > 0:
                kid_take(tile, here, here, True)
            if here < end:
                kid_take(tile, here, here, False)
            start, size = pieces[here]
            for block in range(per_leaf):
                kids[row * blocks + tile * per_leaf + block, :size] = kid_sum[
                    tile, start : start + size, block * BLOCK : (block + 1) * BLOCK
                ].astype(kids.dtype)
            for shift in range(1, row_count):
                kid_share(tile, shift, here).start()

        if stage < end:
            on_chip(stage, right)
            on_chip(end - stage, left)
        for here in range(chips):
            if max(here, end - here) == stage:
                on_chip(here, functools.partial(final, here))

    sub = probes // subs

    def hop(pair, piece, right, last, target):
        span = pl.ds(pl.multiple_of(piece * sub, sub), sub)
        two = last and not right
        dst = came_two.at[span] if two else came.at[pair, span]
        sem = line_recv_two.at[piece] if two else line_recv.at[pair, piece]
        return remote(
            came.at[pair, span], dst, line_send.at[pair, piece], sem, {"col": target}
        )

    def push(pair, piece, here):
        span = pl.ds(pl.multiple_of(piece * sub, sub), sub)
        right = pair > here
        last = pair == here + 1 if right else pair == here - 1
        came[pair, span] = sums[pair, span].astype(jnp.bfloat16)
        hop(pair, piece, right, last, col + 2 if right else col - 2).start()

    def take(pair, piece, here, right):
        span = pl.ds(pl.multiple_of(piece * sub, sub), sub)
        last = pair == here
        hop(pair, piece, right, last, col - 2 if right else col + 2).wait_recv()
        if last and not right:
            sums[pair, span] += came_two[span].astype(jnp.float32)
        else:
            sums[pair, span] += came[pair, span].astype(jnp.float32)

    def head(pair, here):
        def body():
            def one(piece, carry):
                push(pair, piece, here)
                return carry

            lax.fori_loop(0, subs, one, 0)

        on_chip(here, body)

    def stage_of(stage, pair, piece):
        def right():
            take(pair, piece, stage, True)
            push(pair, piece, stage)

        def left():
            take(pair, piece, end - stage, False)
            push(pair, piece, end - stage)

        def final():
            if pair > 0:
                take(pair, piece, pair, True)
            if pair < end:
                take(pair, piece, pair, False)

        if pair > stage and stage < end:
            on_chip(stage, right)
        if pair < end - stage and stage < end:
            on_chip(end - stage, left)
        if max(pair, end - pair) == stage:
            on_chip(pair, final)

    def chain(pairs):
        deepest = max(max(pair, end - pair) for pair in pairs)

        def one(turn, carry):
            for stage in range(1, deepest + 1):
                at = turn - (stage - 1)

                @pl.when((at >= 0) & (at < subs))
                def _(stage=stage, at=at):
                    for pair in pairs:
                        stage_of(stage, pair, at)

            return carry

        lax.fori_loop(0, subs + deepest - 1, one, 0)

    kids[row_count * blocks] = jnp.zeros(kids.shape[1:], kids.dtype)

    def kid_turn(tile, carry):
        pl.when(tile >= 4)(lambda: kid_swap(tile - 4).wait_send())
        load_kid(tile).wait()
        parts[tile % 4] = product(kid_test[tile // kid_each], ring[tile % 2, :, :kid_depth])
        pl.when(tile + 2 < kid_tiles)(lambda: load_kid(tile + 2).start())
        pl.when(tile + 2 >= kid_tiles)(lambda: load_front(tile + 2 - kid_tiles).start())

        @pl.when(tile == 0)
        def _():
            pl.semaphore_wait(barrier, col_count - 1 + row_count - 1)

        kid_swap(tile).start()

        @pl.when(tile > 0)
        def _():
            kid_combine(tile - 1)
            kid_head(tile - 1)

        return carry

    lax.fori_loop(0, kid_tiles, kid_turn, 0)
    test_load.wait()
    turns = 2 * chips

    def turn_of(index, carry):
        at = index // 2

        @pl.when(index < 4)
        def _():
            kid_swap(kid_tiles + index - 4).wait_send()

        @pl.when((index >= 4) & (index % 2 == 0))
        def _():
            swap(at - 2).wait_send()

        load_front(index).wait()
        parts[index % 4] = product(test[...], ring[index % 2])
        pl.when(index + 2 < turns)(lambda: load_front(index + 2).start())

        @pl.when(index % 2 == 0)
        def _():
            swap(at).start()

        @pl.when(index == 0)
        def _():
            kid_combine(kid_tiles - 1)
            kid_head(kid_tiles - 1)

        @pl.when((index % 2 == 0) & (index > 0))
        def _():
            combine(at - 1)

        for spot in range(chips - 1):

            @pl.when(index == 2 * spot + 2)
            def _(spot=spot):
                if order[spot] > 0:
                    head(order[spot], 0)
                if order[spot] < end and spot < chips - 2:
                    head(order[spot], end)

        for stage in range(1, chips):
            tile = index - (stage - 1)
            pl.when((tile >= 0) & (tile < kid_tiles))(
                functools.partial(kid_stage, stage, tile)
            )
        return carry

    lax.fori_loop(0, turns, turn_of, 0)
    combine(chips - 1)
    for at in range(chips - 2, chips):
        swap(at).wait_send()
    for shift in range(1, col_count):
        pl.semaphore_signal(
            ready, inc=1, device_id={"col": (col + shift) % col_count}, device_id_type=MESH
        )
    if order[-1] > 0:
        head(order[-1], 0)
    for pair in (order[-1], order[-2]):
        if pair < end:
            head(pair, end)

    def tail_turn(index, carry):
        for stage in range(1, chips):
            tile = index - (stage - 1)
            pl.when((tile >= 0) & (tile < kid_tiles))(
                functools.partial(kid_stage, stage, tile)
            )
        return carry

    lax.fori_loop(turns, kid_tiles + chips - 2, tail_turn, 0)
    chain(order[:2])

    landing = pl.ds(2 * rows, rows)
    leaving = 3 * rows

    def leaf_move(shift, here):
        start, size = pieces[here]
        goal = (col + shift) % col_count
        src = pl.ds(pl.multiple_of(goal * most, most), size)
        dst = pl.ds(pl.multiple_of(core * half + start, 16), size)
        return remote(
            ring.at[1, src, pl.ds(leaving, rows)], ring.at[1, dst, landing],
            leaf_send.at[shift - 1], leaf_recv.at[shift - 1], {"col": goal},
        )

    def merge(here):
        size = pieces[here][1]

        def arrive(tile, carry):
            for shift in range(1, row_count):
                kid_share(tile, shift, here, -1).wait_recv()
            return carry

        lax.fori_loop(0, kid_tiles, arrive, 0)

        def one(block, carry):
            first = kids[picks_ref[0, block], :size].astype(jnp.float32)
            second = kids[picks_ref[1, block], :size].astype(jnp.float32)
            goal = block // per_leaf
            lane = pl.multiple_of(leaving + block % per_leaf * BLOCK, BLOCK)
            ring[1, pl.ds(pl.multiple_of(goal * most, most), size), pl.ds(lane, BLOCK)] = (
                first + second
            ).astype(jnp.bfloat16)
            return carry

        lax.fori_loop(0, blocks, one, 0)
        for shift in range(1, col_count):
            leaf_move(shift, here).start()
        start = pieces[here][0]
        dst = pl.ds(pl.multiple_of(core * half + start, 16), size)
        src = pl.ds(pl.multiple_of(col * most, most), size)
        ring[1, dst, landing] = ring[1, src, pl.ds(leaving, rows)]

    pl.semaphore_wait(ready, col_count - 1)
    each_chip(merge)
    chain(order[2:])
    work = parts.at[1]
    start_tiles, run = finishing(
        (row_count, col_count, test.shape[1] // rows),
        lambda place: ring.at[0, :, pl.ds(place * rows, rows)],
        lambda parity: ring.at[1, pl.ds(parity * probes, probes), pl.ds(0, rows)],
        front_hbm,
        basis_ref,
        core_ref,
        parts.at[3, :, pl.ds(0, slab_in.shape[0] * BLOCK)],
        work,
        parts.at[0],
        ring.at[1, pl.ds(0, probes), pl.ds(rows, rows)],
        ring.at[1, pl.ds(probes, probes), pl.ds(rows, rows)],
        ring.at[0, pl.ds(0, probes), pl.ds(3 * rows, rows)],
        ring.at[0, pl.ds(probes, probes), pl.ds(3 * rows, rows)],
        test,
        slab_in,
        stage_out,
        stage_in,
        sems,
    )
    start_tiles()

    def land():
        for shift in range(1, col_count):
            source = (col - shift + col_count) % col_count
            far = source // 2
            for there in range(chips):

                def wait(there=there):
                    start, size = pieces[there]
                    dst = pl.ds(pl.multiple_of(source % 2 * half + start, 16), size)
                    remote(
                        ring.at[1, pl.ds(0, size), pl.ds(leaving, rows)],
                        ring.at[1, dst, landing],
                        leaf_send.at[shift - 1], leaf_recv.at[shift - 1], {"col": source},
                    ).wait_recv()

                pl.when(far == there)(wait)

    land()
    work[...] = sums[chip] + ring[1, :probes, 2 * rows : 3 * rows].astype(jnp.float32)

    def drain(here):
        def one(tile, carry):
            for goal in range(chips):
                if goal != here:
                    kid_hop(tile, goal, goal > here, False, col).wait_send()
            for shift in range(1, row_count):
                kid_share(tile, shift, here).wait_send()
            return carry

        lax.fori_loop(0, kid_tiles, one, 0)
        for pair in range(chips):
            if pair != here:
                for piece in range(subs):
                    hop(pair, piece, pair > here, False, col).wait_send()
        for shift in range(1, col_count):
            leaf_move(shift, here).wait_send()

    run()
    each_chip(drain)


def sample_of(picks, kid_test, test, kids, front, row_count, col_count):
    depth = front.shape[1]
    probes = test.shape[0]
    kid_rows, kid_depth = kids.shape[1:]
    chips = col_count // 2
    half = probes // 2
    kid_each = kid_rows // LEAF
    kid_tiles = kids.shape[0] * kid_each
    per_leaf = LEAF // BLOCK
    blocks = front.shape[0] // BLOCK
    subs = probes // PIVOTS
    pieces = spread(half, chips, 16)
    most = max(size for _, size in pieces)
    low, high, order = 0, chips - 1, []
    while low <= high:
        order += [high] if low == high else [high, low]
        low, high = low + 1, high - 1
    f32, bf16 = jnp.float32, jnp.bfloat16
    steps = probes // PIVOTS
    groups = -(-probes // BLOCK)
    rank_rows = probes // col_count
    packed = probes // BLOCK * rank_rows + -(-rank_rows // 16) * 8
    packed = -(-packed // 16) * 16
    slab = pltpu.VMEM((groups, col_count, per_leaf * (BLOCK // col_count), BLOCK), bf16)
    dims = (row_count, col_count, kid_tiles, kid_each, tuple(order), tuple(pieces), subs)
    any_spec = pl.BlockSpec(memory_space=pl.ANY)
    dma = pltpu.SemaphoreType.DMA
    return pl.pallas_call(
        functools.partial(sample_kernel, dims),
        out_shape=(
            jax.ShapeDtypeStruct((blocks, BLOCK // col_count, probes), f32),
            jax.ShapeDtypeStruct((col_count, rank_rows, probes), bf16),
        ),
        in_specs=[pl.BlockSpec(memory_space=pltpu.SMEM)] + [any_spec] * 4,
        out_specs=(
            pl.BlockSpec(memory_space=pltpu.VMEM),
            pl.BlockSpec(memory_space=pltpu.VMEM),
        ),
        scratch_shapes=[
            pltpu.VMEM((kids.shape[0], probes, kid_depth), bf16),
            pltpu.VMEM((probes, depth), bf16),
            pltpu.VMEM((2, LEAF, depth), bf16),
            pltpu.VMEM((4, probes, LEAF), f32),
            pltpu.VMEM((kid_tiles, half, LEAF), f32),
            pltpu.VMEM((chips, probes, LEAF), f32),
            pltpu.VMEM((kid_tiles, half, LEAF), bf16),
            pltpu.VMEM((kid_tiles, most, LEAF), bf16),
            pltpu.VMEM((chips, probes, LEAF), bf16),
            pltpu.VMEM((probes, LEAF), bf16),
            pltpu.VMEM((row_count * blocks + 1, most, BLOCK), bf16),
            dma((2,)),
            dma((2,)),
            dma((kid_tiles + chips,)),
            dma((kid_tiles + chips,)),
            dma((kid_tiles, chips)),
            dma((kid_tiles, chips)),
            dma((kid_tiles,)),
            dma((chips, subs)),
            dma((chips, subs)),
            dma((subs,)),
            dma((kid_tiles, row_count - 1)),
            dma((kid_tiles, row_count - 1)),
            dma((col_count - 1,)),
            dma((col_count - 1,)),
            slab,
            pltpu.VMEM((3, col_count, packed, BLOCK), bf16),
            pltpu.VMEM((col_count, packed, BLOCK), bf16),
            pltpu.SemaphoreType.REGULAR,
            dma((depth // LEAF,)),
            dma((3,)),
            dma((2, steps)),
            dma((2, steps)),
            dma((steps,)),
            dma((2, steps)),
            dma((groups, col_count)),
            dma((groups, col_count)),
            dma((3, col_count)),
            dma((col_count,)),
        ],
        compiler_params=pltpu.CompilerParams(
            collective_id=0, has_side_effects=True, vmem_limit_bytes=67043328
        ),
        cost_estimate=pl.CostEstimate(
            flops=4 * front.shape[0] * depth * probes,
            bytes_accessed=4 * front.shape[0] * depth,
            transcendentals=0,
        ),
        name="sample",
    )(picks, kid_test, test, kids, front)


def general(parent_front, child_update, parent_test, child_test, child_map):
    row_count = lax.axis_size("row")
    col_count = lax.axis_size("col")
    row_index = lax.axis_index("row")
    col_index = lax.axis_index("col")
    slab = BLOCK // col_count
    own_blocks = parent_front.shape[0] // BLOCK
    probes = parent_test.shape[1]
    per_leaf = LEAF // BLOCK
    leaf_count = own_blocks // per_leaf
    col_leaves = parent_front.shape[1] // LEAF
    shrink = 1.0 / math.sqrt(LEAF)

    tie = lax.optimization_barrier
    pair_index = col_index // 2
    parity = col_index % 2
    half = own_blocks // 2 * BLOCK
    sign = jnp.reshape(parity, (1,)).astype(jnp.int32)
    fronts, tests = parent_front[None], parent_test[None]
    kid_rows = child_update.shape[1]

    def send_tile(position, front):
        sibling = col_index * col_leaves + position
        row_start = jnp.bitwise_xor(sibling, 1) % leaf_count * LEAF
        tile = lax.dynamic_slice(front, (row_start, position * LEAF), (LEAF, LEAF))
        routes = []
        for row in range(row_count):
            for slot in range(leaf_count):
                other = (row * leaf_count + slot) ^ 1
                if other % col_leaves == position:
                    routes.append(
                        (row * col_count + other // col_leaves, row * col_count + slot)
                    )
        return lax.ppermute(tile, ("row", "col"), routes)

    pieces = {position: send_tile(position, parent_front) for position in range(0, col_leaves, 2)}

    jobs = (
        (child_update, child_test, 0, 0, kid_rows),
        (child_update, child_test, 1, 0, kid_rows),
        (fronts, tests, 0, 0, half),
        (fronts, tests, 0, half, half),
    )
    sums = []
    for front, test, which, first_row, rows in jobs:
        halves = probe(front, test, which, first_row, rows, col_count, sign)
        kept, swapped = swap_pair(halves, col_count)
        sums.append(send_pairs(kept, swapped, col_count, pair_index))
    (first_own, first_came), (second_own, second_came) = sums[:2]
    (upper_own, upper_came), (lower_own, lower_came) = sums[2:]

    kid_share = jnp.stack([add_up(first_own, first_came), add_up(second_own, second_came)])
    all_kids = lax.all_gather(kid_share, "row", axis=1, tiled=True)
    own_share = jnp.concatenate([add_up(upper_own, upper_came), add_up(lower_own, lower_came)])

    targets = jnp.arange(own_blocks, dtype=jnp.int32)
    mapped = child_map - row_index * own_blocks
    onehot = (mapped[:, None, :] == targets[None, :, None]).astype(jnp.float32)
    sample = own_share + jnp.einsum("cpn,cnsr->psr", onehot, all_kids, precision=HIGH)

    by_leaf = sample.reshape(leaf_count, per_leaf * slab, probes)
    by_leaf = jnp.pad(by_leaf, ((0, col_count - leaf_count), (0, 0), (0, 0)))
    leaf_rows = lax.all_to_all(by_leaf, "col", 0, 0, tiled=True).reshape(LEAF, probes)

    leaf_rows, front = tie((leaf_rows, parent_front))
    for position in range(1, col_leaves, 2):
        pieces[position] = send_tile(position, front)
    wanted = jnp.bitwise_xor(col_index, 1) % col_leaves
    front_tile = pieces[0]
    for position in range(1, col_leaves):
        front_tile = jnp.where(wanted == position, pieces[position], front_tile)

    basis_t = leaf_basis_of(leaf_rows.T)
    basis = basis_t.T
    slabs = lax.all_to_all(
        basis.reshape(col_count, per_leaf * slab, probes), "col", 0, 0, tiled=True
    )
    leaf_basis = slabs[:leaf_count].reshape(own_blocks, slab, probes)

    natural = (
        basis.reshape(col_count, per_leaf, slab, probes)
        .transpose(1, 0, 2, 3)
        .reshape(LEAF, probes)
    )
    sibling_basis = lax.ppermute(natural, "col", [(c, c ^ 1) for c in range(col_count)])
    product = jnp.dot(front_tile, sibling_basis, preferred_element_type=jnp.float32) * shrink
    core = (
        lax.dot_general(
            natural,
            product.astype(jnp.bfloat16),
            (((0,), (0,)), ((), ())),
            preferred_element_type=jnp.float32,
        )
        * shrink
    )
    cores = lax.all_to_all(
        core.reshape(col_count, probes // col_count, probes), "col", 0, 0, tiled=True
    )
    return (leaf_basis, cores[:leaf_count])


def fits(parent_front, child_update, parent_test, row_count, col_count):
    leaf_count = parent_front.shape[0] // LEAF
    return (
        leaf_count == col_count
        and row_count * 2 == col_count
        and child_update.shape[0] == 2
        and child_update.shape[0] * child_update.shape[1] // LEAF % 4 == 0
        and all(
            sum(abs(pair - row) > 1 and pair % 2 == core for pair in range(row_count)) < 2
            for row in range(row_count)
            for core in range(2)
        )
        and parent_front.shape[1] // LEAF * 2 == leaf_count
        and col_count % 2 == 0
        and parent_front.shape[1] % LEAF == 0
        and 2 * PIVOTS == BLOCK
        and parent_front.shape[1] >= 4 * LEAF
        and LEAF // col_count * -(-parent_test.shape[1] // BLOCK) <= parent_test.shape[1]
        and parent_test.shape[1] * 2 <= LEAF
        and parent_test.shape[1] % BLOCK * 2 == BLOCK
        and parent_test.shape[1] % (8 * col_count) == 0
        and child_update.shape[1] % LEAF == 0
        and 2 * parent_front.shape[1] * LEAF * 2 < 16 << 20
    )


def picks_of(child_map, row_index, row_count, own_blocks):
    kid_count, kid_blocks = child_map.shape
    each = kid_blocks // row_count
    at = jnp.arange(kid_blocks, dtype=jnp.int32)
    which = jnp.arange(kid_count, dtype=jnp.int32)
    value = (at // each * own_blocks + at % each)[None, :] + which[:, None] * each
    targets = jnp.arange(own_blocks, dtype=jnp.int32)
    match = (child_map - row_index * own_blocks)[:, None, :] == targets[None, :, None]
    found = jnp.max(jnp.where(match, value[:, None, :], -1), axis=2)
    return jnp.where(found < 0, row_count * own_blocks, found)


def local(parent_front, child_update, parent_test, child_test, child_map):
    row_count = lax.axis_size("row")
    col_count = lax.axis_size("col")
    if not fits(parent_front, child_update, parent_test, row_count, col_count):
        return general(parent_front, child_update, parent_test, child_test, child_map)
    row_index = lax.axis_index("row")
    own_blocks = parent_front.shape[0] // BLOCK
    picks = picks_of(child_map, row_index, row_count, own_blocks)
    basis, cores = sample_of(
        picks, child_test.transpose(0, 2, 1), parent_test.T, child_update, parent_front,
        row_count, col_count,
    )
    return (basis.astype(jnp.bfloat16), cores.astype(jnp.float32))


def solution(mesh):
    in_specs = (P("row", "col"), P(None, "row", "col"), P("col", None), P(None, "col", None), P())
    out_specs = (P("row", "col", None), P("row", "col", None))
    return jax.shard_map(local, mesh=mesh, in_specs=in_specs, out_specs=out_specs, check_vma=False)
```
